32 devices in a mesh: dp: 8 (over z, x), tensor: 4 (over y, core).
Axes of the slice: x: 2, y: 2, z: 4, core: 2. Of those that a mesh axis runs over, the one named last changes fastest.
Arguments:
- tokens: bfloat16 [128, 64, 768], P('dp'), may hold values from -6 to 6
- image_tokens: bfloat16 [128, 256, 768], P('dp', None, 'tensor'), may hold values from -6 to 6
- image_counts: int32 [128], P('dp'), may hold values from 64 to 256, as said below
- ln1_gain: float32 [768], replicated, may hold values from 0.25 to 1.75
- ln1_bias: float32 [768], replicated, may hold values from -2 to 2
- self_qkv: bfloat16 [768, 3, 768], P(None, None, 'tensor'), may hold values from -0.21875 to 0.21875
- self_output_weight: bfloat16 [768, 768], P('tensor'), may hold values from -0.625 to 0.625
- self_output_bias: float32 [768], replicated, may hold values from -2 to 2
- ln2_gain: float32 [768], replicated, may hold values from 0.25 to 1.75
- ln2_bias: float32 [768], replicated, may hold values from -2 to 2
- cross_query_weight: bfloat16 [768, 768], P(None, 'tensor'), may hold values from -0.21875 to 0.21875
- cross_kv: bfloat16 [768, 2, 768], P(None, None, 'tensor'), may hold values from -0.21875 to 0.21875
- cross_output_weight: bfloat16 [768, 768], P('tensor'), may hold values from -0.625 to 0.625
- cross_output_bias: float32 [768], replicated, may hold values from -2 to 2
- ln3_gain: float32 [768], replicated, may hold values from 0.25 to 1.75
- ln3_bias: float32 [768], replicated, may hold values from -2 to 2
- mlp_in: bfloat16 [768, 3072], P(None, 'tensor'), may hold values from -0.21875 to 0.21875
- mlp_in_bias: float32 [3072], P('tensor'), may hold values from -3 to 3
- mlp_out: bfloat16 [3072, 768], P('tensor'), may hold values from -0.15625 to 0.15625
- mlp_out_bias: float32 [768], replicated, may hold values from -2 to 2
- grad_out: bfloat16 [128, 64, 768], P('dp'), may hold values from -6 to 6
Outputs:
- output: bfloat16 [128, 64, 768], P('dp')
- grad_tokens: bfloat16 [128, 64, 768], P('dp')
- grad_image: bfloat16 [128, 256, 768], P('dp', None, 'tensor')
- grad_ln1_gain: float32 [768], replicated
- grad_ln1_bias: float32 [768], replicated
- grad_self_qkv: float32 [768, 3, 768], P('dp', None, 'tensor')
- grad_self_out: float32 [768, 768], P('tensor', 'dp')
- grad_self_out_bias: float32 [768], replicated
- grad_ln2_gain: float32 [768], replicated
- grad_ln2_bias: float32 [768], replicated
- grad_cross_q: float32 [768, 768], P('dp', 'tensor')
- grad_cross_kv: float32 [768, 2, 768], P('dp', None, 'tensor')
- grad_cross_out: float32 [768, 768], P('tensor', 'dp')
- grad_cross_out_bias: float32 [768], replicated
- grad_ln3_gain: float32 [768], replicated
- grad_ln3_bias: float32 [768], replicated
- grad_mlp_in: float32 [768, 3072], P('dp', 'tensor')
- grad_mlp_in_bias: float32 [3072], P('tensor')
- grad_mlp_out: float32 [3072, 768], P('tensor', 'dp')
- grad_mlp_out_bias: float32 [768], replicated
The draws below stay inside these ranges and needn't reach their ends.
Inputs may be any that keep to these rules, and one draw needn't show every extreme that they name: image_counts[c] is the number of leading image tokens that caption c attends to; both bounds are reached in every draw.
All inputs are finite; a program needn't handle non-finite values.
Results may differ from the reference program's by a relative error of at most 0.034.
Values may be sent and summed in bfloat16 or wider, within the bound.
A program may use at most 192 MiB of HBM per device.

```python
import math
import jax
import jax.numpy as jnp
from jax import lax

D = 768
ATTENTION_HEADS = 12
HEAD_SIZE = 64
FF = 3072
IMG = 256
CAPTION_LENGTH = 64
CAPS = 128


def draw_image_counts(key, part):
    first, second, third = jax.random.split(jax.random.fold_in(key, 17), 3)
    counted = jax.random.randint(first, (CAPS,), IMG // 4, IMG + 1)
    highest_at = jax.random.randint(second, (), 0, CAPS)
    lowest_at = (highest_at + 1 + jax.random.randint(third, (), 0, CAPS - 1)) % CAPS
    places = jnp.arange(CAPS)
    counted = jnp.where(places == highest_at, IMG, counted)
    counted = jnp.where(places == lowest_at, IMG // 4, counted)
    return counted.astype(jnp.int32)


def with_spikes(values, key, source, target, shards_of, factor):
    owner, partner = [(jnp.arange(values.shape[position]) // (values.shape[position] // shards_of)).reshape([-1 if axis == position else 1 for axis in range(values.ndim)]) for position in (source, target)]
    chosen = jax.random.permutation(key, shards_of)[partner]
    strong = (owner == chosen) | (owner == (partner + shards_of // 2) % shards_of)
    return jnp.where(strong, factor * values, values)


def level_of(rng, shape, pieces, low, largest):
    loudness, own = 1.0, jax.random.fold_in(rng, 6)
    for position, parts in pieces:
        draws = jnp.exp(jax.random.uniform(jax.random.fold_in(own, position), (parts,), jnp.float32, low / len(pieces), largest / len(pieces)))
        loudness = loudness * jnp.repeat(draws, shape[position] // parts).reshape([-1 if axis == position else 1 for axis in range(len(shape))])
    return loudness


def scatter_about(rng, dims, deviation, reach, cuts=(), dtype=jnp.bfloat16):
    array = jax.random.normal(rng, dims, jnp.float32) * deviation
    if len(cuts) > 0:
        array = level_of(rng, dims, cuts, -0.22, 0.18) * array
    return jnp.clip(array, min=-reach, max=reach).astype(dtype)


def noise_with(own_key, shape, deviation, reach, cuts, heavy, dtype=jnp.bfloat16):
    values = deviation * jax.random.normal(own_key, shape, jnp.float32)
    if cuts:
        values = values * level_of(own_key, shape, cuts, -0.22, 0.18)
    return jnp.clip(with_spikes(values, jax.random.fold_in(own_key, 3), *heavy), -reach, reach).astype(dtype)


def setup_inputs(seed: int = 0) -> dict:
    streams_of = jax.random.split(jax.random.key(seed), 22)
    return {
        "tokens": scatter_about(streams_of[0], (CAPS, CAPTION_LENGTH, D), 1.0, 6.0, ((0, 8),)),
        "image_tokens": scatter_about(streams_of[1], (CAPS, IMG, D), 1.0, 6.0, ((0, 8), (2, 4))),
        "image_counts": draw_image_counts(jax.random.fold_in(streams_of[21], 71), 0),
        "ln1_gain": jnp.clip(1.0 + 0.15 * jax.random.normal(streams_of[3], (D,), jnp.float32), 0.25, 1.75),
        "ln1_bias": scatter_about(streams_of[4], (D,), 0.3, 2.0, (), jnp.float32),
        "self_qkv": scatter_about(streams_of[5], (D, 3, D), D ** -0.5, 0.21875, ((2, 4),)),
        "self_output_weight": scatter_about(streams_of[6], (D, D), (D // 8) ** -0.5, 0.625, ((0, 4),)),
        "self_output_bias": scatter_about(streams_of[7], (D,), 0.3, 2.0, (), jnp.float32),
        "ln2_gain": jnp.clip(1.0 + 0.15 * jax.random.normal(streams_of[8], (D,), jnp.float32), 0.25, 1.75),
        "ln2_bias": scatter_about(streams_of[9], (D,), 0.3, 2.0, (), jnp.float32),
        "cross_query_weight": scatter_about(streams_of[10], (D, D), D ** -0.5, 0.21875, ((1, 4),)),
        "cross_kv": scatter_about(streams_of[11], (D, 2, D), D ** -0.5, 0.21875, ((2, 4),)),
        "cross_output_weight": scatter_about(streams_of[12], (D, D), (D // 8) ** -0.5, 0.625, ((0, 4),)),
        "cross_output_bias": scatter_about(streams_of[13], (D,), 0.3, 2.0, (), jnp.float32),
        "ln3_gain": jnp.clip(1.0 + 0.15 * jax.random.normal(streams_of[14], (D,), jnp.float32), 0.25, 1.75),
        "ln3_bias": scatter_about(streams_of[15], (D,), 0.3, 2.0, (), jnp.float32),
        "mlp_in": scatter_about(streams_of[16], (D, FF), D ** -0.5, 0.21875, ((1, 4),)),
        "mlp_in_bias": scatter_about(streams_of[17], (FF,), 0.5, 3.0, ((0, 4),), jnp.float32),
        "mlp_out": scatter_about(streams_of[18], (FF, D), (FF // 2) ** -0.5, 0.15625, ((0, 4),)),
        "mlp_out_bias": scatter_about(streams_of[19], (D,), 0.3, 2.0, (), jnp.float32),
        "grad_out": noise_with(streams_of[20], (CAPS, CAPTION_LENGTH, D), 1.0, 6.0, ((0, 8),), (0, 2, 8, 2.0)),
    }


@jax.custom_vjp
def low(v):
    return lax.optimization_barrier(v.astype(jnp.bfloat16)).astype(jnp.float32)

@jax.custom_vjp
def reduced_backward(v):
    return v

def low_keep(v):
    return (low(v), None)

def low_pass(kept, grad):
    return (grad,)

def back_keep(v):
    return (v, None)

def back_low(kept, grad):
    return (low(grad),)
low.defvjp(low_keep, low_pass)
reduced_backward.defvjp(back_keep, back_low)
exact_precision = lax.Precision.HIGHEST

def rounding_both_inputs(values):
    return reduced_backward(low(values))

def layer_norm(values, gain_row, bias_row):
    center = values - lax.optimization_barrier(jnp.mean(values, axis=-1, keepdims=True))
    spread = lax.optimization_barrier(jnp.mean(center * center, axis=-1, keepdims=True))
    return center * lax.rsqrt(spread + 1e-05) * gain_row + bias_row

def attend(queries, key_rows, value_rows, allowed):
    scores = jnp.einsum('clhe,cmhe->chlm', queries, key_rows, precision=exact_precision) * HEAD_SIZE ** (-0.5)
    scores = reduced_backward(jnp.where(allowed[:, None], scores, -1000000000.0))
    highest = lax.optimization_barrier(jnp.max(scores, axis=-1, keepdims=True))
    exponent = jnp.exp(scores - highest)
    weights = low(exponent / lax.optimization_barrier(jnp.sum(exponent, axis=-1, keepdims=True)))
    return jnp.einsum('chlm,cmhe->clhe', weights, value_rows, precision=exact_precision)

def forward(params, token_rows, image_rows, count_rows):
    ln1_gain, ln1_bias, self_qkv, self_output_weight, self_output_bias, ln2_gain, ln2_bias, cross_query_weight, cross_kv, cross_output_weight, cross_output_bias, ln3_gain, ln3_bias, mlp_in, mlp_in_bias, mlp_out, mlp_out_bias = params
    count_of_captions = token_rows.shape[0]
    normed_one = low(layer_norm(token_rows, ln1_gain, ln1_bias))
    qkv_all = rounding_both_inputs(jnp.einsum('cld,dtk->cltk', normed_one, self_qkv, precision=exact_precision))
    shaped = qkv_all.reshape(count_of_captions, CAPTION_LENGTH, 3, ATTENTION_HEADS, HEAD_SIZE)
    positions = jnp.arange(CAPTION_LENGTH)
    causal = jnp.broadcast_to(positions[:, None] >= positions[None, :], (count_of_captions, CAPTION_LENGTH, CAPTION_LENGTH))
    first_attention_mix = rounding_both_inputs(attend(shaped[:, :, 0], shaped[:, :, 1], shaped[:, :, 2], causal).reshape(count_of_captions, CAPTION_LENGTH, D))
    after_first_residual = token_rows + reduced_backward(jnp.einsum('qzt,tb->qzb', first_attention_mix, self_output_weight, precision=exact_precision)) + self_output_bias
    second_normalized = low(layer_norm(after_first_residual, ln2_gain, ln2_bias))
    second_query_rows = rounding_both_inputs(jnp.einsum('roq,qz->roz', second_normalized, cross_query_weight, precision=exact_precision)).reshape(count_of_captions, CAPTION_LENGTH, ATTENTION_HEADS, HEAD_SIZE)
    kv_all = rounding_both_inputs(jnp.einsum('cid,dtk->citk', image_rows, cross_kv, precision=exact_precision)).reshape(count_of_captions, IMG, 2, ATTENTION_HEADS, HEAD_SIZE)
    valid_keys = jnp.arange(IMG)[None, :] < count_rows[:, None]
    cross_mask = jnp.broadcast_to(valid_keys[:, None, :], (count_of_captions, CAPTION_LENGTH, IMG))
    second_attention_mix = rounding_both_inputs(attend(second_query_rows, kv_all[:, :, 0], kv_all[:, :, 1], cross_mask).reshape(count_of_captions, CAPTION_LENGTH, D))
    after_second_residual = after_first_residual + reduced_backward(jnp.einsum('qzt,tb->qzb', second_attention_mix, cross_output_weight, precision=exact_precision)) + cross_output_bias
    normed_three = low(layer_norm(after_second_residual, ln3_gain, ln3_bias))
    pre_act = reduced_backward(jnp.einsum('cld,df->clf', normed_three, mlp_in, precision=exact_precision) + mlp_in_bias)
    activated = low(jax.nn.gelu(pre_act, approximate=False))
    return after_second_residual + reduced_backward(jnp.einsum('clf,fd->cld', activated, mlp_out, precision=exact_precision)) + mlp_out_bias

def reference(tokens, image_tokens, image_counts, ln1_gain, ln1_bias, self_qkv, self_output_weight, self_output_bias, ln2_gain, ln2_bias, cross_query_weight, cross_kv, cross_output_weight, cross_output_bias, ln3_gain, ln3_bias, mlp_in, mlp_in_bias, mlp_out, mlp_out_bias, grad_out):
    params = tuple((item_value.astype(jnp.float32) for item_value in (ln1_gain, ln1_bias, self_qkv, self_output_weight, self_output_bias, ln2_gain, ln2_bias, cross_query_weight, cross_kv, cross_output_weight, cross_output_bias, ln3_gain, ln3_bias, mlp_in, mlp_in_bias, mlp_out, mlp_out_bias)))
    group_size = math.gcd(CAPS, max(1, 4096 // CAPTION_LENGTH))
    group_count = CAPS // group_size
    tok_groups = tokens.astype(jnp.float32).reshape(group_count, group_size, CAPTION_LENGTH, D)
    image_groups = image_tokens.astype(jnp.float32).reshape(group_count, group_size, IMG, D)
    count_groups = image_counts.reshape(group_count, group_size)
    grad_groups = grad_out.astype(jnp.float32).reshape(group_count, group_size, CAPTION_LENGTH, D)
    zeros_start = tuple((jnp.zeros_like(item_value) for item_value in params))

    def group_step(totals, batch_items):
        token_rows, image_rows, count_rows, grad_rows = batch_items

        def local_forward(param_set, tok_in, image_in):
            return forward(param_set, tok_in, image_in, count_rows)
        result, pullback = jax.vjp(local_forward, params, token_rows, image_rows)
        grad_params, grad_tok, grad_img = pullback(grad_rows)
        totals = tuple((first + second for first, second in zip(totals, grad_params)))
        return (totals, (result.astype(jnp.bfloat16), grad_tok.astype(jnp.bfloat16), grad_img.astype(jnp.bfloat16)))
    totals, (results, grad_toks, grad_imgs) = lax.scan(group_step, zeros_start, (tok_groups, image_groups, count_groups, grad_groups))
    return (results.reshape(CAPS, CAPTION_LENGTH, D), grad_toks.reshape(CAPS, CAPTION_LENGTH, D), grad_imgs.reshape(CAPS, IMG, D), totals[0], totals[1], totals[2], totals[3], totals[4], totals[5], totals[6], totals[7], totals[8], totals[9], totals[10], totals[11], totals[12], totals[13], totals[14], totals[15], totals[16])
```

```python
from functools import partial

import jax
import jax.numpy as jnp
from jax import lax
from jax.experimental import pallas as pl
from jax.experimental.pallas import tpu as pltpu
from jax.sharding import PartitionSpec as P

HEAD_SIZE = 64

MESH = pl.DeviceIdType.MESH


def log2(value):
    return value.bit_length() - 1


def flipped(value, step):
    return value + step * (1 - 2 * lax.rem(value // step, 2))


def peers():
    d, t = lax.axis_index("dp"), lax.axis_index("tensor")
    return {
        "core": (d, flipped(t, 1)),
        "y": (d, flipped(t, 2)),
        "far": (d, 3 - t),
        "p0": (flipped(d, 1), t),
        "p1": (flipped(d, 2), t),
    }


def greet(devices):
    barrier = pltpu.get_barrier_semaphore()
    for device in devices:
        pl.semaphore_signal(barrier, inc=1, device_id=device, device_id_type=MESH)
    pl.semaphore_wait(barrier, len(devices))


class Links:
    def __init__(self, send, recv):
        self.send, self.recv, self.used, self.begun = send, recv, 0, []

    def copy(self, source, target, device):
        made = pltpu.make_async_remote_copy(
            src_ref=source,
            dst_ref=target,
            send_sem=self.send.at[self.used],
            recv_sem=self.recv.at[self.used],
            device_id=device,
            device_id_type=MESH,
        )
        self.used += 1
        made.start()
        self.begun.append(made)
        return made

    def drain(self):
        for made in self.begun:
            made.wait_send()


def gather_kernel(shapes, captions, *refs):
    count = len(shapes)
    image, weights = refs[0], refs[1 : 1 + count]
    image_all, gathered = refs[1 + count], refs[2 + count : 2 + 2 * count]
    staged = refs[2 + 2 * count : 2 + 3 * count]
    staged_image, send, recv, local_sem = refs[2 + 3 * count :]
    d, t = lax.axis_index("dp"), lax.axis_index("tensor")
    to = peers()
    links = Links(send, recv)
    greet(list(to.values()))
    quarter = lax.rem(d, 4)
    quarters = (quarter, flipped(quarter, 1), flipped(quarter, 2), 3 - quarter)
    other = flipped(t, 2)
    loads = [
        pltpu.make_async_copy(weights[k], staged[k], local_sem.at[k]) for k in range(count)
    ]
    loads.append(
        pltpu.make_async_copy(
            image.at[pl.ds(t * captions, captions)], staged_image, local_sem.at[count]
        )
    )
    for load in loads:
        load.start()

    def rows(k, which, part=None):
        size = shapes[k][0] // 4
        start = quarters[which] * size
        if part is not None:
            first = (size // 2 + 15) // 16 * 16
            start, size = (start, first) if part == 0 else (start + first, size - first)
        return pl.ds(pl.multiple_of(start, 16), size)

    def region(k, which, part=None):
        return gathered[k].at[other, rows(k, which, part)]

    over_y = []
    for k in range(count):
        over_y.append(
            links.copy(weights[k].at[rows(k, 0)], gathered[k].at[t, rows(k, 0)], to["y"])
        )
    images = []
    for name, target in (("y", flipped(t, 2)), ("far", 3 - t), ("core", flipped(t, 1))):
        images.append(
            links.copy(image.at[pl.ds(target * captions, captions)], image_all.at[t], to[name])
        )
    core = []
    for k in range(count):
        core.append(links.copy(weights[k], gathered[k].at[t], to["core"]))
    stores = []
    for k in range(count):
        loads[k].wait()
        stores.append(pltpu.make_async_copy(staged[k], gathered[k].at[t], local_sem.at[k]))
    loads[count].wait()
    stores.append(pltpu.make_async_copy(staged_image, image_all.at[t], local_sem.at[count]))
    for store in stores:
        store.start()
    over_x, over_z, last_x, last_z = {}, {}, {}, {}
    for step in range(count + 2):
        k = step
        if k < count:
            over_y[k].wait_recv()
            over_x[k] = links.copy(region(k, 0), region(k, 0), to["p0"])
            over_z[k] = links.copy(region(k, 0), region(k, 0), to["p1"])
            core.append(links.copy(region(k, 0), region(k, 0), to["core"]))
        k = step - 1
        if 0 <= k < count:
            over_x[k].wait_recv()
            last_z[k] = links.copy(region(k, 1, 0), region(k, 1, 0), to["p1"])
            core.append(links.copy(region(k, 1), region(k, 1), to["core"]))
            over_z[k].wait_recv()
            last_x[k] = links.copy(region(k, 2, 1), region(k, 2, 1), to["p0"])
            core.append(links.copy(region(k, 2), region(k, 2), to["core"]))
        k = step - 2
        if 0 <= k < count:
            last_z[k].wait_recv()
            core.append(links.copy(region(k, 3, 0), region(k, 3, 0), to["core"]))
            last_x[k].wait_recv()
            core.append(links.copy(region(k, 3, 1), region(k, 3, 1), to["core"]))
    for made in images + core:
        made.wait_recv()
    for store in stores:
        store.wait()
    links.drain()


def gather(image, weights, captions):
    shapes = [w.shape for w in weights]
    count = len(weights)
    copies = count * 12 + 3
    any_spec = pl.BlockSpec(memory_space=pl.ANY)
    return pl.pallas_call(
        partial(gather_kernel, shapes, captions),
        out_shape=[jax.ShapeDtypeStruct((4, captions, *image.shape[1:]), jnp.bfloat16)]
        + [jax.ShapeDtypeStruct((4, *s), jnp.bfloat16) for s in shapes],
        in_specs=[any_spec] * (1 + count),
        out_specs=[any_spec] * (1 + count),
        scratch_shapes=[pltpu.VMEM(s, jnp.bfloat16) for s in shapes]
        + [
            pltpu.VMEM((captions, *image.shape[1:]), jnp.bfloat16),
            pltpu.SemaphoreType.DMA((copies,)),
            pltpu.SemaphoreType.DMA((copies,)),
            pltpu.SemaphoreType.DMA((count + 1,)),
        ],
        name="gather_weights",
        compiler_params=pltpu.CompilerParams(
            collective_id=0, has_side_effects=True, vmem_limit_bytes=60 << 20
        ),
    )(image, *weights)


def add_into(target, left, right, rows):
    lead = target.shape[:-2]
    total = 1
    for size in lead:
        total *= size
    columns = target.shape[-1]
    height = target.shape[-2]
    slabs = height // rows

    def body(i, carry):
        index, rest = [], i // slabs
        for size in reversed(lead):
            index.insert(0, lax.rem(rest, size))
            rest = rest // size
        place = (*index, pl.ds(pl.multiple_of(lax.rem(i, slabs) * rows, rows), rows))
        target[place] = (
            left[place].astype(jnp.float32) + right[place].astype(jnp.float32)
        ).astype(target.dtype)
        return carry

    lax.fori_loop(0, total * slabs, body, 0)


def reduce_kernel(pieces, stride, captions, *refs):
    grads = refs[:pieces]
    image, out_rows, token_rows, small = refs[pieces : pieces + 4]
    outs = refs[pieces + 4 : 2 * pieces + 4]
    image_out, out_all, token_all, small_out = refs[2 * pieces + 4 : 2 * pieces + 8]
    rest = refs[2 * pieces + 8 :]
    own, from_core, from_0, from_1, from_2, from_y, result, kept, small_in, sum_vm, send, recv, local_sem = rest
    kept_image, kept_out, kept_token = kept
    d, t = lax.axis_index("dp"), lax.axis_index("tensor")
    y, c = t // 2, lax.rem(t, 2)
    bits = [lax.rem(d // (stride << b), 2) for b in range(3)]
    partner = [(flipped(d, stride << b), t) for b in range(3)]
    to = peers()
    greet([to["core"], to["y"], to["far"], *partner])
    links = Links(send, recv)
    locals_ = []

    def local(source, target):
        made = pltpu.make_async_copy(source, target, local_sem.at[len(locals_)])
        made.start()
        locals_.append(made)
        return made

    sum_load = local(small, sum_vm.at[0])
    own_loads, core_copies = [], []
    for p in range(pieces):
        core_copies.append(
            [
                links.copy(
                    grads[p].at[2 * h + 1 - c], from_core.at[p, h], to["core"]
                )
                for h in range(2)
            ]
        )
        own_loads.append([local(grads[p].at[2 * h + c], own.at[p, h]) for h in range(2)])
    moves = []
    span = pl.ds(t * captions, captions)
    for name, target in (("y", flipped(t, 2)), ("far", 3 - t), ("core", flipped(t, 1))):
        moves.append(links.copy(image.at[target], image_out.at[span], to[name]))
        moves.append(links.copy(out_rows, out_all.at[span], to[name]))
        moves.append(links.copy(token_rows, token_all.at[span], to[name]))
    ins = [
        local(image.at[t], kept_image),
        local(out_rows, kept_out),
        local(token_rows, kept_token),
    ]
    back = []

    hops = {}

    def stage(p, s):
        if s == 0:
            for h in range(2):
                own_loads[p][h].wait()
                core_copies[p][h].wait_recv()
            add_into(own.at[p], own.at[p], from_core.at[p], 32)
            hops[p, 0] = links.copy(
                own.at[p, :, :, :, 1 - bits[0]], from_0.at[p], partner[0]
            )
        elif s == 1:
            hops[p, 0].wait_recv()
            add_into(from_0.at[p], from_0.at[p], own.at[p, :, :, :, bits[0]], 32)
            hops[p, 1] = links.copy(from_0.at[p, :, :, 1 - bits[1]], from_1.at[p], partner[1])
        elif s == 2:
            hops[p, 1].wait_recv()
            add_into(from_1.at[p], from_1.at[p], from_0.at[p, :, :, bits[1]], 32)
            hops[p, 2] = links.copy(from_1.at[p, :, 1 - bits[2]], from_2.at[p], partner[2])
        elif s == 3:
            hops[p, 2].wait_recv()
            add_into(from_2.at[p], from_2.at[p], from_1.at[p, :, bits[2]], 32)
            hops[p, 3] = links.copy(from_2.at[p, 1 - y], from_y.at[p], to["y"])
        else:
            hops[p, 3].wait_recv()
            add_into(result.at[p], from_y.at[p], from_2.at[p, y], 32)
            back.append(local(result.at[p], outs[p]))

    small_to = [to["core"], *partner, to["y"]]
    sum_load.wait()
    sums = 0
    for slot in range(pieces + 4):
        for s in range(4, -1, -1):
            if 0 <= slot - s < pieces:
                stage(slot - s, s)
        if slot >= 1 and sums < 5:
            made = links.copy(sum_vm.at[sums], small_in.at[sums], small_to[sums])
            made.wait_recv()
            sum_vm[sums + 1] = sum_vm[sums] + small_in[sums]
            sums += 1
    back.append(local(sum_vm.at[5], small_out))
    for made in ins:
        made.wait()
    back.append(local(kept_image, image_out.at[span]))
    back.append(local(kept_out, out_all.at[span]))
    back.append(local(kept_token, token_all.at[span]))
    for made in moves:
        made.wait_recv()
    links.drain()
    for made in back:
        made.wait()


def reduce_all(grads, image, out_rows, token_rows, small, stride):
    pieces = len(grads)
    captions = out_rows.shape[0]
    block, columns = grads[0].shape[-2:]
    any_spec = pl.BlockSpec(memory_space=pl.ANY)
    low = jnp.bfloat16
    copies = pieces * 6 + 9 + 5
    shape = jax.ShapeDtypeStruct
    return pl.pallas_call(
        partial(reduce_kernel, pieces, stride, captions),
        out_shape=[shape((block, columns), jnp.float32)] * pieces
        + [
            shape((4 * captions, *image.shape[2:]), low),
            shape((4 * captions, *out_rows.shape[1:]), low),
            shape((4 * captions, *token_rows.shape[1:]), low),
            shape(small.shape, jnp.float32),
        ],
        in_specs=[any_spec] * (pieces + 4),
        out_specs=[any_spec] * (pieces + 4),
        scratch_shapes=[
            pltpu.VMEM((pieces, 2, 2, 2, 2, block, columns), low),
            pltpu.VMEM((pieces, 2, 2, 2, 2, block, columns), low),
            pltpu.VMEM((pieces, 2, 2, 2, block, columns), low),
            pltpu.VMEM((pieces, 2, 2, block, columns), low),
            pltpu.VMEM((pieces, 2, block, columns), low),
            pltpu.VMEM((pieces, block, columns), low),
            pltpu.VMEM((pieces, block, columns), jnp.float32),
            [
                pltpu.VMEM(image.shape[1:], low),
                pltpu.VMEM(out_rows.shape, low),
                pltpu.VMEM(token_rows.shape, low),
            ],
            pltpu.VMEM((5, *small.shape), jnp.float32),
            pltpu.VMEM((6, *small.shape), jnp.float32),
            pltpu.SemaphoreType.DMA((copies,)),
            pltpu.SemaphoreType.DMA((copies,)),
            pltpu.SemaphoreType.DMA((3 * pieces + 8,)),
        ],
        name="reduce_gradients",
        compiler_params=pltpu.CompilerParams(
            collective_id=1, has_side_effects=True, vmem_limit_bytes=62 << 20
        ),
    )(*grads, image, out_rows, token_rows, small)


def norm_parts(values):
    center = values - jnp.mean(values, axis=-1, keepdims=True)
    inv_std = lax.rsqrt(jnp.mean(center * center, axis=-1, keepdims=True) + 1e-05)
    return (center * inv_std, inv_std)


def norm_back(gradient, normed, inv_std, gain_row):
    scaled = gradient * gain_row
    return inv_std * (
        scaled
        - jnp.mean(scaled, axis=-1, keepdims=True)
        - normed * jnp.mean(scaled * normed, axis=-1, keepdims=True)
    )


def low_round(rows):
    return rows.astype(jnp.bfloat16).astype(jnp.float32)


def attend_forward(queries, key_rows, value_rows, allowed, scaling):
    scores = (
        jnp.einsum("clhe,cmhe->chlm", queries, key_rows, preferred_element_type=jnp.float32)
        * scaling
    )
    scores = jnp.where(allowed[:, None], scores, -1000000000.0)
    highest = jnp.max(scores, axis=-1, keepdims=True)
    exponent = jnp.exp(scores - highest)
    chances = exponent / jnp.sum(exponent, axis=-1, keepdims=True)
    mixture = jnp.einsum(
        "chlm,cmhe->clhe",
        chances.astype(jnp.bfloat16),
        value_rows,
        preferred_element_type=jnp.float32,
    )
    return (mixture.astype(jnp.bfloat16), chances)


def attend_back(grad_mixture, queries, key_rows, value_rows, chances, scaling):
    grad_chances = jnp.einsum(
        "clhe,cmhe->chlm", grad_mixture, value_rows, preferred_element_type=jnp.float32
    )
    grad_values = jnp.einsum(
        "chlm,clhe->cmhe",
        chances.astype(jnp.bfloat16),
        grad_mixture,
        preferred_element_type=jnp.float32,
    )
    inner_sum = jnp.sum(grad_chances * chances, axis=-1, keepdims=True)
    grad_scores = (chances * (grad_chances - inner_sum)).astype(jnp.bfloat16)
    grad_queries = (
        jnp.einsum("chlm,cmhe->clhe", grad_scores, key_rows, preferred_element_type=jnp.float32)
        * scaling
    )
    grad_keys = (
        jnp.einsum("chlm,clhe->cmhe", grad_scores, queries, preferred_element_type=jnp.float32)
        * scaling
    )
    return (
        grad_queries.astype(jnp.bfloat16),
        grad_keys.astype(jnp.bfloat16),
        grad_values.astype(jnp.bfloat16),
    )


def local(
    tokens,
    image_tokens,
    image_counts,
    ln1_gain,
    ln1_bias,
    self_qkv,
    self_output_weight,
    self_output_bias,
    ln2_gain,
    ln2_bias,
    cross_query_weight,
    cross_kv,
    cross_output_weight,
    cross_output_bias,
    ln3_gain,
    ln3_bias,
    mlp_in,
    mlp_in_bias,
    mlp_out,
    mlp_out_bias,
    grad_out,
):
    groups = 4
    n = lax.axis_size("dp")
    stride = n // 8
    model_width = tokens.shape[2]
    captions, length = tokens.shape[0] // groups, tokens.shape[1]
    mine = lax.axis_index("tensor") * captions
    tokens = lax.dynamic_slice_in_dim(tokens, mine, captions, 0)
    grad_out = lax.dynamic_slice_in_dim(grad_out, mine, captions, 0)
    image_counts = lax.dynamic_slice_in_dim(image_counts, mine, captions, 0)
    bias_all = lax.all_gather(mlp_in_bias, "tensor", axis=0, tiled=True)
    part = self_output_weight.shape[0]
    image_all, *whole = gather(
        image_tokens,
        [
            self_qkv.reshape(model_width, 3 * part),
            self_output_weight,
            cross_query_weight,
            cross_kv.reshape(model_width, 2 * part),
            cross_output_weight,
            mlp_in,
            mlp_out,
        ],
        captions,
    )

    def joined(parts, many=1):
        split = parts.reshape(groups, parts.shape[1], many, parts.shape[2] // many)
        return split.transpose(1, 2, 0, 3).reshape(parts.shape[1], many, -1)

    self_qkv = joined(whole[0], 3)
    self_output_weight = whole[1].reshape(-1, model_width)
    cross_query_weight = joined(whole[2])[:, 0]
    cross_kv = joined(whole[3], 2)
    cross_output_weight = whole[4].reshape(-1, model_width)
    mlp_in = joined(whole[5])[:, 0]
    mlp_out = whole[6].reshape(-1, model_width)
    mlp_in_bias = bias_all
    image_full = image_all.transpose(1, 2, 0, 3).reshape(captions, image_tokens.shape[1], -1)
    row_count = captions * length
    local_width = self_output_weight.shape[0]
    local_heads = local_width // HEAD_SIZE
    scaling = HEAD_SIZE ** (-0.5)
    residual = tokens.astype(jnp.float32).reshape(row_count, model_width)
    normed_one, inv_one = norm_parts(residual)
    in_one = (normed_one * ln1_gain + ln1_bias).astype(jnp.bfloat16)
    qkv_rows = jnp.einsum(
        "rd,dtk->rtk", in_one, self_qkv, preferred_element_type=jnp.float32
    ).astype(jnp.bfloat16)
    qkv_view = qkv_rows.reshape(captions, length, 3, local_heads, HEAD_SIZE)
    queries_one, keys_one, values_one = (qkv_view[:, :, 0], qkv_view[:, :, 1], qkv_view[:, :, 2])
    positions = jnp.arange(length)
    causal = jnp.broadcast_to(positions[:, None] >= positions[None, :], (captions, length, length))
    mixture_one, chances_one = attend_forward(queries_one, keys_one, values_one, causal, scaling)
    mixture_one = mixture_one.reshape(row_count, local_width)
    after_first_residual = (
        residual
        + low_round(jnp.dot(mixture_one, self_output_weight, preferred_element_type=jnp.float32))
        + self_output_bias
    )
    second_normalized, inv_two = norm_parts(after_first_residual)
    in_two = (second_normalized * ln2_gain + ln2_bias).astype(jnp.bfloat16)
    second_query_rows = (
        jnp.dot(in_two, cross_query_weight, preferred_element_type=jnp.float32)
        .astype(jnp.bfloat16)
        .reshape(captions, length, local_heads, HEAD_SIZE)
    )
    image_count = image_full.shape[1]
    kv_rows = jnp.einsum(
        "cid,dtk->citk", image_full, cross_kv, preferred_element_type=jnp.float32
    ).astype(jnp.bfloat16)
    kv_view = kv_rows.reshape(captions, image_count, 2, local_heads, HEAD_SIZE)
    keys_two, values_two = (kv_view[:, :, 0], kv_view[:, :, 1])
    valid_keys = jnp.arange(image_count)[None, :] < image_counts[:, None]
    cross_mask = jnp.broadcast_to(valid_keys[:, None, :], (captions, length, image_count))
    mixture_two, chances_two = attend_forward(
        second_query_rows, keys_two, values_two, cross_mask, scaling
    )
    mixture_two = mixture_two.reshape(row_count, local_width)
    after_second_residual = (
        after_first_residual
        + low_round(
            jnp.dot(mixture_two, cross_output_weight, preferred_element_type=jnp.float32)
        )
        + cross_output_bias
    )
    normed_three, inv_three = norm_parts(after_second_residual)
    in_three = (normed_three * ln3_gain + ln3_bias).astype(jnp.bfloat16)
    pre_act = jnp.dot(in_three, mlp_in, preferred_element_type=jnp.float32) + mlp_in_bias
    activated, gelu_pull = jax.vjp(partial(jax.nn.gelu, approximate=False), pre_act)
    act_low = activated.astype(jnp.bfloat16)
    result = (
        after_second_residual
        + low_round(jnp.dot(act_low, mlp_out, preferred_element_type=jnp.float32))
        + mlp_out_bias
    )
    output = result.astype(jnp.bfloat16).reshape(tokens.shape)
    grad_rows = grad_out.astype(jnp.float32).reshape(row_count, model_width)
    grad_low = grad_rows.astype(jnp.bfloat16)
    grad_mlp_out_local = jnp.einsum(
        "rf,rd->fd", act_low, grad_low, preferred_element_type=jnp.float32
    )
    grad_hidden = jnp.einsum("rd,fd->rf", grad_low, mlp_out, preferred_element_type=jnp.float32)
    (grad_pre,) = gelu_pull(grad_hidden)
    grad_pre_low = grad_pre.astype(jnp.bfloat16)
    grad_mlp_in_bias = jnp.sum(grad_pre_low, axis=0, dtype=jnp.float32)
    grad_mlp_in_local = jnp.einsum(
        "rd,rf->df", in_three, grad_pre_low, preferred_element_type=jnp.float32
    )
    grad_in_three = low_round(
        jnp.einsum("rf,df->rd", grad_pre_low, mlp_in, preferred_element_type=jnp.float32)
    )
    grad_gain_three = jnp.sum(grad_in_three * normed_three, axis=0)
    grad_bias_three = jnp.sum(grad_in_three, axis=0)
    grad_two = grad_rows + norm_back(grad_in_three, normed_three, inv_three, ln3_gain)
    grad_two_low = grad_two.astype(jnp.bfloat16)
    grad_cross_bias = jnp.sum(grad_two, axis=0)
    grad_cross_out_local = jnp.einsum(
        "rk,rd->kd", mixture_two, grad_two_low, preferred_element_type=jnp.float32
    )
    grad_mix_two = jnp.einsum(
        "rd,kd->rk", grad_two_low, cross_output_weight, preferred_element_type=jnp.float32
    ).astype(jnp.bfloat16)
    grad_mix_two = grad_mix_two.reshape(captions, length, local_heads, HEAD_SIZE)
    grad_query_two, grad_keys_two, grad_values_two = attend_back(
        grad_mix_two, second_query_rows, keys_two, values_two, chances_two, scaling
    )
    grad_kv = jnp.stack([grad_keys_two, grad_values_two], axis=2).reshape(
        captions, image_count, 2, local_width
    )
    grad_cross_kv_local = jnp.einsum(
        "cid,citk->dtk", image_full, grad_kv, preferred_element_type=jnp.float32
    )
    image_terms = jnp.einsum("citk,dtk->cid", grad_kv, cross_kv, preferred_element_type=jnp.float32)
    image_parts = (
        image_terms.astype(jnp.bfloat16)
        .reshape(captions, image_count, groups, -1)
        .transpose(2, 0, 1, 3)
    )
    query_rows_two = grad_query_two.reshape(row_count, local_width)
    grad_cross_q_local = jnp.einsum(
        "rd,rk->dk", in_two, query_rows_two, preferred_element_type=jnp.float32
    )
    grad_in_two = low_round(
        jnp.einsum(
            "rk,dk->rd", query_rows_two, cross_query_weight, preferred_element_type=jnp.float32
        )
    )
    grad_gain_two = jnp.sum(grad_in_two * second_normalized, axis=0)
    grad_bias_two = jnp.sum(grad_in_two, axis=0)
    grad_one = grad_two + norm_back(grad_in_two, second_normalized, inv_two, ln2_gain)
    grad_one_low = grad_one.astype(jnp.bfloat16)
    grad_self_bias = jnp.sum(grad_one, axis=0)
    grad_self_out_local = jnp.einsum(
        "rk,rd->kd", mixture_one, grad_one_low, preferred_element_type=jnp.float32
    )
    grad_mix_one = jnp.einsum(
        "rd,kd->rk", grad_one_low, self_output_weight, preferred_element_type=jnp.float32
    ).astype(jnp.bfloat16)
    grad_mix_one = grad_mix_one.reshape(captions, length, local_heads, HEAD_SIZE)
    grad_query_one, grad_keys_one, grad_values_one = attend_back(
        grad_mix_one, queries_one, keys_one, values_one, chances_one, scaling
    )
    grad_qkv = jnp.stack([grad_query_one, grad_keys_one, grad_values_one], axis=2).reshape(
        row_count, 3, local_width
    )
    grad_self_qkv_local = jnp.einsum(
        "rd,rtk->dtk", in_one, grad_qkv, preferred_element_type=jnp.float32
    )
    grad_in_one = low_round(
        jnp.einsum("rtk,dtk->rd", grad_qkv, self_qkv, preferred_element_type=jnp.float32)
    )
    grad_gain_one = jnp.sum(grad_in_one * normed_one, axis=0)
    grad_bias_one = jnp.sum(grad_in_one, axis=0)
    grad_tokens = (
        (grad_one + norm_back(grad_in_one, normed_one, inv_one, ln1_gain))
        .astype(jnp.bfloat16)
        .reshape(tokens.shape)
    )
    grad_out_bias = jnp.sum(grad_rows, axis=0)
    block = model_width // 8

    def parted(grad, many=1):
        split = grad.astype(jnp.bfloat16).reshape(model_width, many, groups, -1)
        return split.transpose(2, 0, 1, 3).reshape(groups, model_width, -1)

    pieces = [
        parted(grad_mlp_out_local.T),
        parted(grad_mlp_in_local),
        jnp.concatenate(
            [
                parted(grad_cross_kv_local, 2),
                parted(grad_cross_q_local),
                parted(grad_cross_out_local.T),
            ],
            axis=2,
        ),
        jnp.concatenate([parted(grad_self_qkv_local, 3), parted(grad_self_out_local.T)], axis=2),
    ]
    pieces = [g.reshape(groups, 2, 2, 2, block, -1) for g in pieces]
    rows = [
        grad_gain_one,
        grad_bias_one,
        grad_self_bias,
        grad_gain_two,
        grad_bias_two,
        grad_cross_bias,
        grad_gain_three,
        grad_bias_three,
        grad_out_bias,
    ]
    small = jnp.concatenate(
        [jnp.stack(rows), grad_mlp_in_bias.reshape(groups, -1), jnp.zeros((3, model_width))]
    )
    sum_out, sum_in, sum_cross, sum_self, grad_image, output, grad_tokens, small = reduce_all(
        pieces, image_parts, output, grad_tokens, small, stride
    )
    if stride > 1:
        near = [[hi * stride + lo for lo in range(stride)] for hi in range(8)]
        sum_out, sum_in, sum_cross, sum_self = (
            lax.psum_scatter(s, "dp", scatter_dimension=0, axis_index_groups=near, tiled=True)
            for s in (sum_out, sum_in, sum_cross, sum_self)
        )
        small = lax.psum(small, "dp", axis_index_groups=near)
    (
        grad_gain_one,
        grad_bias_one,
        grad_self_bias,
        grad_gain_two,
        grad_bias_two,
        grad_cross_bias,
        grad_gain_three,
        grad_bias_three,
        grad_out_bias,
    ) = (small[i] for i in range(9))
    grad_mlp_in_bias = lax.dynamic_index_in_dim(
        small, 9 + lax.axis_index("tensor"), 0, keepdims=False
    )
    grad_mlp_out = sum_out.T
    grad_mlp_in = sum_in
    grad_cross_kv = sum_cross[:, : 2 * part].reshape(-1, 2, part)
    grad_cross_q = sum_cross[:, 2 * part : 3 * part]
    grad_cross_out = sum_cross[:, 3 * part :].T
    grad_self_qkv = sum_self[:, : 3 * part].reshape(-1, 3, part)
    grad_self_out = sum_self[:, 3 * part :].T
    return (
        output,
        grad_tokens,
        grad_image,
        grad_gain_one,
        grad_bias_one,
        grad_self_qkv,
        grad_self_out,
        grad_self_bias,
        grad_gain_two,
        grad_bias_two,
        grad_cross_q,
        grad_cross_kv,
        grad_cross_out,
        grad_cross_bias,
        grad_gain_three,
        grad_bias_three,
        grad_mlp_in,
        grad_mlp_in_bias,
        grad_mlp_out,
        grad_out_bias,
    )


def solution(mesh):
    return jax.shard_map(
        local,
        mesh=mesh,
        in_specs=(
            P("dp", None, None),
            P("dp", None, "tensor"),
            P("dp"),
            P(),
            P(),
            P(None, None, "tensor"),
            P("tensor", None),
            P(),
            P(),
            P(),
            P(None, "tensor"),
            P(None, None, "tensor"),
            P("tensor", None),
            P(),
            P(),
            P(),
            P(None, "tensor"),
            P("tensor"),
            P("tensor", None),
            P(),
            P("dp", None, None),
        ),
        out_specs=(
            P("dp", None, None),
            P("dp", None, None),
            P("dp", None, "tensor"),
            P(),
            P(),
            P("dp", None, "tensor"),
            P("tensor", "dp"),
            P(),
            P(),
            P(),
            P("dp", "tensor"),
            P("dp", None, "tensor"),
            P("tensor", "dp"),
            P(),
            P(),
            P(),
            P("dp", "tensor"),
            P("tensor"),
            P("tensor", "dp"),
            P(),
        ),
        check_vma=False,
    )
```

```python
from functools import partial

import jax
import jax.numpy as jnp
from jax import lax
from jax.experimental import pallas as pl
from jax.experimental.pallas import tpu as pltpu
from jax.sharding import PartitionSpec as P

HEAD_SIZE = 64
LOW = jnp.bfloat16
HIGH = jnp.float32
MESH = pl.DeviceIdType.MESH
SCALING = HEAD_SIZE**-0.5


def dot(left, right):
    return jnp.dot(left, right, preferred_element_type=HIGH)


def dot_rows(left, right):
    return lax.dot_general(left, right, (((1,), (1,)), ((), ())), preferred_element_type=HIGH)


def dot_columns(left, right):
    return lax.dot_general(left, right, (((0,), (0,)), ((), ())), preferred_element_type=HIGH)


def norm_parts(values):
    center = values - jnp.mean(values, axis=-1, keepdims=True)
    inv_std = lax.rsqrt(jnp.mean(center * center, axis=-1, keepdims=True) + 1e-05)
    return center * inv_std, inv_std


def folded(values):
    return jnp.sum(values.reshape(values.shape[0] // 8, 8, values.shape[1]), axis=0)


def flipped(value, step):
    return value + step * (1 - 2 * lax.rem(value // step, 2))


def peers():
    d, t = lax.axis_index("dp"), lax.axis_index("tensor")
    return {"core": (d, flipped(t, 1)), "y": (d, flipped(t, 2)), "far": (d, 3 - t)}


def greet(devices):
    barrier = pltpu.get_barrier_semaphore()
    for device in devices:
        pl.semaphore_signal(barrier, inc=1, device_id=device, device_id_type=MESH)
    pl.semaphore_wait(barrier, len(devices))


class Copies:
    def __init__(self, send, recv, local):
        self.send, self.recv, self.local = send, recv, local
        self.remotes, self.locals = [], 0

    def to(self, source, target, device):
        slot = len(self.remotes)
        assert slot < self.send.shape[0]
        made = pltpu.make_async_remote_copy(
            src_ref=source,
            dst_ref=target,
            send_sem=self.send.at[slot],
            recv_sem=self.recv.at[slot],
            device_id=device,
            device_id_type=MESH,
        )
        made.start()
        self.remotes.append(made)
        return made

    def move(self, source, target):
        assert self.locals < self.local.shape[0]
        made = pltpu.make_async_copy(source, target, self.local.at[self.locals])
        made.start()
        self.locals += 1
        return made

    def drain(self):
        for made in self.remotes:
            made.wait_send()


def softmax(scores, allowed):
    scores = jnp.where(allowed, scores * SCALING, -1000000000.0)
    exponent = jnp.exp(scores - jnp.max(scores, axis=-1, keepdims=True))
    return exponent / jnp.sum(exponent, axis=-1, keepdims=True)


def window_allowed(length, window):
    row = lax.broadcasted_iota(jnp.int32, (window, window), 0)
    column = lax.broadcasted_iota(jnp.int32, (window, window), 1)
    return (row // length == column // length) & (row >= column)


def head(j):
    return pl.ds(j * HEAD_SIZE, HEAD_SIZE)


def lanes(j):
    return slice(j * HEAD_SIZE, (j + 1) * HEAD_SIZE)


VEC = ("ln1g", "ln1b", "sob", "ln2g", "ln2b", "cob", "ln3g", "ln3b", "mob")


def forward_kernel(dims, *refs):
    captions, length, images, width, part = dims
    rows = captions * length
    (counts, vec, tokens, image, bias, *weights), refs = refs[:12], refs[12:]
    (q1, kv1, o1, x1, q2, kv2, o2, x2, img, w_back, kv_turned, w_in, w_out, bias_all), refs = (
        refs[:14],
        refs[14:],
    )
    (
        (v_q1, v_kv1, v_o1, v_x1, v_q2, v_kv2, v_o2, v_x2, v_img),
        v_w,
        v_turned,
        v_tokens,
        v_h,
        send,
        recv,
        local,
    ) = refs
    w_keep = list(v_w) + [w_in, w_out]
    d, t = lax.axis_index("dp"), lax.axis_index("tensor")
    near = {"p0": (flipped(d, 1), t), "p1": (flipped(d, 2), t), **peers()}
    order = [t, flipped(t, 1), flipped(t, 2), 3 - t]
    copies = Copies(send, recv, local)
    token_load = copies.move(tokens.at[pl.ds(t * rows, rows)], v_tokens)
    loads = [copies.move(weights[k], v_w[k].at[t]) for k in range(5)]
    image_load = copies.move(image.at[pl.ds(t * captions, captions)], v_img.at[:, t])
    greet(list(near.values()))
    quarter = lax.rem(d, 4)
    quarters = (quarter, flipped(quarter, 1), flipped(quarter, 2), 3 - quarter)
    other = order[2]

    def part_of(k, which, half=None):
        size = weights[k].shape[0] // 4
        start = quarters[which] * size
        if half is not None:
            first = (size // 2 + 15) // 16 * 16
            start, size = (start, first) if half == 0 else (start + first, size - first)
        return pl.ds(pl.multiple_of(start, 16), size)

    def region(k, which, half=None):
        return w_keep[k].at[other, part_of(k, which, half)]

    count = len(weights)
    over_y, over, own_core, images_in = {}, {}, {}, []

    def send_y(k):
        over_y[k] = copies.to(
            weights[k].at[part_of(k, 0)], w_keep[k].at[t, part_of(k, 0)], near["y"]
        )

    def send_image(name, target):
        images_in.append(
            copies.to(image.at[pl.ds(target * captions, captions)], v_img.at[:, t], near[name])
        )

    own_core[0] = copies.to(weights[0], w_keep[0].at[t], near["core"])
    own_core[1] = copies.to(weights[1], w_keep[1].at[t], near["core"])
    for k in range(6):
        send_y(k)
    send_image("y", order[2])
    send_image("far", order[3])
    send_y(6)
    send_image("core", order[1])
    for k in range(2, count):
        own_core[k] = copies.to(weights[k], w_keep[k].at[t], near["core"])
    biases = [copies.to(bias, bias_all.at[t], near[name]) for name in ("core", "y", "far")]
    core = {k: [] for k in range(count)}

    def first(k):
        over_y[k].wait_recv()
        over[k, 0] = copies.to(region(k, 0), region(k, 0), near["p0"])
        over[k, 1] = copies.to(region(k, 0), region(k, 0), near["p1"])
        core[k].append(copies.to(region(k, 0), region(k, 0), near["core"]))

    def second(k):
        over[k, 0].wait_recv()
        over[k, 2] = copies.to(region(k, 1, 0), region(k, 1, 0), near["p1"])
        core[k].append(copies.to(region(k, 1), region(k, 1), near["core"]))
        over[k, 1].wait_recv()
        over[k, 3] = copies.to(region(k, 2, 1), region(k, 2, 1), near["p0"])
        core[k].append(copies.to(region(k, 2), region(k, 2), near["core"]))

    def third(k):
        over[k, 2].wait_recv()
        core[k].append(copies.to(region(k, 3, 0), region(k, 3, 0), near["core"]))
        over[k, 3].wait_recv()
        core[k].append(copies.to(region(k, 3, 1), region(k, 3, 1), near["core"]))

    def arrived(k):
        for made in core[k]:
            made.wait_recv()

    g = {name: vec[i : i + 1, :] for i, name in enumerate(VEC)}
    slab = 32

    def normed(source, gain, shift):
        def body(i, carry):
            place = pl.ds(pl.multiple_of(i * slab, slab), slab)
            n, _ = norm_parts(source[place, :].astype(HIGH))
            v_h[place, :] = (n * gain + shift).astype(LOW)
            return carry

        lax.fori_loop(0, rows // slab, body, 0)

    token_load.wait()
    normed(v_tokens, g["ln1g"], g["ln1b"])

    def start_sum(target, source, shift):
        def body(i, carry):
            place = pl.ds(pl.multiple_of(i * slab, slab), slab)
            target[place, :] = source[place, :].astype(HIGH) + shift
            return carry

        lax.fori_loop(0, rows // slab, body, 0)

    start_sum(v_x1, v_tokens, g["sob"])
    window = 2 * length
    causal = window_allowed(length, window)
    heads = part // HEAD_SIZE

    def self_part(s):
        h = v_h[...]
        v_q1[s] = dot_rows(h, v_w[0][s, :part, :]).astype(LOW)
        v_kv1[s] = dot_rows(v_w[0][s, part:, :], h).astype(LOW)
        for w in range(rows // window):
            span = pl.ds(w * window, window)
            mixed = []
            for j in range(heads):
                q = v_q1[s, span, :][:, lanes(j)]
                p = softmax(dot(q, v_kv1[s, head(j), span]), causal)
                mixed.append(dot_rows(p.astype(LOW), v_kv1[s, head(heads + j), span]))
            v_o1[s, span, :] = jnp.concatenate(mixed, axis=1).astype(LOW)
        v_x1[...] += dot(v_o1[s], v_w[1][s])

    def queries(s):
        v_q2[s] = dot_rows(v_h[...], v_w[2][s]).astype(LOW)

    def turn(s):
        v_turned[:, pl.ds(pl.multiple_of(s * 2 * part, 128), 2 * part)] = v_w[3][s].T

    def cross_part(s):
        def body(c, carry):
            span = pl.ds(pl.multiple_of(c * images, images), images)
            v_kv2[s, :, span] = dot(v_w[3][s], v_img[c].reshape(width, images)).astype(LOW)
            own = pl.ds(pl.multiple_of(c * length, length), length)
            allowed = (
                lax.broadcasted_iota(jnp.int32, (length, images), 1)
                < counts[t * captions + c]
            )
            mixed = []
            for j in range(heads):
                q = v_q2[s, own, :][:, lanes(j)]
                p = softmax(dot(q, v_kv2[s, head(j), span]), allowed)
                mixed.append(dot_rows(p.astype(LOW), v_kv2[s, head(heads + j), span]))
            v_o2[s, own, :] = jnp.concatenate(mixed, axis=1).astype(LOW)
            return carry

        lax.fori_loop(0, captions, body, 0)
        v_x2[...] += dot(v_o2[s], v_w[4][s])

    back = []
    loads[0].wait()
    loads[1].wait()
    self_part(order[0])
    own_core[0].wait_recv()
    own_core[1].wait_recv()
    first(0)
    self_part(order[1])
    first(1)
    first(2)
    second(0)
    first(3)
    second(1)
    first(4)
    third(0)
    second(2)
    third(1)
    second(3)
    arrived(0)
    arrived(1)
    self_part(order[2])
    third(2)
    second(4)
    self_part(order[3])
    first(5)
    third(3)
    third(4)
    back.append(copies.move(v_q1, q1))
    back.append(copies.move(v_kv1, kv1))
    back.append(copies.move(v_o1, o1))
    back.append(copies.move(v_x1, x1))
    normed(v_x1, g["ln2g"], g["ln2b"])
    start_sum(v_x2, v_x1, g["cob"])
    for k in range(2, 5):
        loads[k].wait()
        own_core[k].wait_recv()
        arrived(k)
    for s in order:
        queries(s)
        turn(s)
    back.append(copies.move(v_turned, kv_turned))
    for i, k in enumerate((0, 1, 2, 4)):
        back.append(copies.move(v_w[k], w_back[i]))
    second(5)
    third(5)
    image_load.wait()
    for made in images_in:
        made.wait_recv()
    back.append(copies.move(v_q2, q2))
    back.append(copies.move(v_img, img))
    cross_part(order[0])
    first(6)
    cross_part(order[1])
    cross_part(order[2])
    second(6)
    cross_part(order[3])
    back.append(copies.move(v_kv2, kv2))
    back.append(copies.move(v_o2, o2))
    back.append(copies.move(v_x2, x2))
    third(6)
    for k in (5, 6):
        own_core[k].wait_recv()
        arrived(k)
    for made in biases:
        made.wait_recv()
    copies.drain()
    for made in back:
        made.wait()


def forward(dims, counts, vec, tokens, image, bias, weights):
    captions, length, images, width, part = dims
    rows = captions * length
    shape = jax.ShapeDtypeStruct
    kept = [
        ((4, rows, part), LOW),
        ((4, 2 * part, rows), LOW),
        ((4, rows, part), LOW),
        ((rows, width), HIGH),
        ((4, rows, part), LOW),
        ((4, 2 * part, captions * images), LOW),
        ((4, rows, part), LOW),
        ((rows, width), HIGH),
        ((captions, 4, part, images), LOW),
    ]
    sizes = [(4, *w.shape) for w in weights]
    any_spec = pl.BlockSpec(memory_space=pl.ANY)
    vmem, smem = pl.BlockSpec(memory_space=pltpu.VMEM), pl.BlockSpec(memory_space=pltpu.SMEM)
    remote = 7 * 12 + 6
    return pl.pallas_call(
        partial(forward_kernel, dims),
        out_shape=[shape(*k) for k in kept]
        + [
            [shape(sizes[k], LOW) for k in (0, 1, 2, 4)],
            shape((width, 8 * part), LOW),
            shape(sizes[5], LOW),
            shape(sizes[6], LOW),
            shape((4, *bias.shape), HIGH),
        ],
        in_specs=[smem, vmem] + [any_spec] * 10,
        out_specs=[any_spec] * 9 + [[any_spec] * 4] + [any_spec] * 4,
        scratch_shapes=[
            [pltpu.VMEM(*k) for k in kept],
            [pltpu.VMEM(sizes[k], LOW) for k in range(5)],
            pltpu.VMEM((width, 8 * part), LOW),
            pltpu.VMEM((rows, width), LOW),
            pltpu.VMEM((rows, width), LOW),
            pltpu.SemaphoreType.DMA((remote,)),
            pltpu.SemaphoreType.DMA((remote,)),
            pltpu.SemaphoreType.DMA((32,)),
        ],
        name="forward",
        compiler_params=pltpu.CompilerParams(
            collective_id=0, has_side_effects=True, vmem_limit_bytes=62 << 20
        ),
    )(counts, vec, tokens, image, bias, *weights)


def backward_kernel(dims, stride, plan, *refs):
    captions, length, images, width, part = dims
    rows = captions * length
    block = width // 8
    heads = part // HEAD_SIZE
    window = 2 * length
    (
        (counts, vec, bias, bias_all, tokens, grads, raw_in, raw_out),
        (q1, kv1, o1, x1, q2, kv2, o2, x2, img),
        w_back,
        kv_turned,
        w_in,
        w_out,
        sums,
        image_out,
        out_all,
        token_all,
        small_out,
        (v_q1, v_kv1, v_o1, v_x1, v_q2, v_kv2, v_o2, v_x2, v_img),
        (v_w0, v_w1, v_w2, v_w4),
        v_turned,
        v_in,
        v_out,
        v_bias,
        v_tokens,
        v_grads,
        g_out,
        g_in,
        v_h,
        v_turn_a,
        v_turn_b,
        v_f0,
        v_f1,
        v_y,
        v_g,
        v_small_a,
        v_low,
        v_narrow,
        v_image,
        from_core,
        halves,
        from_y,
        result,
        v_sum,
        sum_in,
        credit,
        send,
        recv,
        local,
    ) = refs
    d, t = lax.axis_index("dp"), lax.axis_index("tensor")
    y, c = t // 2, lax.rem(t, 2)
    near = peers()
    bits = [lax.rem(d // (stride << b), 2) for b in range(3)]
    partner = [(flipped(d, stride << b), t) for b in range(3)]
    order = [3 - t, flipped(t, 2), flipped(t, 1), t]
    copies = Copies(send, recv, local)

    mine = pl.ds(t * rows, rows)
    load_x2 = copies.move(x2, v_x2)
    load_grads = copies.move(grads.at[mine], v_grads)
    load_mlp = []
    for i, s in enumerate(order):
        sources = (raw_in, raw_out, bias) if i == 3 else (
            w_in.at[s // 2, lax.rem(s, 2)],
            w_out.at[s // 2, lax.rem(s, 2)],
            bias_all.at[s],
        )
        targets = (v_in.at[s // 2, lax.rem(s, 2)], v_out.at[s // 2, lax.rem(s, 2)], v_bias.at[s])
        load_mlp.append([copies.move(a, b) for a, b in zip(sources, targets)])
    load_rest = [
        copies.move(a, b)
        for a, b in (
            (w_back[3], v_w4),
            (q2, v_q2),
            (kv2, v_kv2),
            (o2, v_o2),
            (x1, v_x1),
            (img, v_img),
            (w_back[2], v_w2),
            (kv_turned, v_turned),
            (w_back[1], v_w1),
            (w_back[0], v_w0),
            (q1, v_q1),
            (kv1, v_kv1),
            (o1, v_o1),
            (tokens.at[mine], v_tokens),
        )
    ]
    greet([*near.values(), *partner])

    g = {name: vec[i : i + 1, :] for i, name in enumerate(VEC)}
    slab = 32

    def loop(body, init, step=slab):
        def run(i, carry):
            return body(pl.ds(pl.multiple_of(i * step, step), step), carry)

        return lax.fori_loop(0, rows // step, run, init)

    zeros = jnp.zeros((8, width), HIGH)
    small_rows = {}

    def keep(name, total):
        v_sum[0, pl.ds(name, 1), :] = jnp.sum(total, axis=0, keepdims=True)

    units = [(p, o) for p in range(4) for o in (0, 1)]
    pieces = [g_out, g_in, v_in, v_out]
    to_core, hops, places = {}, {}, {}
    side = (1 - y, y)

    def offer(p, o):
        u = 2 * p + o
        if p >= 2:
            pl.semaphore_wait(credit.at[u - 4], 1)
        to_core[p, o] = copies.to(
            pieces[p].at[side[o], 1 - c], from_core.at[u % 4], near["core"]
        )

    def add(target, left, *others):
        lead = target.shape[:-2]
        total = 1
        for size in lead:
            total *= size
        tall = 32
        slabs = target.shape[-2] // tall

        def body(i, carry):
            index, rest = [], i // slabs
            for size in reversed(lead):
                index.insert(0, lax.rem(rest, size))
                rest = rest // size
            place = (*index, pl.ds(pl.multiple_of(lax.rem(i, slabs) * tall, tall), tall))
            value = left[place].astype(HIGH)
            for ref in others:
                value = value + ref[place].astype(HIGH)
            target[place] = value.astype(target.dtype)
            return carry

        lax.fori_loop(0, total * slabs, body, 0)

    def cut(bit, left, value):
        return tuple(value if b == bit else slice(None) for b in sorted(left, reverse=True))

    back = []

    def advance(p, o, stage):
        u = 2 * p + o
        turn = plan[p]
        y_first = turn[0] == "y"
        xyz = [b for b in turn if b != "y"]
        base = pieces[p].at[side[o], c]
        if stage == 0:
            to_core[p, o].wait_recv()
            if y_first and o == 1:
                hops[p, 0, "y"].wait_recv()
                add(base, base, from_core.at[u % 4], from_y[p])
            else:
                add(base, base, from_core.at[u % 4])
            if p < 2:
                pl.semaphore_signal(
                    credit.at[u], inc=1, device_id=near["core"], device_id_type=MESH
                )
            places[u] = base, [0, 1, 2]
            if y_first and o == 0:
                hops[p, 0, "y"] = copies.to(base, from_y[p], near["y"])
                return
        if stage > 0:
            source, left = places[u]
            bit = xyz[stage - 1]
            hops[p, o, stage].wait_recv()
            target = halves[stage - 1].at[u]
            kept = source.at[cut(bit, left, bits[bit])]
            remaining = [b for b in left if b != bit]
            last = stage == 3
            if last and o == 1:
                if y_first:
                    add(result.at[p], target, kept)
                else:
                    hops[p, 0, "y"].wait_recv()
                    add(result.at[p], target, kept, from_y[p])
                back.append(copies.move(result.at[p], sums[p]))
                return
            add(target, target, kept)
            places[u] = target, remaining
            if last:
                hops[p, 0, "y"] = copies.to(target, from_y[p], near["y"])
                return
        source, left = places[u]
        bit = xyz[stage]
        shape = halves[stage].at[u]
        hops[p, o, stage + 1] = copies.to(
            source.at[cut(bit, left, 1 - bits[bit])], shape, partner[bit]
        )

    def stages(p, o):
        return 1 if plan[p][0] == "y" and o == 0 else 4

    load_x2.wait()
    load_grads.wait()

    def start(place, carry):
        n, _ = norm_parts(v_x2[place, :])
        v_h[place, :] = (n * g["ln3g"] + g["ln3b"]).astype(LOW)
        v_y[place, :] = v_x2[place, :] + g["mob"]
        v_g[place, :] = jnp.zeros((slab, width), HIGH)
        return carry + folded(v_grads[place, :].astype(HIGH))

    keep(8, loop(start, zeros))
    v_turn_a[...] = v_h[...].T
    v_turn_b[...] = v_grads[...].T

    def weight(ref, s):
        return ref[s // 2, lax.rem(s, 2)].reshape(width, width)

    def put(ref, s, first, values):
        half, values = values
        ref[s // 2, lax.rem(s, 2), half, :, :, :, first : first + values.shape[1]] = (
            values.astype(LOW).reshape(2, 2, block, values.shape[1])
        )

    def half_rows(half):
        return pl.ds(half * (width // 2), width // 2)

    def feed(s):
        v_f0[...] = dot(v_h[...], weight(v_in, s))
        v_f1[...] = dot_rows(v_grads[...], weight(v_out, s))
        shift = v_bias[s]

        def act(place, carry):
            a = v_f0[place, :] + shift
            cumulative = 0.5 * (1.0 + lax.erf(a * (0.5**0.5)))
            density = jnp.exp(-0.5 * a * a) * 0.3989422804014327
            v_low[0, place, :] = (a * cumulative).astype(LOW)
            ga = (v_f1[place, :] * (cumulative + a * density)).astype(LOW)
            v_low[1, place, :] = ga
            return carry + folded(ga.astype(HIGH))

        total = loop(act, zeros, 16)
        v_small_a[s] = jnp.sum(total, axis=0, keepdims=True)
        u, ga = v_low[0], v_low[1]
        v_y[...] += dot(u, weight(v_out, s))
        v_g[...] += dot_rows(ga, weight(v_in, s))
        for half in range(2):
            put(g_out, s, 0, (half, dot(v_turn_b[half_rows(half), :], u)))
            put(g_in, s, 0, (half, dot(v_turn_a[half_rows(half), :], ga)))

    for i, s in enumerate(order):
        for load in load_mlp[i]:
            load.wait()
        feed(s)
        if i == 0:
            offer(0, 0)
            offer(1, 0)
        if i == 1:
            advance(0, 0, 0)
            advance(1, 0, 0)
        if i == 2:
            offer(0, 1)
            offer(1, 1)

    def shared(source, target):
        place = target.at[pl.ds(t * rows, rows)]
        back.append(copies.move(source, place))
        return [copies.to(source, place, near[name]) for name in ("core", "y", "far")]

    def norm_back(source, gain, old, new, low):
        def body(place, carry):
            a, b, e = carry
            n, inv_std = norm_parts(source[place, :].astype(HIGH))
            gh = v_g[place, :]
            scaled = gh * gain
            grad = inv_std * (
                scaled
                - jnp.mean(scaled, axis=-1, keepdims=True)
                - n * jnp.mean(scaled * n, axis=-1, keepdims=True)
            )
            grad = old[place, :].astype(HIGH) + grad
            if new is not None:
                new[place, :] = grad
                e = e + folded(grad)
            low[place, :] = grad.astype(LOW)
            return a + folded(gh * n), b + folded(gh), e

        return loop(body, (zeros, zeros, zeros))

    def finish(place, carry):
        v_h[place, :] = v_y[place, :].astype(LOW)
        return carry

    advance(0, 0, 1)
    advance(1, 0, 1)
    advance(0, 1, 0)
    advance(1, 1, 0)
    loop(finish, 0)
    v_out_low = v_low.at[0]
    v_out_low[...] = v_h[...]
    out_moves = shared(v_out_low, out_all)
    gain_sum, bias_sum, total = norm_back(v_x2, g["ln3g"], v_grads, v_f0, v_grads)
    keep(6, gain_sum)
    keep(7, bias_sum)
    keep(5, total)

    for load in load_rest:
        load.wait()

    def again(source, gain, shift):
        def body(place, carry):
            n, _ = norm_parts(source[place, :].astype(HIGH))
            v_h[place, :] = (n * gain + shift).astype(LOW)
            v_g[place, :] = jnp.zeros((slab, width), HIGH)
            return carry

        loop(body, 0)

    again(v_x1, g["ln2g"], g["ln2b"])
    v_turn_a[...] = v_h[...].T
    v_turn_b[...] = v_grads[...].T
    go, gq = v_narrow.at[0], v_narrow.at[1]

    def attend_back(p, q, k, v, g_mix):
        low_p = p.astype(LOW)
        gp = dot(g_mix, v)
        inner = jnp.sum(gp * p, axis=-1, keepdims=True)
        gs = (p * (gp - inner)).astype(LOW)
        return (
            dot_rows(gs, k) * SCALING,
            (dot_columns(q, gs) * SCALING).astype(LOW),
            dot_columns(g_mix, low_p).astype(LOW),
        )

    def gradients(piece, s, of_keys, o_kept):
        for half in range(2):
            put(piece, s, 0, (half, of_keys(half)))
            both = [dot(v_turn_a[half_rows(half), :], gq[...])]
            both.append(dot(v_turn_b[half_rows(half), :], o_kept[s]))
            put(piece, s, 2 * part, (half, jnp.concatenate(both, axis=1)))

    def cross_back(s):
        go[...] = dot_rows(v_grads[...], v_w4[s]).astype(LOW)

        def body(caption, carry):
            span = pl.ds(pl.multiple_of(caption * images, images), images)
            own = pl.ds(pl.multiple_of(caption * length, length), length)
            allowed = (
                lax.broadcasted_iota(jnp.int32, (length, images), 1)
                < counts[t * captions + caption]
            )
            all_q, all_go, queries = v_q2[s, own, :], go[own, :], []
            for j in range(heads):
                q, k, v = all_q[:, lanes(j)], v_kv2[s, head(j), span], v_kv2[s, head(heads + j), span]
                p = softmax(dot(q, k), allowed)
                g_q, g_k, g_v = attend_back(p, q, k, v, all_go[:, lanes(j)])
                queries.append(g_q)
                v_kv2[s, head(j), span] = g_k
                v_kv2[s, head(heads + j), span] = g_v
            gq[own, :] = jnp.concatenate(queries, axis=1).astype(LOW)
            return carry

        lax.fori_loop(0, captions, body, 0)
        v_g[...] += dot(gq[...], v_w2[s])

        def of_keys(half):
            total = 0
            for caption in range(captions):
                span = slice(caption * images, (caption + 1) * images)
                features = v_img[caption, 2 * half : 2 * half + 2].reshape(width // 2, images)
                total = total + dot_rows(features, v_kv2[s, :, span])
            return total

        gradients(v_in, s, of_keys, v_o2)

    for i, s in enumerate(order):
        cross_back(s)
        if i == 0:
            offer(2, 0)
            advance(0, 1, 1)
            advance(1, 1, 1)
            advance(0, 0, 2)
        if i == 1:
            advance(1, 0, 2)
            advance(2, 0, 0)
            advance(0, 0, 3)
        if i == 2:
            offer(2, 1)
            advance(1, 0, 3)
            advance(0, 1, 2)
        if i == 3:
            advance(1, 1, 2)
            if stages(2, 0) > 1:
                advance(2, 0, 1)
    image_span = pl.ds(t * captions, captions)

    def image_part(caption, carry):
        span = pl.ds(pl.multiple_of(caption * images, images), images)
        values = dot(v_turned[...], v_kv2[:, :, span].reshape(8 * part, images))
        v_image[caption] = values.astype(LOW).reshape(4, part, images)
        return carry

    lax.fori_loop(0, captions, image_part, 0)
    advance(2, 1, 0)
    image_moves = [
        copies.to(v_image.at[:, target], image_out.at[image_span], near[name])
        for name, target in (("y", flipped(t, 2)), ("far", 3 - t), ("core", flipped(t, 1)))
    ]
    back.append(copies.move(v_image.at[:, t], image_out.at[image_span]))
    gain_sum, bias_sum, total = norm_back(v_x1, g["ln2g"], v_f0, v_f1, v_grads)
    keep(3, gain_sum)
    keep(4, bias_sum)
    keep(2, total)
    advance(0, 1, 3)
    advance(1, 1, 3)

    again(v_tokens, g["ln1g"], g["ln1b"])
    v_turn_a[...] = v_h[...].T
    v_turn_b[...] = v_grads[...].T
    causal = window_allowed(length, window)

    def self_back(s):
        go[...] = dot_rows(v_grads[...], v_w1[s]).astype(LOW)
        for w in range(rows // window):
            span = pl.ds(w * window, window)
            all_q, all_go, queries = v_q1[s, span, :], go[span, :], []
            for j in range(heads):
                q, k, v = all_q[:, lanes(j)], v_kv1[s, head(j), span], v_kv1[s, head(heads + j), span]
                p = softmax(dot(q, k), causal)
                g_q, g_k, g_v = attend_back(p, q, k, v, all_go[:, lanes(j)])
                queries.append(g_q)
                v_kv1[s, head(j), span] = g_k
                v_kv1[s, head(heads + j), span] = g_v
            gq[span, :] = jnp.concatenate(queries, axis=1).astype(LOW)
        v_g[...] += dot(gq[...], v_w0[s, :part, :]) + dot_columns(v_kv1[s], v_w0[s, part:, :])

        def of_keys(half):
            return dot_rows(v_turn_a[half_rows(half), :], v_kv1[s])

        gradients(v_out, s, of_keys, v_o1)

    for i, s in enumerate(order):
        self_back(s)
        if i == 0:
            offer(3, 0)
            if stages(2, 0) > 1:
                advance(2, 0, 2)
            advance(2, 1, 1)
        if i == 1:
            advance(3, 0, 0)
        if i == 2:
            offer(3, 1)
            if stages(2, 0) > 1:
                advance(2, 0, 3)
            advance(2, 1, 2)
        if i == 3:
            if stages(3, 0) > 1:
                advance(3, 0, 1)
    advance(3, 1, 0)
    gain_sum, bias_sum, _ = norm_back(v_tokens, g["ln1g"], v_f1, None, v_h)
    keep(0, gain_sum)
    keep(1, bias_sum)
    token_moves = shared(v_h, token_all)
    for s in range(4):
        v_sum[0, 9 + s : 10 + s, :] = v_small_a[s]
    v_sum[0, 13:16, :] = jnp.zeros((3, width), HIGH)
    small_to = [near["core"], *partner, near["y"]]

    def total_step(i):
        made = copies.to(v_sum.at[i], sum_in.at[i], small_to[i])
        made.wait_recv()
        v_sum[i + 1] = v_sum[i] + sum_in[i]

    advance(2, 1, 3)
    total_step(0)
    total_step(1)
    if stages(3, 0) > 1:
        advance(3, 0, 2)
    advance(3, 1, 1)
    total_step(2)
    total_step(3)
    if stages(3, 0) > 1:
        advance(3, 0, 3)
    advance(3, 1, 2)
    total_step(4)
    back.append(copies.move(v_sum.at[5], small_out))
    advance(3, 1, 3)
    for made in out_moves + image_moves + token_moves:
        made.wait_recv()
    copies.drain()
    for made in back:
        made.wait()


def backward(dims, stride, counts, vec, bias, bias_all, tokens, grads, raw, kept, w_back, turned, mlp):
    captions, length, images, width, part = dims
    rows = captions * length
    block = width // 8
    plan = ((0, 1, 2, "y"), (1, 0, 2, "y"), ("y", 0, 1, 2), (0, 1, 2, "y"))
    shape = jax.ShapeDtypeStruct
    any_spec = pl.BlockSpec(memory_space=pl.ANY)
    vmem, smem = pl.BlockSpec(memory_space=pltpu.VMEM), pl.BlockSpec(memory_space=pltpu.SMEM)
    whole = (2, 2, 2, 2, 2, block, width)
    raw = [w.reshape(whole[2:]) for w in raw]
    mlp = [w.reshape(whole) for w in mlp]
    remote = 8 * 6 + 4 * 3 + 5

    def scratch(*size, dtype=LOW):
        return pltpu.VMEM(size, dtype)

    flat = [scratch(*k.shape, dtype=k.dtype) for k in kept]
    return pl.pallas_call(
        lambda *refs: backward_kernel(
            dims,
            stride,
            plan,
            refs[:8],
            refs[8:17],
            refs[17:21],
            refs[21],
            refs[22],
            refs[23],
            refs[24:28],
            *refs[28:],
        ),
        out_shape=[shape((block, width), HIGH)] * 4
        + [
            shape((4 * captions, part, images), LOW),
            shape((4 * rows, width), LOW),
            shape((4 * rows, width), LOW),
            shape((16, width), HIGH),
        ],
        in_specs=[smem, vmem] + [any_spec] * 22,
        out_specs=[any_spec] * 8,
        scratch_shapes=[
            flat,
            [scratch(*w.shape) for w in w_back],
            scratch(*turned.shape),
            scratch(*whole),
            scratch(*whole),
            scratch(4, 1, width, dtype=HIGH),
            scratch(rows, width),
            scratch(rows, width),
            scratch(*whole),
            scratch(*whole),
            scratch(rows, width),
            scratch(width, rows),
            scratch(width, rows),
            scratch(rows, width, dtype=HIGH),
            scratch(rows, width, dtype=HIGH),
            scratch(rows, width, dtype=HIGH),
            scratch(rows, width, dtype=HIGH),
            scratch(4, 1, width, dtype=HIGH),
            scratch(2, rows, width),
            scratch(2, rows, part),
            scratch(captions, 4, part, images),
            scratch(4, 2, 2, 2, block, width),
            [
                scratch(8, 2, 2, block, width),
                scratch(8, 2, block, width),
                scratch(8, block, width),
            ],
            [
                scratch(*((2, 2, 2) if turn[0] == "y" else ()), block, width)
                for turn in plan
            ],
            scratch(4, block, width, dtype=HIGH),
            scratch(6, 16, width, dtype=HIGH),
            scratch(5, 16, width, dtype=HIGH),
            pltpu.SemaphoreType.REGULAR((4,)),
            pltpu.SemaphoreType.DMA((remote,)),
            pltpu.SemaphoreType.DMA((remote,)),
            pltpu.SemaphoreType.DMA((48,)),
        ],
        name="backward",
        compiler_params=pltpu.CompilerParams(
            collective_id=1, has_side_effects=True, vmem_limit_bytes=67043328
        ),
    )(counts, vec, bias, bias_all, tokens, grads, *raw, *kept, *w_back, turned, *mlp)


def local(
    tokens,
    image_tokens,
    image_counts,
    ln1_gain,
    ln1_bias,
    self_qkv,
    self_output_weight,
    self_output_bias,
    ln2_gain,
    ln2_bias,
    cross_query_weight,
    cross_kv,
    cross_output_weight,
    cross_output_bias,
    ln3_gain,
    ln3_bias,
    mlp_in,
    mlp_in_bias,
    mlp_out,
    mlp_out_bias,
    grad_out,
):
    stride = lax.axis_size("dp") // 8
    all_captions, length, width = tokens.shape
    images, part = image_tokens.shape[1:]
    captions = all_captions // 4
    dims = (captions, length, images, width, part)
    rows = [
        ln1_gain,
        ln1_bias,
        self_output_bias,
        ln2_gain,
        ln2_bias,
        cross_output_bias,
        ln3_gain,
        ln3_bias,
        mlp_out_bias,
    ]
    vec = jnp.concatenate([jnp.stack(rows), jnp.zeros((7, width), HIGH)])
    tokens = tokens.reshape(-1, width)
    grads = grad_out.reshape(-1, width)
    bias = mlp_in_bias.reshape(1, -1)
    weights = [
        self_qkv.transpose(1, 2, 0).reshape(3 * part, width),
        self_output_weight,
        cross_query_weight.T,
        cross_kv.transpose(1, 2, 0).reshape(2 * part, width),
        cross_output_weight,
        mlp_in,
        mlp_out,
    ]
    *kept, w_back, turned, w_in, w_out, bias_all = forward(
        dims, image_counts, vec, tokens, image_tokens.transpose(0, 2, 1), bias, weights
    )
    sum_out, sum_in, sum_cross, sum_self, grad_image, output, grad_tokens, small = backward(
        dims,
        stride,
        image_counts,
        vec,
        bias,
        bias_all,
        tokens,
        grads,
        (mlp_in, mlp_out),
        kept,
        w_back,
        turned,
        (w_in, w_out),
    )
    if stride > 1:
        groups = [[hi * stride + lo for lo in range(stride)] for hi in range(8)]
        sum_out, sum_in, sum_cross, sum_self = (
            lax.psum_scatter(s, "dp", scatter_dimension=0, axis_index_groups=groups, tiled=True)
            for s in (sum_out, sum_in, sum_cross, sum_self)
        )
        small = lax.psum(small, "dp", axis_index_groups=groups)
    own_bias = lax.dynamic_index_in_dim(small, 9 + lax.axis_index("tensor"), 0, keepdims=False)
    keys, rest = slice(0, part), slice(part, 2 * part)
    third, fourth = slice(2 * part, 3 * part), slice(3 * part, 4 * part)
    return (
        output.reshape(all_captions, length, width),
        grad_tokens.reshape(all_captions, length, width),
        grad_image.transpose(0, 2, 1),
        small[0],
        small[1],
        jnp.stack([sum_self[:, third], sum_self[:, keys], sum_self[:, rest]], axis=1),
        sum_self[:, fourth].T,
        small[2],
        small[3],
        small[4],
        sum_cross[:, third],
        sum_cross[:, : 2 * part].reshape(-1, 2, part),
        sum_cross[:, fourth].T,
        small[5],
        small[6],
        small[7],
        sum_in,
        own_bias,
        sum_out.T,
        small[8],
    )


def solution(mesh):
    return jax.shard_map(
        local,
        mesh=mesh,
        in_specs=(
            P("dp", None, None),
            P("dp", None, "tensor"),
            P("dp"),
            P(),
            P(),
            P(None, None, "tensor"),
            P("tensor", None),
            P(),
            P(),
            P(),
            P(None, "tensor"),
            P(None, None, "tensor"),
            P("tensor", None),
            P(),
            P(),
            P(),
            P(None, "tensor"),
            P("tensor"),
            P("tensor", None),
            P(),
            P("dp", None, None),
        ),
        out_specs=(
            P("dp", None, None),
            P("dp", None, None),
            P("dp", None, "tensor"),
            P(),
            P(),
            P("dp", None, "tensor"),
            P("tensor", "dp"),
            P(),
            P(),
            P(),
            P("dp", "tensor"),
            P("dp", None, "tensor"),
            P("tensor", "dp"),
            P(),
            P(),
            P(),
            P("dp", "tensor"),
            P("tensor"),
            P("tensor", "dp"),
            P(),
        ),
        check_vma=False,
    )
```

```python
from functools import partial

import jax
import jax.numpy as jnp
from jax import lax
from jax.experimental import pallas as pl
from jax.experimental.pallas import tpu as pltpu
from jax.sharding import PartitionSpec as P

HEAD_SIZE = 64
LOW = jnp.bfloat16
HIGH = jnp.float32
MESH = pl.DeviceIdType.MESH
SCALING = HEAD_SIZE**-0.5


def dot(left, right):
    return jnp.dot(left, right, preferred_element_type=HIGH)


def dot_rows(left, right):
    return lax.dot_general(left, right, (((1,), (1,)), ((), ())), preferred_element_type=HIGH)


def dot_columns(left, right):
    return lax.dot_general(left, right, (((0,), (0,)), ((), ())), preferred_element_type=HIGH)


def norm_parts(values):
    center = values - jnp.mean(values, axis=-1, keepdims=True)
    inv_std = lax.rsqrt(jnp.mean(center * center, axis=-1, keepdims=True) + 1e-05)
    return center * inv_std, inv_std


def folded(values):
    return jnp.sum(values.reshape(values.shape[0] // 8, 8, values.shape[1]), axis=0)


def flipped(value, step):
    return value + step * (1 - 2 * lax.rem(value // step, 2))


def peers():
    d, t = lax.axis_index("dp"), lax.axis_index("tensor")
    return {"core": (d, flipped(t, 1)), "y": (d, flipped(t, 2)), "far": (d, 3 - t)}


def greet(devices):
    barrier = pltpu.get_barrier_semaphore()
    for device in devices:
        pl.semaphore_signal(barrier, inc=1, device_id=device, device_id_type=MESH)
    pl.semaphore_wait(barrier, len(devices))


class Copies:
    def __init__(self, send, recv, local):
        self.send, self.recv, self.local = send, recv, local
        self.remotes, self.locals = [], 0

    def to(self, source, target, device):
        slot = len(self.remotes)
        assert slot < self.send.shape[0]
        made = pltpu.make_async_remote_copy(
            src_ref=source,
            dst_ref=target,
            send_sem=self.send.at[slot],
            recv_sem=self.recv.at[slot],
            device_id=device,
            device_id_type=MESH,
        )
        made.start()
        self.remotes.append(made)
        return made

    def move(self, source, target):
        assert self.locals < self.local.shape[0]
        made = pltpu.make_async_copy(source, target, self.local.at[self.locals])
        made.start()
        self.locals += 1
        return made

    def drain(self):
        for made in self.remotes:
            made.wait_send()


def softmax(scores, allowed):
    scores = jnp.where(allowed, scores * SCALING, -1000000000.0)
    exponent = jnp.exp(scores - jnp.max(scores, axis=-1, keepdims=True))
    return exponent / jnp.sum(exponent, axis=-1, keepdims=True)


def window_allowed(length, window, heads):
    row = lax.rem(lax.broadcasted_iota(jnp.int32, (heads * window, window), 0), window)
    column = lax.broadcasted_iota(jnp.int32, (heads * window, window), 1)
    return (row // length == column // length) & (row >= column)


def head_masks(width, dtype):
    lane = lax.broadcasted_iota(jnp.int32, (1, width), 1) // HEAD_SIZE
    return [(lane == j).astype(dtype) for j in range(width // HEAD_SIZE)]


def spread(values, masks):
    return jnp.concatenate([values * mask for mask in masks], axis=0)


def gathered(values, masks):
    n = values.shape[0] // len(masks)
    total = 0
    for j, mask in enumerate(masks):
        total = total + values[j * n : (j + 1) * n] * mask
    return total


FORWARD_VEC = ("ln1g", "ln1b", "sob", "ln2g", "ln2b", "cob")
BACKWARD_VEC = ("ln1g", "ln1b", "ln2g", "ln2b", "ln3g", "ln3b", "mob")


def as_rows(names, refs):
    return {name: ref[...].reshape(1, -1) for name, ref in zip(names, refs)}


def forward_kernel(dims, *refs):
    captions, length, images, width, part = dims
    rows = captions * length
    (counts, *vec), refs = refs[:7], refs[7:]
    (tokens, image, *weights), refs = refs[:7], refs[7:]
    (q1, kv1, o1, x1, q2, kv2, o2, x2, img, w_back, kv_turned), refs = refs[:11], refs[11:]
    (
        (v_q1, v_kv1, v_o1, v_x1, v_q2, v_kv2, v_o2, v_x2, v_img),
        v_w,
        v_turned,
        v_tokens,
        v_h,
        send,
        recv,
        local,
    ) = refs
    d, t = lax.axis_index("dp"), lax.axis_index("tensor")
    near = {"p0": (flipped(d, 1), t), "p1": (flipped(d, 2), t), **peers()}
    order = [t, flipped(t, 1), flipped(t, 2), 3 - t]
    copies = Copies(send, recv, local)
    token_load = copies.move(tokens.at[pl.ds(t * rows, rows)], v_tokens)
    loads = [copies.move(weights[k], v_w[k].at[t]) for k in range(5)]
    image_load = copies.move(image.at[pl.ds(t * captions, captions)], v_img.at[:, t])
    g = as_rows(FORWARD_VEC, vec)
    greet(list(near.values()))
    quarter = lax.rem(d, 4)
    quarters = (quarter, flipped(quarter, 1), flipped(quarter, 2), 3 - quarter)
    other = order[2]

    def part_of(k, which, half=None):
        size = weights[k].shape[0] // 4
        start = quarters[which] * size
        if half is not None:
            first = (size // 2 + 15) // 16 * 16
            start, size = (start, first) if half == 0 else (start + first, size - first)
        return pl.ds(pl.multiple_of(start, 16), size)

    def region(k, which, half=None):
        return v_w[k].at[other, part_of(k, which, half)]

    count = len(weights)
    over_y, over, own_core = {}, {}, {}

    def send_y(k):
        over_y[k] = copies.to(
            weights[k].at[part_of(k, 0)], v_w[k].at[t, part_of(k, 0)], near["y"]
        )

    for k in range(count):
        own_core[k] = copies.to(weights[k], v_w[k].at[t], near["core"])
        send_y(k)
    images_in = [
        [
            copies.to(image.at[target * captions + caption], v_img.at[caption, t], near[name])
            for name, target in (("y", order[2]), ("far", order[3]), ("core", order[1]))
        ]
        for caption in range(captions)
    ]
    core = {k: [] for k in range(count)}

    def first(k):
        over_y[k].wait_recv()
        over[k, 0] = copies.to(region(k, 0), region(k, 0), near["p0"])
        over[k, 1] = copies.to(region(k, 0), region(k, 0), near["p1"])
        core[k].append(copies.to(region(k, 0), region(k, 0), near["core"]))

    def second(k):
        over[k, 0].wait_recv()
        over[k, 2] = copies.to(region(k, 1, 0), region(k, 1, 0), near["p1"])
        core[k].append(copies.to(region(k, 1), region(k, 1), near["core"]))
        over[k, 1].wait_recv()
        over[k, 3] = copies.to(region(k, 2, 1), region(k, 2, 1), near["p0"])
        core[k].append(copies.to(region(k, 2), region(k, 2), near["core"]))

    def third(k):
        over[k, 2].wait_recv()
        core[k].append(copies.to(region(k, 3, 0), region(k, 3, 0), near["core"]))
        over[k, 3].wait_recv()
        core[k].append(copies.to(region(k, 3, 1), region(k, 3, 1), near["core"]))

    def arrived(k):
        for made in core[k]:
            made.wait_recv()

    slab = 32

    def normed(source, gain, shift):
        def body(i, carry):
            place = pl.ds(pl.multiple_of(i * slab, slab), slab)
            n, _ = norm_parts(source[place, :].astype(HIGH))
            v_h[place, :] = (n * gain + shift).astype(LOW)
            return carry

        lax.fori_loop(0, rows // slab, body, 0)

    token_load.wait()
    normed(v_tokens, g["ln1g"], g["ln1b"])

    def start_sum(target, source, shift):
        def body(i, carry):
            place = pl.ds(pl.multiple_of(i * slab, slab), slab)
            target[place, :] = source[place, :].astype(HIGH) + shift
            return carry

        lax.fori_loop(0, rows // slab, body, 0)

    start_sum(v_x1, v_tokens, g["sob"])
    window = 2 * length
    heads = part // HEAD_SIZE
    causal = window_allowed(length, window, heads)
    masks, wide_masks = head_masks(part, LOW), head_masks(part, HIGH)

    def self_part(s):
        h = v_h[...]
        v_q1[s] = dot_rows(h, v_w[0][s, :part, :]).astype(LOW)
        v_kv1[s] = dot_rows(v_w[0][s, part:, :], h).astype(LOW)
        for w in range(rows // window):
            span = pl.ds(w * window, window)
            q = spread(v_q1[s, span, :], masks)
            p = softmax(dot(q, v_kv1[s, :part, span]), causal)
            mixed = dot_rows(p.astype(LOW), v_kv1[s, part:, span])
            v_o1[s, span, :] = gathered(mixed, wide_masks).astype(LOW)
        v_x1[...] += dot(v_o1[s], v_w[1][s])

    def queries(s):
        v_q2[s] = dot_rows(v_h[...], v_w[2][s]).astype(LOW)

    def turn(s):
        v_turned[:, pl.ds(pl.multiple_of(s * 2 * part, 128), 2 * part)] = v_w[3][s].T

    def cross_part(c):
        allowed = lax.broadcasted_iota(jnp.int32, (1, images), 1) < counts[t * captions + c]
        span, own = pl.ds(c * images, images), pl.ds(c * length, length)

        def body(s, carry):
            kv = dot(v_w[3][s], v_img[c].reshape(width, images)).astype(LOW)
            v_kv2[s, :, span] = kv
            q = spread(v_q2[s, own, :], masks)
            p = softmax(dot(q, kv[:part]), allowed)
            mixed = dot_rows(p.astype(LOW), kv[part:])
            v_o2[s, own, :] = gathered(mixed, wide_masks).astype(LOW)
            return carry

        lax.fori_loop(0, 4, body, 0)

    back = []
    loads[0].wait()
    loads[1].wait()
    self_part(order[0])
    own_core[0].wait_recv()
    own_core[1].wait_recv()
    first(0)
    self_part(order[1])
    first(1)
    first(2)
    second(0)
    first(3)
    second(1)
    first(4)
    third(0)
    second(2)
    third(1)
    second(3)
    arrived(0)
    arrived(1)
    self_part(order[2])
    third(2)
    second(4)
    self_part(order[3])
    third(3)
    third(4)
    back.append(copies.move(v_q1, q1))
    back.append(copies.move(v_kv1, kv1))
    back.append(copies.move(v_o1, o1))
    back.append(copies.move(v_x1, x1))
    normed(v_x1, g["ln2g"], g["ln2b"])
    for k in range(2, 5):
        loads[k].wait()
        own_core[k].wait_recv()
        arrived(k)
    for s in order:
        queries(s)
        turn(s)
    back.append(copies.move(v_turned, kv_turned))
    for i, k in enumerate((0, 1, 2, 4)):
        back.append(copies.move(v_w[k], w_back[i]))
    back.append(copies.move(v_q2, q2))
    start_sum(v_x2, v_x1, g["cob"])
    image_load.wait()
    for caption in range(captions):
        for made in images_in[caption]:
            made.wait_recv()
        cross_part(caption)
    back.append(copies.move(v_img, img))
    back.append(copies.move(v_kv2, kv2))
    back.append(copies.move(v_o2, o2))
    for s in range(4):
        v_x2[...] += dot(v_o2[s], v_w[4][s])
    back.append(copies.move(v_x2, x2))
    copies.drain()
    for made in back:
        made.wait()


def forward(dims, counts, vec, tokens, image, weights):
    captions, length, images, width, part = dims
    rows = captions * length
    shape = jax.ShapeDtypeStruct
    kept = [
        ((4, rows, part), LOW),
        ((4, 2 * part, rows), LOW),
        ((4, rows, part), LOW),
        ((rows, width), HIGH),
        ((4, rows, part), LOW),
        ((4, 2 * part, captions * images), LOW),
        ((4, rows, part), LOW),
        ((rows, width), HIGH),
        ((captions, 4, part, images), LOW),
    ]
    sizes = [(4, *w.shape) for w in weights]
    any_spec = pl.BlockSpec(memory_space=pl.ANY)
    vmem, smem = pl.BlockSpec(memory_space=pltpu.VMEM), pl.BlockSpec(memory_space=pltpu.SMEM)
    remote = 5 * 11 + 3 * captions
    return pl.pallas_call(
        partial(forward_kernel, dims),
        out_shape=[shape(*k) for k in kept]
        + [
            [shape(sizes[k], LOW) for k in (0, 1, 2, 4)],
            shape((width, 8 * part), LOW),
        ],
        in_specs=[smem] + [vmem] * 6 + [any_spec] * 7,
        out_specs=[any_spec] * 9 + [[any_spec] * 4] + [any_spec],
        scratch_shapes=[
            [pltpu.VMEM(*k) for k in kept],
            [pltpu.VMEM(sizes[k], LOW) for k in range(5)],
            pltpu.VMEM((width, 8 * part), LOW),
            pltpu.VMEM((rows, width), LOW),
            pltpu.VMEM((rows, width), LOW),
            pltpu.SemaphoreType.DMA((remote,)),
            pltpu.SemaphoreType.DMA((remote,)),
            pltpu.SemaphoreType.DMA((32,)),
        ],
        name="forward",
        compiler_params=pltpu.CompilerParams(
            collective_id=0, has_side_effects=True, vmem_limit_bytes=62 << 20
        ),
    )(counts, *vec, tokens, image, *weights)


def backward_kernel(dims, stride, *refs):
    captions, length, images, width, part = dims
    rows = captions * length
    block, wide = width // 8, width // 2
    heads = part // HEAD_SIZE
    window = 2 * length
    (
        counts,
        vec,
        (bias, tokens, grads, raw_in, raw_out),
        (q1, kv1, o1, x1, q2, kv2, o2, x2, img),
        w_back,
        kv_turned,
        sums,
        image_out,
        out_all,
        token_all,
        small_out,
        (v_q1, v_kv1, v_o1, v_x1, v_q2, v_kv2, v_o2, v_x2, v_img),
        (v_w0, v_w1, v_w2, v_w4),
        v_turned,
        (v_in, v_out, g_out, g_in, g_cross, g_self),
        v_bias,
        v_tokens,
        v_grads,
        v_h3,
        v_h,
        v_turn_a,
        v_turn_b,
        v_f0,
        v_f1,
        v_y,
        v_g,
        v_low,
        v_parts,
        v_narrow,
        from_core,
        halves,
        from_y,
        result,
        v_sum,
        sum_in,
        credit,
        send,
        recv,
        local,
    ) = refs
    d, t = lax.axis_index("dp"), lax.axis_index("tensor")
    y, c = t // 2, lax.rem(t, 2)
    near = peers()
    bits = [lax.rem(d // (stride << b), 2) for b in range(3)]
    partner = [(flipped(d, stride << b), t) for b in range(3)]
    order = [3 - t, flipped(t, 2), flipped(t, 1), t]
    copies = Copies(send, recv, local)

    mine = pl.ds(t * rows, rows)
    load_x2 = copies.move(x2, v_x2)
    load_grads = [
        copies.move(grads.at[mine], v_grads.at[0]),
        copies.move(grads.at[pl.ds(flipped(t, 2) * rows, rows)], v_grads.at[1]),
    ]
    load_mlp = [copies.move(raw_in, v_in.at[c]), copies.move(raw_out, v_out.at[c])]
    load_rest = [
        copies.move(a, b)
        for a, b in (
            (w_back[3], v_w4),
            (q2, v_q2),
            (kv2, v_kv2),
            (o2, v_o2),
            (x1, v_x1),
            (img, v_img),
            (w_back[2], v_w2),
            (kv_turned, v_turned),
            (w_back[1], v_w1),
            (w_back[0], v_w0),
            (q1, v_q1),
            (kv1, v_kv1),
            (o1, v_o1),
            (tokens.at[mine], v_tokens),
        )
    ]
    greet([*near.values(), *partner])
    mlp_in = [
        copies.to(raw_in, v_in.at[c], near["core"]),
        copies.to(raw_out, v_out.at[c], near["core"]),
        copies.to(bias, v_bias, near["core"]),
    ]

    g = as_rows(BACKWARD_VEC, vec)
    slab = 32

    def loop(body, init, step=slab):
        def run(i, carry):
            return body(pl.ds(pl.multiple_of(i * step, step), step), carry)

        return lax.fori_loop(0, rows // step, run, init)

    zeros = jnp.zeros((8, width), HIGH)

    def keep(name, total):
        v_sum[0, name : name + 1, :] = jnp.sum(total, axis=0, keepdims=True)

    pieces = [g_out, g_in, g_cross, g_self]
    plan = {
        (0, 0): (0, 1, 2),
        (0, 1): (1, 0, 2),
        (1, 0): (0, 1, 2),
        (1, 1): (1, 0, 2),
        (2, 0): ("y", 0, 1, 2),
        (2, 1): (0, 1, 2, "y"),
        (3, 0): (0, 1, 2, "y"),
        (3, 1): (1, 0, 2, "y"),
    }
    units = [(p, o, h) for p in range(4) for o in ((1,) if p < 2 else (0, 1)) for h in (0, 1)]
    y_places = {(2, 0): from_y[0], (2, 1): from_y[1], (3, 0): from_y[2], (3, 1): from_y[3]}
    to_core, hops, places = {}, {}, {}
    side = (1 - y, y)

    def lanes(h):
        return pl.ds(h * wide, wide)

    def slot(p, o):
        return p if p < 2 else 2 + o if p == 2 else o

    def own(p, o, core):
        return (core,) if p < 2 else (side[o], core)

    def offer(p, o):
        if p == 3:
            pl.semaphore_wait(credit.at[o], 1)
        to_core[p, o] = copies.to(
            pieces[p].at[own(p, o, 1 - c)], from_core.at[slot(p, o)], near["core"]
        )

    def add(target, left, *others):
        lead = left.shape[:-2]
        total = 1
        for size in lead:
            total *= size
        low = len(others) == 1 and target.dtype == LOW

        def body(i, carry):
            index, rest = [], i
            for size in reversed(lead):
                index.insert(0, lax.rem(rest, size))
                rest = rest // size
            place = (*index, slice(None), slice(None))
            value = left[place] if low else left[place].astype(HIGH)
            for ref in others:
                value = value + (ref[place] if low else ref[place].astype(HIGH))
            target[place] = value.astype(target.dtype)
            return carry

        if total == 1:
            body(0, 0)
        else:
            lax.fori_loop(0, total, body, 0)

    def cut(bit, left, value):
        return tuple(value if b == bit else slice(None) for b in sorted(left, reverse=True))

    back = []

    def advance(p, o, h, stage):
        u = units.index((p, o, h))
        turn = plan[p, h]
        y_first, with_y = turn[0] == "y", "y" in turn
        xyz = [b for b in turn if b != "y"]
        if stage == 0:
            base = pieces[p].at[(*own(p, o, c), *[slice(None)] * 4, lanes(h))]
            sent = from_core.at[(slot(p, o), *[slice(None)] * 4, lanes(h))]
            if (p, o, "core") not in places:
                to_core[p, o].wait_recv()
                places[p, o, "core"] = True
            if y_first and o == 1:
                hops[p, 0, h, "y"].wait_recv()
                add(base, base, sent, y_places[p, h])
            else:
                add(base, base, sent)
            places[u] = base, [0, 1, 2]
            if y_first and o == 0:
                hops[p, 0, h, "y"] = copies.to(base, y_places[p, h], near["y"])
                return
        if stage > 0:
            source, left = places[u]
            bit = xyz[stage - 1]
            hops[p, o, h, stage].wait_recv()
            target = halves[stage - 1].at[u]
            kept = source.at[cut(bit, left, bits[bit])]
            remaining = [b for b in left if b != bit]
            last = stage == 3
            if last and o == 1:
                total = result.at[p, :, lanes(h)]
                if y_first or not with_y:
                    add(total, target, kept)
                else:
                    hops[p, 0, h, "y"].wait_recv()
                    add(total, target, kept, y_places[p, h])
                back.append(copies.move(total, sums[p].at[:, lanes(h)]))
                return
            add(target, target, kept)
            places[u] = target, remaining
            if last:
                hops[p, 0, h, "y"] = copies.to(target, y_places[p, h], near["y"])
                return
        source, left = places[u]
        bit = xyz[stage]
        hops[p, o, h, stage + 1] = copies.to(
            source.at[cut(bit, left, 1 - bits[bit])], halves[stage].at[u], partner[bit]
        )

    def free(o):
        pl.semaphore_signal(credit.at[o], inc=1, device_id=near["core"], device_id_type=MESH)

    def forth(p, o, stage):
        advance(p, o, 0, stage)
        advance(p, o, 1, stage)

    load_x2.wait()
    for load in load_grads:
        load.wait()

    def start(place, carry):
        n, _ = norm_parts(v_x2[place, :])
        v_h3[0, place, :] = (n * g["ln3g"] + g["ln3b"]).astype(LOW)
        return carry + folded(v_grads[0, place, :].astype(HIGH))

    keep(8, loop(start, zeros))
    rows_in = copies.to(v_h3.at[0], v_h3.at[1], near["y"])
    own_rows, other_rows = slice(0, rows), slice(rows, 2 * rows)
    v_turn_a[:, own_rows] = v_h3[0].T
    v_turn_b[:, own_rows] = v_grads[0].T
    v_turn_b[:, other_rows] = v_grads[1].T

    def weight(ref, e):
        return ref[e].reshape(width, width)

    def put(ref, index, first, values):
        half, values = values
        ref[(*index, half, slice(None), slice(None), slice(None), slice(first, first + values.shape[1]))] = (
            values.astype(LOW).reshape(2, 2, block, values.shape[1])
        )

    def half_rows(half):
        return pl.ds(half * (width // 2), width // 2)

    bias_sums = [zeros, zeros]
    hidden = g_self.reshape(4 * width, width)

    def hidden_rows(kind, i, r, size=rows):
        return hidden.at[pl.ds(((kind * 2 + i) * 2 + r) * rows, size)]

    def feed(i, r):
        e = 1 - c if i else c
        v_f0[...] = dot(v_h3[r], weight(v_in, e))
        v_f1[...] = dot_rows(v_grads[r], weight(v_out, e))
        shift = (v_bias if i else bias)[...].reshape(1, -1)

        v_u, v_ga = hidden_rows(0, i, r), hidden_rows(1, i, r)

        def act(place, carry):
            a = v_f0[place, :] + shift
            cumulative = 0.5 * (1.0 + lax.erf(a * (0.5**0.5)))
            density = jnp.exp(-0.5 * a * a) * 0.3989422804014327
            v_u[place, :] = (a * cumulative).astype(LOW)
            ga = (v_f1[place, :] * (cumulative + a * density)).astype(LOW)
            v_ga[place, :] = ga
            return carry + folded(ga.astype(HIGH))

        bias_sums[i] += loop(act, zeros, 16)
        if i == 0:
            v_y[r] = dot(v_u[...], weight(v_out, e))
            v_g[r] = dot_rows(v_ga[...], weight(v_in, e))
        else:
            v_y[r] += dot(v_u[...], weight(v_out, e))
            v_g[r] += dot_rows(v_ga[...], weight(v_in, e))

    for load in load_mlp:
        load.wait()
    feed(0, 0)
    for made in mlp_in:
        made.wait_recv()
    feed(1, 0)
    rows_in.wait_recv()
    feed(0, 1)
    feed(1, 1)

    def rounded(place, carry):
        v_low[0, place, :] = v_g[1, place, :].astype(LOW)
        v_low[1, place, :] = v_y[1, place, :].astype(LOW)
        return carry

    loop(rounded, 0)
    parts_in = [copies.to(v_low.at[i], v_parts.at[i], near["y"]) for i in range(2)]
    v_turn_a[:, other_rows] = v_h3[1].T
    for i in (1, 0):
        e = 1 - c if i else c
        u, ga = (hidden_rows(kind, i, 0, size=2 * rows)[...] for kind in (0, 1))
        for half in range(2):
            put(g_out, (e,), 0, (half, dot(v_turn_b[half_rows(half), :], u)))
            put(g_in, (e,), 0, (half, dot(v_turn_a[half_rows(half), :], ga)))
        if i == 1:
            offer(0, 1)
            offer(1, 1)
    for s in range(4):
        total = jnp.sum(jnp.where(c == s % 2, bias_sums[0], bias_sums[1]), axis=0, keepdims=True)
        v_sum[0, 9 + s : 10 + s, :] = jnp.where(y == s // 2, total, 0.0)
    v_sum[0, 13:16, :] = jnp.zeros((3, width), HIGH)
    for p in (0, 1):
        forth(p, 1, 0)
        free(p)

    def shared(source, target):
        place = target.at[pl.ds(t * rows, rows)]
        back.append(copies.move(source, place))
        return [copies.to(source, place, near[name]) for name in ("core", "y", "far")]

    def norm_back(source, gain, old, new, low, more=None):
        def body(place, carry):
            a, b, e = carry
            n, inv_std = norm_parts(source[place, :].astype(HIGH))
            gh = v_g[0, place, :]
            if more is not None:
                gh = gh + more[place, :].astype(HIGH)
            scaled = gh * gain
            grad = inv_std * (
                scaled
                - jnp.mean(scaled, axis=-1, keepdims=True)
                - n * jnp.mean(scaled * n, axis=-1, keepdims=True)
            )
            grad = old[place, :].astype(HIGH) + grad
            if new is not None:
                new[place, :] = grad
                e = e + folded(grad)
            low[place, :] = grad.astype(LOW)
            return a + folded(gh * n), b + folded(gh), e

        return loop(body, (zeros, zeros, zeros))

    def finish(place, carry):
        total = v_x2[place, :] + g["mob"] + v_y[0, place, :] + v_parts[1, place, :].astype(HIGH)
        v_low[2, place, :] = total.astype(LOW)
        return carry

    for made in parts_in:
        made.wait_recv()
    loop(finish, 0)
    out_moves = shared(v_low.at[2], out_all)
    own_grads = v_grads.at[0]
    gain_sum, bias_sum, total = norm_back(
        v_x2, g["ln3g"], own_grads, v_f0, own_grads, v_parts.at[0]
    )
    keep(6, gain_sum)
    keep(7, bias_sum)
    keep(5, total)

    for load in load_rest:
        load.wait()

    def again(source, gain, shift):
        def body(place, carry):
            n, _ = norm_parts(source[place, :].astype(HIGH))
            v_h[place, :] = (n * gain + shift).astype(LOW)
            v_g[0, place, :] = jnp.zeros((slab, width), HIGH)
            return carry

        loop(body, 0)

    again(v_x1, g["ln2g"], g["ln2b"])
    v_turn_a[:, own_rows] = v_h[...].T
    v_turn_b[:, own_rows] = v_grads[0].T
    go, gq = v_narrow.at[0], v_narrow.at[1]
    masks, wide_masks = head_masks(part, LOW), head_masks(part, HIGH)

    def attend_back(q, k, v, g_mix, allowed):
        q, g_mix = spread(q, masks), spread(g_mix, masks)
        p = softmax(dot(q, k), allowed)
        low_p = p.astype(LOW)
        gp = dot(g_mix, v)
        inner = jnp.sum(gp * p, axis=-1, keepdims=True)
        gs = (p * (gp - inner)).astype(LOW)
        return (
            (gathered(dot_rows(gs, k), wide_masks) * SCALING).astype(LOW),
            (dot_columns(q, gs) * SCALING).astype(LOW),
            dot_columns(g_mix, low_p).astype(LOW),
        )

    def gradients(piece, s, of_keys, o_kept):
        for half in range(2):
            index = (s // 2, lax.rem(s, 2))
            put(piece, index, 0, (half, of_keys(half)))
            both = [dot(v_turn_a[half_rows(half), own_rows], gq[...])]
            both.append(dot(v_turn_b[half_rows(half), own_rows], o_kept[s]))
            put(piece, index, 2 * part, (half, jnp.concatenate(both, axis=1)))

    def cross_back(s):
        go[...] = dot_rows(v_grads[0], v_w4[s]).astype(LOW)

        def body(caption, carry):
            span = pl.ds(pl.multiple_of(caption * images, images), images)
            own = pl.ds(pl.multiple_of(caption * length, length), length)
            allowed = (
                lax.broadcasted_iota(jnp.int32, (1, images), 1) < counts[t * captions + caption]
            )
            g_q, g_k, g_v = attend_back(
                v_q2[s, own, :], v_kv2[s, :part, span], v_kv2[s, part:, span], go[own, :], allowed
            )
            v_kv2[s, :part, span] = g_k
            v_kv2[s, part:, span] = g_v
            gq[own, :] = g_q
            return carry

        lax.fori_loop(0, captions, body, 0)
        v_g[0] += dot(gq[...], v_w2[s])

        def of_keys(half):
            total = 0
            for caption in range(captions):
                span = slice(caption * images, (caption + 1) * images)
                features = v_img[caption, 2 * half : 2 * half + 2].reshape(width // 2, images)
                total = total + dot_rows(features, v_kv2[s, :, span])
            return total

        gradients(g_cross, s, of_keys, v_o2)

    for i, s in enumerate(order):
        cross_back(s)
        if i == 0:
            offer(2, 0)
            forth(0, 1, 1)
        if i == 1:
            forth(1, 1, 1)
            forth(2, 0, 0)
        if i == 2:
            offer(2, 1)
            forth(0, 1, 2)
        if i == 3:
            forth(1, 1, 2)
            advance(2, 0, 1, 1)
            advance(2, 1, 1, 0)
    image_span = pl.ds(t * captions, captions)

    def image_part(caption, carry):
        span = pl.ds(pl.multiple_of(caption * images, images), images)
        values = dot(v_turned[...], v_kv2[:, :, span].reshape(8 * part, images))
        v_img[caption] = values.astype(LOW).reshape(4, part, images)
        return carry

    lax.fori_loop(0, captions, image_part, 0)
    forth(0, 1, 3)
    image_moves = [
        copies.to(v_img.at[:, target], image_out.at[image_span], near[name])
        for name, target in (("y", flipped(t, 2)), ("far", 3 - t), ("core", flipped(t, 1)))
    ]
    back.append(copies.move(v_img.at[:, t], image_out.at[image_span]))
    gain_sum, bias_sum, total = norm_back(v_x1, g["ln2g"], v_f0, v_f1, own_grads)
    keep(3, gain_sum)
    keep(4, bias_sum)
    keep(2, total)
    forth(1, 1, 3)
    advance(2, 1, 0, 0)
    advance(2, 0, 1, 2)

    again(v_tokens, g["ln1g"], g["ln1b"])
    v_turn_a[:, own_rows] = v_h[...].T
    v_turn_b[:, own_rows] = v_grads[0].T
    causal = window_allowed(length, window, heads)

    def self_back(s):
        go[...] = dot_rows(v_grads[0], v_w1[s]).astype(LOW)
        for w in range(rows // window):
            span = pl.ds(w * window, window)
            g_q, g_k, g_v = attend_back(
                v_q1[s, span, :], v_kv1[s, :part, span], v_kv1[s, part:, span], go[span, :], causal
            )
            v_kv1[s, :part, span] = g_k
            v_kv1[s, part:, span] = g_v
            gq[span, :] = g_q
        v_g[0] += dot(gq[...], v_w0[s, :part, :]) + dot_columns(v_kv1[s], v_w0[s, part:, :])

        def of_keys(half):
            return dot_rows(v_turn_a[half_rows(half), own_rows], v_kv1[s])

        gradients(g_self, s, of_keys, v_o1)

    for i, s in enumerate(order):
        self_back(s)
        if i == 0:
            offer(3, 0)
            advance(2, 1, 1, 1)
            advance(2, 1, 0, 1)
            advance(2, 0, 1, 3)
        if i == 1:
            forth(3, 0, 0)
            advance(2, 1, 1, 2)
        if i == 2:
            offer(3, 1)
            advance(2, 1, 0, 2)
        if i == 3:
            forth(3, 0, 1)
            forth(2, 1, 3)
    forth(3, 1, 0)
    gain_sum, bias_sum, _ = norm_back(v_tokens, g["ln1g"], v_f1, None, v_h)
    keep(0, gain_sum)
    keep(1, bias_sum)
    small_to = [near["core"], *partner, near["y"]]
    small = []

    def total_start():
        i = len(small)
        small.append(copies.to(v_sum.at[i], sum_in.at[i], small_to[i]))

    def total_end():
        i = len(small) - 1
        small[i].wait_recv()
        v_sum[i + 1] = v_sum[i] + sum_in[i]

    total_start()
    token_moves = shared(v_h, token_all)
    forth(3, 0, 2)
    total_end()
    total_start()
    forth(3, 1, 1)
    total_end()
    total_start()
    forth(3, 0, 3)
    total_end()
    total_start()
    forth(3, 1, 2)
    total_end()
    total_start()
    forth(3, 1, 3)
    total_end()
    back.append(copies.move(v_sum.at[5], small_out))
    for made in out_moves + image_moves + token_moves:
        made.wait_recv()
    copies.drain()
    for made in back:
        made.wait()


def backward(dims, stride, counts, vec, bias, tokens, grads, raw, kept, w_back, turned):
    captions, length, images, width, part = dims
    rows = captions * length
    block, wide = width // 8, width // 2
    shape = jax.ShapeDtypeStruct
    any_spec = pl.BlockSpec(memory_space=pl.ANY)
    vmem, smem = pl.BlockSpec(memory_space=pltpu.VMEM), pl.BlockSpec(memory_space=pltpu.SMEM)
    shard = (2, 2, 2, block, width)
    raw = [w.reshape(shard) for w in raw]
    remote = 128

    def scratch(*size, dtype=LOW):
        return pltpu.VMEM(size, dtype)

    flat = [scratch(*k.shape, dtype=k.dtype) for k in kept]
    return pl.pallas_call(
        lambda *refs: backward_kernel(
            dims,
            stride,
            refs[0],
            refs[1:8],
            refs[8:13],
            refs[13:22],
            refs[22:26],
            refs[26],
            refs[27:31],
            *refs[31:],
        ),
        out_shape=[shape((block, width), HIGH)] * 4
        + [
            shape((4 * captions, part, images), LOW),
            shape((4 * rows, width), LOW),
            shape((4 * rows, width), LOW),
            shape((16, width), HIGH),
        ],
        in_specs=[smem] + [vmem] * 8 + [any_spec] * 18,
        out_specs=[any_spec] * 8,
        scratch_shapes=[
            flat,
            [scratch(*w.shape) for w in w_back],
            scratch(*turned.shape),
            [scratch(2, *shard)] * 4 + [scratch(2, 2, *shard)] * 2,
            scratch(*bias.shape, dtype=HIGH),
            scratch(rows, width),
            scratch(2, rows, width),
            scratch(2, rows, width),
            scratch(rows, width),
            scratch(width, 2 * rows),
            scratch(width, 2 * rows),
            scratch(rows, width, dtype=HIGH),
            scratch(rows, width, dtype=HIGH),
            scratch(2, rows, width, dtype=HIGH),
            scratch(2, rows, width, dtype=HIGH),
            scratch(3, rows, width),
            scratch(2, rows, width),
            scratch(2, rows, part),
            scratch(4, *shard),
            [
                scratch(12, 2, 2, block, wide),
                scratch(12, 2, block, wide),
                scratch(12, block, wide),
            ],
            [scratch(2, 2, 2, block, wide)] + [scratch(block, wide)] * 3,
            scratch(4, block, width, dtype=HIGH),
            scratch(6, 16, width, dtype=HIGH),
            scratch(5, 16, width, dtype=HIGH),
            pltpu.SemaphoreType.REGULAR((2,)),
            pltpu.SemaphoreType.DMA((remote,)),
            pltpu.SemaphoreType.DMA((remote,)),
            pltpu.SemaphoreType.DMA((48,)),
        ],
        name="backward",
        compiler_params=pltpu.CompilerParams(
            collective_id=1, has_side_effects=True, vmem_limit_bytes=67043328
        ),
    )(counts, *vec, bias, tokens, grads, *raw, *kept, *w_back, turned)


def local(
    tokens,
    image_tokens,
    image_counts,
    ln1_gain,
    ln1_bias,
    self_qkv,
    self_output_weight,
    self_output_bias,
    ln2_gain,
    ln2_bias,
    cross_query_weight,
    cross_kv,
    cross_output_weight,
    cross_output_bias,
    ln3_gain,
    ln3_bias,
    mlp_in,
    mlp_in_bias,
    mlp_out,
    mlp_out_bias,
    grad_out,
):
    stride = lax.axis_size("dp") // 8
    all_captions, length, width = tokens.shape
    images, part = image_tokens.shape[1:]
    captions = all_captions // 4
    dims = (captions, length, images, width, part)
    first = [ln1_gain, ln1_bias, self_output_bias, ln2_gain, ln2_bias, cross_output_bias]
    second = [ln1_gain, ln1_bias, ln2_gain, ln2_bias, ln3_gain, ln3_bias, mlp_out_bias]
    tokens = tokens.reshape(-1, width)
    grads = grad_out.reshape(-1, width)
    weights = [
        self_qkv.transpose(1, 2, 0).reshape(3 * part, width),
        self_output_weight,
        cross_query_weight.T,
        cross_kv.transpose(1, 2, 0).reshape(2 * part, width),
        cross_output_weight,
    ]
    *kept, w_back, turned = forward(
        dims, image_counts, first, tokens, image_tokens.transpose(0, 2, 1), weights
    )
    sum_out, sum_in, sum_cross, sum_self, grad_image, output, grad_tokens, small = backward(
        dims,
        stride,
        image_counts,
        second,
        mlp_in_bias,
        tokens,
        grads,
        (mlp_in, mlp_out),
        kept,
        w_back,
        turned,
    )
    if stride > 1:
        groups = [[hi * stride + lo for lo in range(stride)] for hi in range(8)]
        sum_out, sum_in, sum_cross, sum_self = (
            lax.psum_scatter(s, "dp", scatter_dimension=0, axis_index_groups=groups, tiled=True)
            for s in (sum_out, sum_in, sum_cross, sum_self)
        )
        small = lax.psum(small, "dp", axis_index_groups=groups)
    own_bias = lax.dynamic_index_in_dim(small, 9 + lax.axis_index("tensor"), 0, keepdims=False)
    keys, rest = slice(0, part), slice(part, 2 * part)
    third, fourth = slice(2 * part, 3 * part), slice(3 * part, 4 * part)
    return (
        output.reshape(all_captions, length, width),
        grad_tokens.reshape(all_captions, length, width),
        grad_image.transpose(0, 2, 1),
        small[0],
        small[1],
        jnp.stack([sum_self[:, third], sum_self[:, keys], sum_self[:, rest]], axis=1),
        sum_self[:, fourth].T,
        small[2],
        small[3],
        small[4],
        sum_cross[:, third],
        sum_cross[:, : 2 * part].reshape(-1, 2, part),
        sum_cross[:, fourth].T,
        small[5],
        small[6],
        small[7],
        sum_in,
        own_bias,
        sum_out.T,
        small[8],
    )


def solution(mesh):
    return jax.shard_map(
        local,
        mesh=mesh,
        in_specs=(
            P("dp", None, None),
            P("dp", None, "tensor"),
            P("dp"),
            P(),
            P(),
            P(None, None, "tensor"),
            P("tensor", None),
            P(),
            P(),
            P(),
            P(None, "tensor"),
            P(None, None, "tensor"),
            P("tensor", None),
            P(),
            P(),
            P(),
            P(None, "tensor"),
            P("tensor"),
            P("tensor", None),
            P(),
            P("dp", None, None),
        ),
        out_specs=(
            P("dp", None, None),
            P("dp", None, None),
            P("dp", None, "tensor"),
            P(),
            P(),
            P("dp", None, "tensor"),
            P("tensor", "dp"),
            P(),
            P(),
            P(),
            P("dp", "tensor"),
            P("dp", None, "tensor"),
            P("tensor", "dp"),
            P(),
            P(),
            P(),
            P("dp", "tensor"),
            P("tensor"),
            P("tensor", "dp"),
            P(),
        ),
        check_vma=False,
    )
```

```python
from functools import partial

import jax
import jax.numpy as jnp
from jax import lax
from jax.experimental import pallas as pl
from jax.experimental.pallas import tpu as pltpu
from jax.sharding import PartitionSpec as P

HEAD_SIZE = 64
LOW = jnp.bfloat16
HIGH = jnp.float32
MESH = pl.DeviceIdType.MESH
SCALING = HEAD_SIZE**-0.5


def dot(left, right):
    return jnp.dot(left, right, preferred_element_type=HIGH)


def dot_rows(left, right):
    return lax.dot_general(left, right, (((1,), (1,)), ((), ())), preferred_element_type=HIGH)


def dot_columns(left, right):
    return lax.dot_general(left, right, (((0,), (0,)), ((), ())), preferred_element_type=HIGH)


def norm_parts(values):
    center = values - jnp.mean(values, axis=-1, keepdims=True)
    inv_std = lax.rsqrt(jnp.mean(center * center, axis=-1, keepdims=True) + 1e-05)
    return center * inv_std, inv_std


def folded(values):
    return jnp.sum(values.reshape(values.shape[0] // 8, 8, values.shape[1]), axis=0)


def flipped(value, step):
    return value + step * (1 - 2 * lax.rem(value // step, 2))


def peers():
    d, t = lax.axis_index("dp"), lax.axis_index("tensor")
    return {"core": (d, flipped(t, 1)), "y": (d, flipped(t, 2)), "far": (d, 3 - t)}


def greet(devices):
    barrier = pltpu.get_barrier_semaphore()
    for device in devices:
        pl.semaphore_signal(barrier, inc=1, device_id=device, device_id_type=MESH)
    pl.semaphore_wait(barrier, len(devices))


class Copies:
    def __init__(self, send, recv, local):
        self.send, self.recv, self.local = send, recv, local
        self.remotes, self.locals = [], 0

    def to(self, source, target, device):
        slot = len(self.remotes)
        assert slot < self.send.shape[0]
        made = pltpu.make_async_remote_copy(
            src_ref=source,
            dst_ref=target,
            send_sem=self.send.at[slot],
            recv_sem=self.recv.at[slot],
            device_id=device,
            device_id_type=MESH,
        )
        made.start()
        self.remotes.append(made)
        return made

    def move(self, source, target):
        assert self.locals < self.local.shape[0]
        made = pltpu.make_async_copy(source, target, self.local.at[self.locals])
        made.start()
        self.locals += 1
        return made

    def drain(self):
        for made in self.remotes:
            made.wait_send()


def softmax(scores, allowed):
    scores = jnp.where(allowed, scores * SCALING, -1000000000.0)
    exponent = jnp.exp(scores - jnp.max(scores, axis=-1, keepdims=True))
    return exponent / jnp.sum(exponent, axis=-1, keepdims=True)


def window_allowed(length, window, heads):
    row = lax.rem(lax.broadcasted_iota(jnp.int32, (heads * window, window), 0), window)
    column = lax.broadcasted_iota(jnp.int32, (heads * window, window), 1)
    return (row // length == column // length) & (row >= column)


def head_masks(width, dtype):
    lane = lax.broadcasted_iota(jnp.int32, (1, width), 1) // HEAD_SIZE
    return [(lane == j).astype(dtype) for j in range(width // HEAD_SIZE)]


def spread(values, masks):
    return jnp.concatenate([values * mask for mask in masks], axis=0)


def gathered(values, masks):
    n = values.shape[0] // len(masks)
    total = 0
    for j, mask in enumerate(masks):
        total = total + values[j * n : (j + 1) * n] * mask
    return total


FORWARD_VEC = ("ln1g", "ln1b", "sob", "ln2g", "ln2b", "cob", "ln3g", "ln3b")
BACKWARD_VEC = ("ln1g", "ln1b", "ln2g", "ln2b", "ln3g", "mob")


def as_rows(names, refs):
    return {name: ref[...].reshape(1, -1) for name, ref in zip(names, refs)}


def forward_kernel(dims, *refs):
    captions, length, images, width, part = dims
    rows = captions * length
    (counts, *vec), refs = refs[:9], refs[9:]
    (tokens, image, raw_in, raw_out, *weights), refs = refs[:9], refs[9:]
    (q1, kv1, o1, x1, q2, kv2, o2, x2, img, w_back, kv_turned), refs = refs[:11], refs[11:]
    (own_h3, other_h3, other_in, other_out), refs = refs[:4], refs[4:]
    (
        (v_q1, v_kv1, v_o1, v_x1, v_q2, v_kv2, v_o2, v_x2, v_img),
        v_w,
        v_turned,
        v_tokens,
        v_h,
        v_h3,
        send,
        recv,
        local,
    ) = refs
    d, t = lax.axis_index("dp"), lax.axis_index("tensor")
    near = {"p0": (flipped(d, 1), t), "p1": (flipped(d, 2), t), **peers()}
    order = [t, flipped(t, 1), flipped(t, 2), 3 - t]
    copies = Copies(send, recv, local)
    token_load = copies.move(tokens.at[pl.ds(t * rows, rows)], v_tokens)
    loads = [copies.move(weights[k], v_w[k].at[t]) for k in range(5)]
    image_load = copies.move(image.at[pl.ds(t * captions, captions)], v_img.at[:, t])
    g = as_rows(FORWARD_VEC, vec)
    greet(list(near.values()))
    quarter = lax.rem(d, 4)
    quarters = (quarter, flipped(quarter, 1), flipped(quarter, 2), 3 - quarter)
    other = order[2]

    def part_of(k, which, half=None):
        size = weights[k].shape[0] // 4
        start = quarters[which] * size
        if half is not None:
            first = (size // 2 + 15) // 16 * 16
            start, size = (start, first) if half == 0 else (start + first, size - first)
        return pl.ds(pl.multiple_of(start, 16), size)

    def region(k, which, half=None):
        return v_w[k].at[other, part_of(k, which, half)]

    count = len(weights)
    over_y, over, own_core = {}, {}, {}

    def send_y(k):
        over_y[k] = copies.to(
            weights[k].at[part_of(k, 0)], v_w[k].at[t, part_of(k, 0)], near["y"]
        )

    for k in range(count):
        own_core[k] = copies.to(weights[k], v_w[k].at[t], near["core"])
        send_y(k)
    images_in = [
        [
            copies.to(image.at[target * captions + caption], v_img.at[caption, t], near[name])
            for name, target in (("y", order[2]), ("far", order[3]), ("core", order[1]))
        ]
        for caption in range(captions)
    ]
    mlp_in = [
        copies.to(a, b, near["core"]) for a, b in ((raw_in, other_in), (raw_out, other_out))
    ]
    core = {k: [] for k in range(count)}

    def first(k):
        over_y[k].wait_recv()
        over[k, 0] = copies.to(region(k, 0), region(k, 0), near["p0"])
        over[k, 1] = copies.to(region(k, 0), region(k, 0), near["p1"])
        core[k].append(copies.to(region(k, 0), region(k, 0), near["core"]))

    def second(k):
        over[k, 0].wait_recv()
        over[k, 2] = copies.to(region(k, 1, 0), region(k, 1, 0), near["p1"])
        core[k].append(copies.to(region(k, 1), region(k, 1), near["core"]))
        over[k, 1].wait_recv()
        over[k, 3] = copies.to(region(k, 2, 1), region(k, 2, 1), near["p0"])
        core[k].append(copies.to(region(k, 2), region(k, 2), near["core"]))

    def third(k):
        over[k, 2].wait_recv()
        core[k].append(copies.to(region(k, 3, 0), region(k, 3, 0), near["core"]))
        over[k, 3].wait_recv()
        core[k].append(copies.to(region(k, 3, 1), region(k, 3, 1), near["core"]))

    def arrived(k):
        for made in core[k]:
            made.wait_recv()

    slab = 64

    def normed(source, gain, shift):
        def body(i, carry):
            place = pl.ds(pl.multiple_of(i * slab, slab), slab)
            n, _ = norm_parts(source[place, :].astype(HIGH))
            v_h[place, :] = (n * gain + shift).astype(LOW)
            return carry

        lax.fori_loop(0, rows // slab, body, 0)

    token_load.wait()
    normed(v_tokens, g["ln1g"], g["ln1b"])

    def start_sum(target, source, shift):
        def body(i, carry):
            place = pl.ds(pl.multiple_of(i * slab, slab), slab)
            target[place, :] = source[place, :].astype(HIGH) + shift
            return carry

        lax.fori_loop(0, rows // slab, body, 0)

    start_sum(v_x1, v_tokens, g["sob"])
    window = 2 * length
    heads = part // HEAD_SIZE
    causal = window_allowed(length, window, heads)
    masks, wide_masks = head_masks(part, LOW), head_masks(part, HIGH)

    def self_part(s):
        h = v_h[...]
        v_q1[s] = dot_rows(h, v_w[0][s, :part, :]).astype(LOW)
        v_kv1[s] = dot_rows(v_w[0][s, part:, :], h).astype(LOW)
        for w in range(rows // window):
            span = pl.ds(w * window, window)
            q = spread(v_q1[s, span, :], masks)
            p = softmax(dot(q, v_kv1[s, :part, span]), causal)
            mixed = dot_rows(p.astype(LOW), v_kv1[s, part:, span])
            v_o1[s, span, :] = gathered(mixed, wide_masks).astype(LOW)
        v_x1[...] += dot(v_o1[s], v_w[1][s])

    def queries(s):
        v_q2[s] = dot_rows(v_h[...], v_w[2][s]).astype(LOW)

    def turn(s):
        v_turned[:, pl.ds(pl.multiple_of(s * 2 * part, 128), 2 * part)] = v_w[3][s].T

    def cross_part(c):
        allowed = lax.broadcasted_iota(jnp.int32, (1, images), 1) < counts[t * captions + c]
        span, own = pl.ds(c * images, images), pl.ds(c * length, length)

        def body(s, carry):
            kv = dot(v_w[3][s], v_img[c].reshape(width, images)).astype(LOW)
            v_kv2[s, :, span] = kv
            q = spread(v_q2[s, own, :], masks)
            p = softmax(dot(q, kv[:part]), allowed)
            mixed = dot_rows(p.astype(LOW), kv[part:])
            v_o2[s, own, :] = gathered(mixed, wide_masks).astype(LOW)
            return carry

        lax.fori_loop(0, 4, body, 0)
        total = v_x2[own, :]
        for s in range(4):
            total = total + dot(v_o2[s, own, :], v_w[4][s])
        v_x2[own, :] = total
        n, _ = norm_parts(total)
        v_h3[own, :] = (n * g["ln3g"] + g["ln3b"]).astype(LOW)
        h3_in.append(copies.to(v_h3.at[own], other_h3.at[own], near["y"]))

    h3_in = []
    back = []
    loads[0].wait()
    loads[1].wait()
    self_part(order[0])
    own_core[0].wait_recv()
    own_core[1].wait_recv()
    first(0)
    self_part(order[1])
    first(1)
    first(2)
    second(0)
    first(3)
    second(1)
    first(4)
    third(0)
    second(2)
    third(1)
    second(3)
    arrived(0)
    arrived(1)
    self_part(order[2])
    third(2)
    second(4)
    self_part(order[3])
    third(3)
    third(4)
    back.append(copies.move(v_q1, q1))
    back.append(copies.move(v_kv1, kv1))
    back.append(copies.move(v_o1, o1))
    back.append(copies.move(v_x1, x1))
    normed(v_x1, g["ln2g"], g["ln2b"])
    for k in range(2, 5):
        loads[k].wait()
        own_core[k].wait_recv()
        arrived(k)
    for s in order:
        queries(s)
        turn(s)
    back.append(copies.move(v_turned, kv_turned))
    for i, k in enumerate((0, 1, 2, 4)):
        back.append(copies.move(v_w[k], w_back[i]))
    back.append(copies.move(v_q2, q2))
    start_sum(v_x2, v_x1, g["cob"])
    image_load.wait()
    for caption in range(captions):
        for made in images_in[caption]:
            made.wait_recv()
        cross_part(caption)
    back.append(copies.move(v_img, img))
    back.append(copies.move(v_kv2, kv2))
    back.append(copies.move(v_o2, o2))
    back.append(copies.move(v_x2, x2))
    back.append(copies.move(v_h3, own_h3))
    for made in mlp_in + h3_in:
        made.wait_recv()
    copies.drain()
    for made in back:
        made.wait()


def forward(dims, counts, vec, tokens, image, raw, weights):
    captions, length, images, width, part = dims
    rows = captions * length
    shape = jax.ShapeDtypeStruct
    kept = [
        ((4, rows, part), LOW),
        ((4, 2 * part, rows), LOW),
        ((4, rows, part), LOW),
        ((rows, width), HIGH),
        ((4, rows, part), LOW),
        ((4, 2 * part, captions * images), LOW),
        ((4, rows, part), LOW),
        ((rows, width), HIGH),
        ((captions, 4, part, images), LOW),
    ]
    sizes = [(4, *w.shape) for w in weights]
    any_spec = pl.BlockSpec(memory_space=pl.ANY)
    vmem, smem = pl.BlockSpec(memory_space=pltpu.VMEM), pl.BlockSpec(memory_space=pltpu.SMEM)
    remote = 5 * 11 + 4 * captions + 2
    return pl.pallas_call(
        partial(forward_kernel, dims),
        out_shape=[shape(*k) for k in kept]
        + [
            [shape(sizes[k], LOW) for k in (0, 1, 2, 4)],
            shape((width, 8 * part), LOW),
            shape((rows, width), LOW),
            shape((rows, width), LOW),
            shape(raw[0].shape, LOW),
            shape(raw[1].shape, LOW),
        ],
        in_specs=[smem] + [vmem] * 8 + [any_spec] * 9,
        out_specs=[any_spec] * 9 + [[any_spec] * 4] + [any_spec] * 5,
        scratch_shapes=[
            [pltpu.VMEM(*k) for k in kept],
            [pltpu.VMEM(sizes[k], LOW) for k in range(5)],
            pltpu.VMEM((width, 8 * part), LOW),
            pltpu.VMEM((rows, width), LOW),
            pltpu.VMEM((rows, width), LOW),
            pltpu.VMEM((rows, width), LOW),
            pltpu.SemaphoreType.DMA((remote,)),
            pltpu.SemaphoreType.DMA((remote,)),
            pltpu.SemaphoreType.DMA((32,)),
        ],
        name="forward",
        compiler_params=pltpu.CompilerParams(
            collective_id=0, has_side_effects=True, vmem_limit_bytes=62 << 20
        ),
    )(counts, *vec, tokens, image, *raw, *weights)


def backward_kernel(dims, stride, *refs):
    captions, length, images, width, part = dims
    rows = captions * length
    block, wide = width // 8, width // 2
    heads = part // HEAD_SIZE
    window = 2 * length
    (
        counts,
        vec,
        (bias, tokens, grads, raw_in, raw_out, own_h3, other_h3, other_in, other_out),
        (q1, kv1, o1, x1, q2, kv2, o2, x2, img),
        w_back,
        kv_turned,
        sums,
        image_out,
        out_all,
        token_all,
        small_out,
        (v_q1, v_kv1, v_o1, v_x1, v_q2, v_kv2, v_o2, v_x2, v_img),
        (v_w0, v_w1, v_w2, v_w4),
        v_turned,
        (v_in, v_out, g_out, g_in, g_cross, g_self),
        v_bias,
        v_tokens,
        v_grads,
        v_h3,
        v_h,
        v_turn_a,
        v_turn_b,
        v_f0,
        v_f1,
        v_y,
        v_g,
        v_low,
        v_parts,
        v_narrow,
        from_core,
        halves,
        from_y,
        result,
        v_sum,
        sum_in,
        credit,
        send,
        recv,
        local,
    ) = refs
    d, t = lax.axis_index("dp"), lax.axis_index("tensor")
    y, c = t // 2, lax.rem(t, 2)
    near = peers()
    bits = [lax.rem(d // (stride << b), 2) for b in range(3)]
    partner = [(flipped(d, stride << b), t) for b in range(3)]
    order = [3 - t, flipped(t, 2), flipped(t, 1), t]
    copies = Copies(send, recv, local)

    mine = pl.ds(t * rows, rows)
    load_x2 = copies.move(x2, v_x2)
    load_grads = [
        copies.move(grads.at[mine], v_grads.at[0]),
        copies.move(grads.at[pl.ds(flipped(t, 2) * rows, rows)], v_grads.at[1]),
    ]
    load_mlp = [
        [copies.move(a, v_h3.at[i]) for i, a in ((0, own_h3), (1, other_h3))],
        [copies.move(raw_in, v_in.at[c]), copies.move(raw_out, v_out.at[c])],
        [copies.move(other_in, v_in.at[1 - c]), copies.move(other_out, v_out.at[1 - c])],
    ]
    load_rest = [
        copies.move(a, b)
        for a, b in (
            (w_back[3], v_w4),
            (q2, v_q2),
            (kv2, v_kv2),
            (o2, v_o2),
            (x1, v_x1),
            (img, v_img),
            (w_back[2], v_w2),
            (kv_turned, v_turned),
            (w_back[1], v_w1),
            (w_back[0], v_w0),
            (q1, v_q1),
            (kv1, v_kv1),
            (o1, v_o1),
            (tokens.at[mine], v_tokens),
        )
    ]
    greet([*near.values(), *partner])
    bias_in = copies.to(bias, v_bias, near["core"])

    g = as_rows(BACKWARD_VEC, vec)
    slab = 64

    def loop(body, init, step=slab):
        def run(i, carry):
            return body(pl.ds(pl.multiple_of(i * step, step), step), carry)

        return lax.fori_loop(0, rows // step, run, init)

    zeros = jnp.zeros((8, width), HIGH)

    def keep(name, total):
        v_sum[0, name : name + 1, :] = jnp.sum(total, axis=0, keepdims=True)

    pieces = [g_out, g_in, g_cross, g_self]
    plan = {
        (0, 0): (0, 1, 2),
        (0, 1): (1, 0, 2),
        (1, 0): (0, 1, 2),
        (1, 1): (1, 0, 2),
        (2, 0): ("y", 0, 1, 2),
        (2, 1): (0, 1, 2, "y"),
        (3, 0): (0, 1, 2, "y"),
        (3, 1): (1, 0, 2, "y"),
    }
    units = [(p, o, h) for p in range(4) for o in ((1,) if p < 2 else (0, 1)) for h in (0, 1)]
    y_places = {(2, 0): from_y[0], (2, 1): from_y[1], (3, 0): from_y[2], (3, 1): from_y[3]}
    to_core, hops, places = {}, {}, {}
    side = (1 - y, y)

    def lanes(h):
        return pl.ds(h * wide, wide)

    def slot(p, o):
        return p if p < 2 else 2 + o if p == 2 else o

    def own(p, o, core):
        return (core,) if p < 2 else (side[o], core)

    def offer(p, o):
        if p == 3:
            pl.semaphore_wait(credit.at[o], 1)
        to_core[p, o] = copies.to(
            pieces[p].at[own(p, o, 1 - c)], from_core.at[slot(p, o)], near["core"]
        )

    def add(target, left, *others):
        lead = left.shape[:-2]
        total = 1
        for size in lead:
            total *= size
        low = len(others) == 1 and target.dtype == LOW

        def body(i, carry):
            index, rest = [], i
            for size in reversed(lead):
                index.insert(0, lax.rem(rest, size))
                rest = rest // size
            place = (*index, slice(None), slice(None))
            value = left[place] if low else left[place].astype(HIGH)
            for ref in others:
                value = value + (ref[place] if low else ref[place].astype(HIGH))
            target[place] = value.astype(target.dtype)
            return carry

        if total == 1:
            body(0, 0)
        else:
            lax.fori_loop(0, total, body, 0)

    def cut(bit, left, value):
        return tuple(value if b == bit else slice(None) for b in sorted(left, reverse=True))

    back = []

    def advance(p, o, h, stage):
        u = units.index((p, o, h))
        turn = plan[p, h]
        y_first, with_y = turn[0] == "y", "y" in turn
        xyz = [b for b in turn if b != "y"]
        if stage == 0:
            base = pieces[p].at[(*own(p, o, c), *[slice(None)] * 4, lanes(h))]
            sent = from_core.at[(slot(p, o), *[slice(None)] * 4, lanes(h))]
            if (p, o, "core") not in places:
                to_core[p, o].wait_recv()
                places[p, o, "core"] = True
            if y_first and o == 1:
                hops[p, 0, h, "y"].wait_recv()
                add(base, base, sent, y_places[p, h])
            else:
                add(base, base, sent)
            places[u] = base, [0, 1, 2]
            if y_first and o == 0:
                hops[p, 0, h, "y"] = copies.to(base, y_places[p, h], near["y"])
                return
        if stage > 0:
            source, left = places[u]
            bit = xyz[stage - 1]
            hops[p, o, h, stage].wait_recv()
            target = halves[stage - 1].at[u]
            kept = source.at[cut(bit, left, bits[bit])]
            remaining = [b for b in left if b != bit]
            last = stage == 3
            if last and o == 1:
                total = result.at[p, :, lanes(h)]
                if y_first or not with_y:
                    add(total, target, kept)
                else:
                    hops[p, 0, h, "y"].wait_recv()
                    add(total, target, kept, y_places[p, h])
                back.append(copies.move(total, sums[p].at[:, lanes(h)]))
                return
            add(target, target, kept)
            places[u] = target, remaining
            if last:
                hops[p, 0, h, "y"] = copies.to(target, y_places[p, h], near["y"])
                return
        source, left = places[u]
        bit = xyz[stage]
        hops[p, o, h, stage + 1] = copies.to(
            source.at[cut(bit, left, 1 - bits[bit])], halves[stage].at[u], partner[bit]
        )

    def free(o):
        pl.semaphore_signal(credit.at[o], inc=1, device_id=near["core"], device_id_type=MESH)

    def forth(p, o, stage):
        advance(p, o, 0, stage)
        advance(p, o, 1, stage)

    own_rows, other_rows = slice(0, rows), slice(rows, 2 * rows)

    def weight(ref, e):
        return ref[e].reshape(width, width)

    def put(ref, index, first, values):
        half, values = values
        ref[(*index, half, slice(None), slice(None), slice(None), slice(first, first + values.shape[1]))] = (
            values.astype(LOW).reshape(2, 2, block, values.shape[1])
        )

    def half_rows(half):
        return pl.ds(half * (width // 2), width // 2)

    bias_sums = [zeros, zeros]
    hidden = g_self.reshape(4 * width, width)

    def hidden_rows(kind, i, r, size=rows):
        return hidden.at[pl.ds(((kind * 2 + i) * 2 + r) * rows, size)]

    def feed(i, r):
        e = 1 - c if i else c
        v_f0[...] = dot(v_h3[r], weight(v_in, e))
        v_f1[...] = dot_rows(v_grads[r], weight(v_out, e))
        shift = (v_bias if i else bias)[...].reshape(1, -1)

        v_u, v_ga = hidden_rows(0, i, r), hidden_rows(1, i, r)

        def act(place, carry):
            a = v_f0[place, :] + shift
            cumulative = 0.5 * (1.0 + lax.erf(a * (0.5**0.5)))
            density = jnp.exp(-0.5 * a * a) * 0.3989422804014327
            v_u[place, :] = (a * cumulative).astype(LOW)
            ga = (v_f1[place, :] * (cumulative + a * density)).astype(LOW)
            v_ga[place, :] = ga
            return carry + folded(ga.astype(HIGH))

        bias_sums[i] += loop(act, zeros, 16)
        if i == 0:
            v_y[r] = dot(v_u[...], weight(v_out, e))
            v_g[r] = dot_rows(v_ga[...], weight(v_in, e))
        else:
            v_y[r] += dot(v_u[...], weight(v_out, e))
            v_g[r] += dot_rows(v_ga[...], weight(v_in, e))

    for load in load_grads + load_mlp[0] + load_mlp[1]:
        load.wait()
    feed(0, 1)
    for load in load_mlp[2]:
        load.wait()
    bias_in.wait_recv()
    feed(1, 1)

    def rounded(place, carry):
        v_low[0, place, :] = v_g[1, place, :].astype(LOW)
        v_low[1, place, :] = v_y[1, place, :].astype(LOW)
        return carry

    loop(rounded, 0)
    parts_in = [copies.to(v_low.at[i], v_parts.at[i], near["y"]) for i in range(2)]
    feed(0, 0)
    feed(1, 0)

    def start(place, carry):
        return carry + folded(v_grads[0, place, :].astype(HIGH))

    keep(8, loop(start, zeros))
    v_turn_a[:, own_rows] = v_h3[0].T
    v_turn_a[:, other_rows] = v_h3[1].T
    v_turn_b[:, own_rows] = v_grads[0].T
    v_turn_b[:, other_rows] = v_grads[1].T
    for i in (1, 0):
        e = 1 - c if i else c
        u, ga = (hidden_rows(kind, i, 0, size=2 * rows)[...] for kind in (0, 1))
        for half in range(2):
            put(g_out, (e,), 0, (half, dot(v_turn_b[half_rows(half), :], u)))
            put(g_in, (e,), 0, (half, dot(v_turn_a[half_rows(half), :], ga)))
        if i == 1:
            offer(0, 1)
            offer(1, 1)
    for s in range(4):
        total = jnp.sum(jnp.where(c == s % 2, bias_sums[0], bias_sums[1]), axis=0, keepdims=True)
        v_sum[0, 9 + s : 10 + s, :] = jnp.where(y == s // 2, total, 0.0)
    v_sum[0, 13:16, :] = jnp.zeros((3, width), HIGH)
    for p in (0, 1):
        forth(p, 1, 0)
        free(p)

    def shared(source, target):
        place = target.at[pl.ds(t * rows, rows)]
        back.append(copies.move(source, place))
        return [copies.to(source, place, near[name]) for name in ("y", "core")]

    def passed_on(moves, target):
        place = target.at[pl.ds(flipped(t, 2) * rows, rows)]
        moves[0].wait_recv()
        return [moves[1], copies.to(place, place, near["core"])]

    def norm_back(source, gain, old, new, low, more=None):
        def body(place, carry):
            a, b, e = carry
            n, inv_std = norm_parts(source[place, :].astype(HIGH))
            gh = v_g[0, place, :]
            if more is not None:
                gh = gh + more[place, :].astype(HIGH)
            scaled = gh * gain
            grad = inv_std * (
                scaled
                - jnp.mean(scaled, axis=-1, keepdims=True)
                - n * jnp.mean(scaled * n, axis=-1, keepdims=True)
            )
            grad = old[place, :].astype(HIGH) + grad
            if new is not None:
                new[place, :] = grad
                e = e + folded(grad)
            low[place, :] = grad.astype(LOW)
            return a + folded(gh * n), b + folded(gh), e

        return loop(body, (zeros, zeros, zeros))

    def finish(place, carry):
        total = v_x2[place, :] + g["mob"] + v_y[0, place, :] + v_parts[1, place, :].astype(HIGH)
        v_low[2, place, :] = total.astype(LOW)
        return carry

    load_x2.wait()
    parts_in[0].wait_recv()
    own_grads = v_grads.at[0]
    gain_sum, bias_sum, total = norm_back(
        v_x2, g["ln3g"], own_grads, v_f0, own_grads, v_parts.at[0]
    )
    keep(6, gain_sum)
    keep(7, bias_sum)
    keep(5, total)

    for load in load_rest:
        load.wait()

    def again(source, gain, shift):
        def body(place, carry):
            n, _ = norm_parts(source[place, :].astype(HIGH))
            v_h[place, :] = (n * gain + shift).astype(LOW)
            v_g[0, place, :] = jnp.zeros((slab, width), HIGH)
            return carry

        loop(body, 0)

    again(v_x1, g["ln2g"], g["ln2b"])
    v_turn_a[:, own_rows] = v_h[...].T
    v_turn_b[:, own_rows] = v_grads[0].T
    go, gq = v_narrow.at[0], v_narrow.at[1]
    masks, wide_masks = head_masks(part, LOW), head_masks(part, HIGH)

    def attend_back(q, k, v, g_mix, allowed):
        q, g_mix = spread(q, masks), spread(g_mix, masks)
        p = softmax(dot(q, k), allowed)
        low_p = p.astype(LOW)
        gp = dot(g_mix, v)
        inner = jnp.sum(gp * p, axis=-1, keepdims=True)
        gs = (p * (gp - inner)).astype(LOW)
        return (
            (gathered(dot_rows(gs, k), wide_masks) * SCALING).astype(LOW),
            (dot_columns(q, gs) * SCALING).astype(LOW),
            dot_columns(g_mix, low_p).astype(LOW),
        )

    def gradients(piece, s, of_keys, o_kept):
        for half in range(2):
            index = (s // 2, lax.rem(s, 2))
            put(piece, index, 0, (half, of_keys(half)))
            both = [dot(v_turn_a[half_rows(half), own_rows], gq[...])]
            both.append(dot(v_turn_b[half_rows(half), own_rows], o_kept[s]))
            put(piece, index, 2 * part, (half, jnp.concatenate(both, axis=1)))

    def cross_back(s):
        go[...] = dot_rows(v_grads[0], v_w4[s]).astype(LOW)

        def body(caption, carry):
            span = pl.ds(pl.multiple_of(caption * images, images), images)
            own = pl.ds(pl.multiple_of(caption * length, length), length)
            allowed = (
                lax.broadcasted_iota(jnp.int32, (1, images), 1) < counts[t * captions + caption]
            )
            g_q, g_k, g_v = attend_back(
                v_q2[s, own, :], v_kv2[s, :part, span], v_kv2[s, part:, span], go[own, :], allowed
            )
            v_kv2[s, :part, span] = g_k
            v_kv2[s, part:, span] = g_v
            gq[own, :] = g_q
            return carry

        lax.fori_loop(0, captions, body, 0)
        v_g[0] += dot(gq[...], v_w2[s])

        def of_keys(half):
            total = 0
            for caption in range(captions):
                span = slice(caption * images, (caption + 1) * images)
                features = v_img[caption, 2 * half : 2 * half + 2].reshape(width // 2, images)
                total = total + dot_rows(features, v_kv2[s, :, span])
            return total

        gradients(g_cross, s, of_keys, v_o2)

    for i, s in enumerate(order):
        cross_back(s)
        if i == 0:
            parts_in[1].wait_recv()
            loop(finish, 0)
            out_moves = shared(v_low.at[2], out_all)
            offer(2, 0)
            forth(0, 1, 1)
        if i == 1:
            forth(1, 1, 1)
            forth(2, 0, 0)
        if i == 2:
            offer(2, 1)
            forth(0, 1, 2)
            out_moves = passed_on(out_moves, out_all)
        if i == 3:
            forth(1, 1, 2)
            advance(2, 0, 1, 1)
            advance(2, 1, 1, 0)
    image_span = pl.ds(t * captions, captions)

    def image_part(caption, carry):
        span = pl.ds(pl.multiple_of(caption * images, images), images)
        values = dot(v_turned[...], v_kv2[:, :, span].reshape(8 * part, images))
        v_img[caption] = values.astype(LOW).reshape(4, part, images)
        return carry

    lax.fori_loop(0, captions, image_part, 0)
    forth(0, 1, 3)
    image_moves = [
        copies.to(v_img.at[:, target], image_out.at[image_span], near[name])
        for name, target in (("y", flipped(t, 2)), ("far", 3 - t), ("core", flipped(t, 1)))
    ]
    back.append(copies.move(v_img.at[:, t], image_out.at[image_span]))
    gain_sum, bias_sum, total = norm_back(v_x1, g["ln2g"], v_f0, v_f1, own_grads)
    keep(3, gain_sum)
    keep(4, bias_sum)
    keep(2, total)
    forth(1, 1, 3)
    advance(2, 1, 0, 0)
    advance(2, 0, 1, 2)

    again(v_tokens, g["ln1g"], g["ln1b"])
    v_turn_a[:, own_rows] = v_h[...].T
    v_turn_b[:, own_rows] = v_grads[0].T
    causal = window_allowed(length, window, heads)

    def self_back(s):
        go[...] = dot_rows(v_grads[0], v_w1[s]).astype(LOW)
        for w in range(rows // window):
            span = pl.ds(w * window, window)
            g_q, g_k, g_v = attend_back(
                v_q1[s, span, :], v_kv1[s, :part, span], v_kv1[s, part:, span], go[span, :], causal
            )
            v_kv1[s, :part, span] = g_k
            v_kv1[s, part:, span] = g_v
            gq[span, :] = g_q
        v_g[0] += dot(gq[...], v_w0[s, :part, :]) + dot_columns(v_kv1[s], v_w0[s, part:, :])

        def of_keys(half):
            return dot_rows(v_turn_a[half_rows(half), own_rows], v_kv1[s])

        gradients(g_self, s, of_keys, v_o1)

    for i, s in enumerate(order):
        self_back(s)
        if i == 0:
            offer(3, 0)
            advance(2, 1, 1, 1)
            advance(2, 1, 0, 1)
            advance(2, 0, 1, 3)
        if i == 1:
            forth(3, 0, 0)
            advance(2, 1, 1, 2)
        if i == 2:
            offer(3, 1)
            advance(2, 1, 0, 2)
    forth(3, 1, 0)
    gain_sum, bias_sum, _ = norm_back(v_tokens, g["ln1g"], v_f1, None, v_h)
    keep(0, gain_sum)
    keep(1, bias_sum)
    small_to = [near["core"], *partner, near["y"]]
    small = []

    def total_start():
        i = len(small)
        small.append(copies.to(v_sum.at[i], sum_in.at[i], small_to[i]))

    def total_end():
        i = len(small) - 1
        small[i].wait_recv()
        v_sum[i + 1] = v_sum[i] + sum_in[i]

    total_start()
    token_moves = shared(v_h, token_all)
    forth(3, 0, 1)
    forth(2, 1, 3)
    total_end()
    total_start()
    forth(3, 1, 1)
    total_end()
    total_start()
    forth(3, 0, 2)
    total_end()
    total_start()
    forth(3, 1, 2)
    forth(3, 0, 3)
    total_end()
    total_start()
    token_moves = passed_on(token_moves, token_all)
    forth(3, 1, 3)
    total_end()
    back.append(copies.move(v_sum.at[5], small_out))
    for made in out_moves + image_moves + token_moves:
        made.wait_recv()
    copies.drain()
    for made in back:
        made.wait()


def backward(dims, stride, counts, vec, bias, tokens, grads, raw, mlp, kept, w_back, turned):
    captions, length, images, width, part = dims
    rows = captions * length
    block, wide = width // 8, width // 2
    shape = jax.ShapeDtypeStruct
    any_spec = pl.BlockSpec(memory_space=pl.ANY)
    vmem, smem = pl.BlockSpec(memory_space=pltpu.VMEM), pl.BlockSpec(memory_space=pltpu.SMEM)
    shard = (2, 2, 2, block, width)
    raw = [w.reshape(shard) for w in raw]
    own_h3, other_h3, *others = mlp
    mlp = [own_h3, other_h3, *(w.reshape(shard) for w in others)]
    remote = 128

    def scratch(*size, dtype=LOW):
        return pltpu.VMEM(size, dtype)

    flat = [scratch(*k.shape, dtype=k.dtype) for k in kept]
    return pl.pallas_call(
        lambda *refs: backward_kernel(
            dims,
            stride,
            refs[0],
            refs[1:7],
            refs[7:16],
            refs[16:25],
            refs[25:29],
            refs[29],
            refs[30:34],
            *refs[34:],
        ),
        out_shape=[shape((block, width), HIGH)] * 4
        + [
            shape((4 * captions, part, images), LOW),
            shape((4 * rows, width), LOW),
            shape((4 * rows, width), LOW),
            shape((16, width), HIGH),
        ],
        in_specs=[smem] + [vmem] * 7 + [any_spec] * 22,
        out_specs=[any_spec] * 8,
        scratch_shapes=[
            flat,
            [scratch(*w.shape) for w in w_back],
            scratch(*turned.shape),
            [scratch(2, *shard)] * 4 + [scratch(2, 2, *shard)] * 2,
            scratch(*bias.shape, dtype=HIGH),
            scratch(rows, width),
            scratch(2, rows, width),
            scratch(2, rows, width),
            scratch(rows, width),
            scratch(width, 2 * rows),
            scratch(width, 2 * rows),
            scratch(rows, width, dtype=HIGH),
            scratch(rows, width, dtype=HIGH),
            scratch(2, rows, width, dtype=HIGH),
            scratch(2, rows, width, dtype=HIGH),
            scratch(3, rows, width),
            scratch(2, rows, width),
            scratch(2, rows, part),
            scratch(4, *shard),
            [
                scratch(12, 2, 2, block, wide),
                scratch(12, 2, block, wide),
                scratch(12, block, wide),
            ],
            [scratch(2, 2, 2, block, wide)] + [scratch(block, wide)] * 3,
            scratch(4, block, width, dtype=HIGH),
            scratch(6, 16, width, dtype=HIGH),
            scratch(5, 16, width, dtype=HIGH),
            pltpu.SemaphoreType.REGULAR((2,)),
            pltpu.SemaphoreType.DMA((remote,)),
            pltpu.SemaphoreType.DMA((remote,)),
            pltpu.SemaphoreType.DMA((48,)),
        ],
        name="backward",
        compiler_params=pltpu.CompilerParams(
            collective_id=1, has_side_effects=True, vmem_limit_bytes=67043328
        ),
    )(counts, *vec, bias, tokens, grads, *raw, *mlp, *kept, *w_back, turned)


def finish_kernel(dims, *refs):
    captions, length, images, width, part = dims
    ins, refs = refs[:8], refs[8:]
    outs, vectors, refs = (*refs[:9], refs[19]), refs[9:19], refs[20:]
    buffers, made_qkv, made_self, made_q, made_cross, made_kv, arrive, leave = refs
    loads = [
        pltpu.make_async_copy(a, b, arrive.at[i]) for i, (a, b) in enumerate(zip(ins, buffers))
    ]
    for load in loads[::-1]:
        load.start()
    v_self, v_cross, v_small = buffers[:3]
    leaving = []

    def put(source, target):
        made = pltpu.make_async_copy(source, target, leave.at[len(leaving)])
        made.start()
        leaving.append(made)

    def columns(ref, i):
        return ref[:, i * part : (i + 1) * part]

    for i in range(7, 2, -1):
        loads[i].wait()
        put(buffers[i], outs[i + 1])
    loads[0].wait()
    for i, j in enumerate((2, 0, 1)):
        made_qkv[i] = columns(v_self, j)
    put(made_qkv, outs[0])
    made_self[...] = columns(v_self, 3).T
    put(made_self, outs[1])
    loads[1].wait()
    made_q[...] = columns(v_cross, 2)
    put(made_q, outs[2])
    made_cross[...] = columns(v_cross, 3).T
    put(made_cross, outs[3])
    for i in range(2):
        made_kv[:, i, :] = columns(v_cross, i)
    put(made_kv, outs[9])
    loads[2].wait()
    for i, ref in enumerate(vectors[:9]):
        ref[...] = v_small[i : i + 1, :].reshape(width)
    own = v_small[pl.ds(9 + lax.axis_index("tensor"), 1), :]
    vectors[9][...] = own.reshape(width)
    for made in leaving:
        made.wait()


def finish(dims, ins):
    captions, length, images, width, part = dims
    block = ins[0].shape[0]
    any_spec, vmem = pl.BlockSpec(memory_space=pl.ANY), pl.BlockSpec(memory_space=pltpu.VMEM)
    made = [(3, block, part), (part, block), (block, part), (part, block)]
    return pl.pallas_call(
        partial(finish_kernel, dims),
        out_shape=[jax.ShapeDtypeStruct(size, HIGH) for size in made]
        + [jax.ShapeDtypeStruct(x.shape, x.dtype) for x in ins[3:]]
        + [jax.ShapeDtypeStruct((width,), HIGH)] * 10
        + [jax.ShapeDtypeStruct((block, 2, part), HIGH)],
        in_specs=[any_spec] * 8,
        out_specs=[any_spec] * 9 + [vmem] * 10 + [any_spec],
        scratch_shapes=[
            [pltpu.VMEM(x.shape, x.dtype) for x in ins],
            *(pltpu.VMEM(size, HIGH) for size in made),
            pltpu.VMEM((block, 2, part), HIGH),
            pltpu.SemaphoreType.DMA((8,)),
            pltpu.SemaphoreType.DMA((10,)),
        ],
        name="finish",
    )(*ins)


def local(
    tokens,
    image_tokens,
    image_counts,
    ln1_gain,
    ln1_bias,
    self_qkv,
    self_output_weight,
    self_output_bias,
    ln2_gain,
    ln2_bias,
    cross_query_weight,
    cross_kv,
    cross_output_weight,
    cross_output_bias,
    ln3_gain,
    ln3_bias,
    mlp_in,
    mlp_in_bias,
    mlp_out,
    mlp_out_bias,
    grad_out,
):
    stride = lax.axis_size("dp") // 8
    all_captions, length, width = tokens.shape
    images, part = image_tokens.shape[1:]
    captions = all_captions // 4
    dims = (captions, length, images, width, part)
    first = [ln1_gain, ln1_bias, self_output_bias, ln2_gain, ln2_bias, cross_output_bias]
    first += [ln3_gain, ln3_bias]
    second = [ln1_gain, ln1_bias, ln2_gain, ln2_bias, ln3_gain, mlp_out_bias]
    tokens = tokens.reshape(-1, width)
    grads = grad_out.reshape(-1, width)
    weights = [
        self_qkv.transpose(1, 2, 0).reshape(3 * part, width),
        self_output_weight,
        cross_query_weight.T,
        cross_kv.transpose(1, 2, 0).reshape(2 * part, width),
        cross_output_weight,
    ]
    raw = (mlp_in, mlp_out)
    *kept, w_back, turned, own_h3, other_h3, other_in, other_out = forward(
        dims, image_counts, first, tokens, image_tokens.transpose(0, 2, 1), raw, weights
    )
    sum_out, sum_in, sum_cross, sum_self, grad_image, output, grad_tokens, small = backward(
        dims,
        stride,
        image_counts,
        second,
        mlp_in_bias,
        tokens,
        grads,
        raw,
        (own_h3, other_h3, other_in, other_out),
        kept,
        w_back,
        turned,
    )
    if stride > 1:
        groups = [[hi * stride + lo for lo in range(stride)] for hi in range(8)]
        sum_out, sum_in, sum_cross, sum_self = (
            lax.psum_scatter(s, "dp", scatter_dimension=0, axis_index_groups=groups, tiled=True)
            for s in (sum_out, sum_in, sum_cross, sum_self)
        )
        small = lax.psum(small, "dp", axis_index_groups=groups)
    qkv, self_out, cross_q, cross_out, sum_in, sum_out, *rest = finish(
        dims, [sum_self, sum_cross, small, sum_in, sum_out, output, grad_tokens, grad_image]
    )
    output, grad_tokens, grad_image, *vectors, cross_kv = rest
    return (
        output.reshape(all_captions, length, width),
        grad_tokens.reshape(all_captions, length, width),
        grad_image.transpose(0, 2, 1),
        vectors[0],
        vectors[1],
        qkv.transpose(1, 0, 2),
        self_out,
        vectors[2],
        vectors[3],
        vectors[4],
        cross_q,
        cross_kv,
        cross_out,
        vectors[5],
        vectors[6],
        vectors[7],
        sum_in,
        vectors[9],
        sum_out.T,
        vectors[8],
    )


def solution(mesh):
    return jax.shard_map(
        local,
        mesh=mesh,
        in_specs=(
            P("dp", None, None),
            P("dp", None, "tensor"),
            P("dp"),
            P(),
            P(),
            P(None, None, "tensor"),
            P("tensor", None),
            P(),
            P(),
            P(),
            P(None, "tensor"),
            P(None, None, "tensor"),
            P("tensor", None),
            P(),
            P(),
            P(),
            P(None, "tensor"),
            P("tensor"),
            P("tensor", None),
            P(),
            P("dp", None, None),
        ),
        out_specs=(
            P("dp", None, None),
            P("dp", None, None),
            P("dp", None, "tensor"),
            P(),
            P(),
            P("dp", None, "tensor"),
            P("tensor", "dp"),
            P(),
            P(),
            P(),
            P("dp", "tensor"),
            P("dp", None, "tensor"),
            P("tensor", "dp"),
            P(),
            P(),
            P(),
            P("dp", "tensor"),
            P("tensor"),
            P("tensor", "dp"),
            P(),
        ),
        check_vma=False,
    )
```

```python
from functools import partial

import jax
import jax.numpy as jnp
from jax import lax
from jax.experimental import pallas as pl
from jax.experimental.pallas import tpu as pltpu
from jax.sharding import PartitionSpec as P

HEAD_SIZE = 64
LOW = jnp.bfloat16
HIGH = jnp.float32
MESH = pl.DeviceIdType.MESH
SCALING = HEAD_SIZE**-0.5


def dot(left, right):
    return jnp.dot(left, right, preferred_element_type=HIGH)


def dot_rows(left, right):
    return lax.dot_general(left, right, (((1,), (1,)), ((), ())), preferred_element_type=HIGH)


def dot_columns(left, right):
    return lax.dot_general(left, right, (((0,), (0,)), ((), ())), preferred_element_type=HIGH)


def norm_parts(values):
    center = values - jnp.mean(values, axis=-1, keepdims=True)
    inv_std = lax.rsqrt(jnp.mean(center * center, axis=-1, keepdims=True) + 1e-05)
    return center * inv_std, inv_std


def folded(values):
    return jnp.sum(values.reshape(values.shape[0] // 8, 8, values.shape[1]), axis=0)


def flipped(value, step):
    return value + step * (1 - 2 * lax.rem(value // step, 2))


def peers():
    d, t = lax.axis_index("dp"), lax.axis_index("tensor")
    return {"core": (d, flipped(t, 1)), "y": (d, flipped(t, 2)), "far": (d, 3 - t)}


def greet(devices):
    barrier = pltpu.get_barrier_semaphore()
    for device in devices:
        pl.semaphore_signal(barrier, inc=1, device_id=device, device_id_type=MESH)
    pl.semaphore_wait(barrier, len(devices))


class Copies:
    def __init__(self, send, recv, local):
        self.send, self.recv, self.local = send, recv, local
        self.remotes, self.locals = [], 0

    def to(self, source, target, device):
        slot = len(self.remotes)
        assert slot < self.send.shape[0]
        made = pltpu.make_async_remote_copy(
            src_ref=source,
            dst_ref=target,
            send_sem=self.send.at[slot],
            recv_sem=self.recv.at[slot],
            device_id=device,
            device_id_type=MESH,
        )
        made.start()
        self.remotes.append(made)
        return made

    def move(self, source, target):
        assert self.locals < self.local.shape[0]
        made = pltpu.make_async_copy(source, target, self.local.at[self.locals])
        made.start()
        self.locals += 1
        return made

    def drain(self):
        for made in self.remotes:
            made.wait_send()


def softmax(scores, allowed):
    scores = jnp.where(allowed, scores * SCALING, -1000000000.0)
    exponent = jnp.exp(scores - jnp.max(scores, axis=-1, keepdims=True))
    return exponent / jnp.sum(exponent, axis=-1, keepdims=True)


def window_allowed(length, window, heads):
    row = lax.rem(lax.broadcasted_iota(jnp.int32, (heads * window, window), 0), window)
    column = lax.broadcasted_iota(jnp.int32, (heads * window, window), 1)
    return (row // length == column // length) & (row >= column)


def head_masks(width, dtype):
    lane = lax.broadcasted_iota(jnp.int32, (1, width), 1) // HEAD_SIZE
    return [(lane == j).astype(dtype) for j in range(width // HEAD_SIZE)]


def spread(values, masks):
    return jnp.concatenate([values * mask for mask in masks], axis=0)


def gathered(values, masks):
    n = values.shape[0] // len(masks)
    total = 0
    for j, mask in enumerate(masks):
        total = total + values[j * n : (j + 1) * n] * mask
    return total


FORWARD_VEC = ("ln1g", "ln1b", "sob", "ln2g", "ln2b", "cob", "ln3g", "ln3b")
BACKWARD_VEC = ("ln1g", "ln1b", "ln2g", "ln2b", "ln3g", "mob")


def as_rows(names, refs):
    return {name: ref[...].reshape(1, -1) for name, ref in zip(names, refs)}


def forward_kernel(dims, *refs):
    captions, length, images, width, part = dims
    rows = captions * length
    (counts, *vec), refs = refs[:9], refs[9:]
    (tokens, image, raw_in, raw_out, *weights), refs = refs[:9], refs[9:]
    (q1, kv1, o1, x1, q2, kv2, o2, x2, img, w_back, kv_turned), refs = refs[:11], refs[11:]
    (own_h3, other_h3, other_in, other_out), refs = refs[:4], refs[4:]
    (
        (v_q1, v_kv1, v_o1, v_x1, v_q2, v_kv2, v_o2, v_x2, v_img),
        v_w,
        v_turned,
        v_tokens,
        v_h,
        v_h3,
        send,
        recv,
        local,
    ) = refs
    d, t = lax.axis_index("dp"), lax.axis_index("tensor")
    near = {"p0": (flipped(d, 1), t), "p1": (flipped(d, 2), t), **peers()}
    order = [t, flipped(t, 1), flipped(t, 2), 3 - t]
    copies = Copies(send, recv, local)
    token_load = copies.move(tokens.at[pl.ds(t * rows, rows)], v_tokens)
    loads = [copies.move(weights[k], v_w[k].at[t]) for k in range(5)]
    image_load = copies.move(image.at[pl.ds(t * captions, captions)], v_img.at[:, t])
    g = as_rows(FORWARD_VEC, vec)
    greet(list(near.values()))
    quarter = lax.rem(d, 4)
    quarters = (quarter, flipped(quarter, 1), flipped(quarter, 2), 3 - quarter)
    other = order[2]

    def part_of(k, which, half=None):
        size = weights[k].shape[0] // 4
        start = quarters[which] * size
        if half is not None:
            first = (size // 2 + 15) // 16 * 16
            start, size = (start, first) if half == 0 else (start + first, size - first)
        return pl.ds(pl.multiple_of(start, 16), size)

    def region(k, which, half=None):
        return v_w[k].at[other, part_of(k, which, half)]

    count = len(weights)
    over_y, over, own_core = {}, {}, {}

    def send_y(k):
        over_y[k] = copies.to(
            weights[k].at[part_of(k, 0)], v_w[k].at[t, part_of(k, 0)], near["y"]
        )

    for k in range(count):
        own_core[k] = copies.to(weights[k], v_w[k].at[t], near["core"])
        send_y(k)
    images_in = [
        [
            copies.to(image.at[target * captions + caption], v_img.at[caption, t], near[name])
            for name, target in (("y", order[2]), ("far", order[3]), ("core", order[1]))
        ]
        for caption in range(captions)
    ]
    core = {k: [] for k in range(count)}

    def first(k):
        over_y[k].wait_recv()
        over[k, 0] = copies.to(region(k, 0), region(k, 0), near["p0"])
        over[k, 1] = copies.to(region(k, 0), region(k, 0), near["p1"])
        core[k].append(copies.to(region(k, 0), region(k, 0), near["core"]))

    def second(k):
        over[k, 0].wait_recv()
        over[k, 2] = copies.to(region(k, 1, 0), region(k, 1, 0), near["p1"])
        core[k].append(copies.to(region(k, 1), region(k, 1), near["core"]))
        over[k, 1].wait_recv()
        over[k, 3] = copies.to(region(k, 2, 1), region(k, 2, 1), near["p0"])
        core[k].append(copies.to(region(k, 2), region(k, 2), near["core"]))

    def third(k):
        over[k, 2].wait_recv()
        core[k].append(copies.to(region(k, 3, 0), region(k, 3, 0), near["core"]))
        over[k, 3].wait_recv()
        core[k].append(copies.to(region(k, 3, 1), region(k, 3, 1), near["core"]))

    def arrived(k):
        for made in core[k]:
            made.wait_recv()

    slab = 64

    def normed(source, gain, shift):
        def body(i, carry):
            place = pl.ds(pl.multiple_of(i * slab, slab), slab)
            n, _ = norm_parts(source[place, :].astype(HIGH))
            v_h[place, :] = (n * gain + shift).astype(LOW)
            return carry

        lax.fori_loop(0, rows // slab, body, 0)

    token_load.wait()
    normed(v_tokens, g["ln1g"], g["ln1b"])

    def start_sum(target, source, shift):
        def body(i, carry):
            place = pl.ds(pl.multiple_of(i * slab, slab), slab)
            target[place, :] = source[place, :].astype(HIGH) + shift
            return carry

        lax.fori_loop(0, rows // slab, body, 0)

    start_sum(v_x1, v_tokens, g["sob"])
    window = 2 * length
    heads = part // HEAD_SIZE
    causal = window_allowed(length, window, heads)
    masks, wide_masks = head_masks(part, LOW), head_masks(part, HIGH)

    def self_part(s):
        h = v_h[...]
        v_q1[s] = dot_rows(h, v_w[0][s, :part, :]).astype(LOW)
        v_kv1[s] = dot_rows(v_w[0][s, part:, :], h).astype(LOW)
        for w in range(rows // window):
            span = pl.ds(w * window, window)
            q = spread(v_q1[s, span, :], masks)
            p = softmax(dot(q, v_kv1[s, :part, span]), causal)
            mixed = dot_rows(p.astype(LOW), v_kv1[s, part:, span])
            v_o1[s, span, :] = gathered(mixed, wide_masks).astype(LOW)
        v_x1[...] += dot(v_o1[s], v_w[1][s])

    def queries(groups):
        def body(i, carry):
            s = pair(groups, i)
            v_q2[s] = dot_rows(v_h[...], v_w[2][s]).astype(LOW)
            return carry

        lax.fori_loop(0, 2, body, 0)

    def turn(groups):
        def body(i, carry):
            s = pair(groups, i)
            v_turned[:, pl.ds(pl.multiple_of(s * 2 * part, 128), 2 * part)] = v_w[3][s].T
            return carry

        lax.fori_loop(0, 2, body, 0)

    def spans(c):
        return (
            pl.ds(pl.multiple_of(c * images, images), images),
            pl.ds(pl.multiple_of(c * length, length), length),
        )

    def pair(groups, i):
        return groups[0] + i * (groups[1] - groups[0])

    def mix(c, s):
        allowed = lax.broadcasted_iota(jnp.int32, (1, images), 1) < counts[t * captions + c]
        span, own = spans(c)
        kv = dot(v_w[3][s], v_img[c].reshape(width, images)).astype(LOW)
        v_kv2[s, :, span] = kv
        q = spread(v_q2[s, own, :], masks)
        p = softmax(dot(q, kv[:part]), allowed)
        mixed = dot_rows(p.astype(LOW), kv[part:])
        v_o2[s, own, :] = gathered(mixed, wide_masks).astype(LOW)

    def near_part(first_caption, count):
        def body(i, carry):
            mix(first_caption + i // 2, pair(order[:2], lax.rem(i, 2)))
            return carry

        lax.fori_loop(0, 2 * count, body, 0)

    def cross_part(c):
        own = spans(c)[1]

        def body(i, carry):
            mix(c, pair(order[2:], i))
            return carry

        lax.fori_loop(0, 2, body, 0)
        total = v_x2[own, :]
        for s in range(4):
            total = total + dot(v_o2[s, own, :], v_w[4][s])
        v_x2[own, :] = total
        n, _ = norm_parts(total)
        v_h3[own, :] = (n * g["ln3g"] + g["ln3b"]).astype(LOW)
        h3_in.append(copies.to(v_h3.at[own], other_h3.at[own], near["y"]))

    h3_in = []
    back = []

    def image_arrived(c):
        for made in images_in[c]:
            made.wait_recv()

    loads[0].wait()
    loads[1].wait()
    self_part(order[0])
    own_core[0].wait_recv()
    own_core[1].wait_recv()
    first(0)
    self_part(order[1])
    first(1)
    for k in range(2, 5):
        loads[k].wait()
        own_core[k].wait_recv()
    turn(order[:2])
    second(0)
    second(1)
    first(2)
    first(3)
    first(4)
    third(0)
    third(1)
    image_load.wait()
    arrived(0)
    arrived(1)
    second(2)

    def far_self(i, carry):
        self_part(pair(order[2:], i))
        return carry

    lax.fori_loop(0, 2, far_self, 0)
    second(3)
    second(4)
    normed(v_x1, g["ln2g"], g["ln2b"])
    queries(order[:2])
    start_sum(v_x2, v_x1, g["cob"])
    image_arrived(0)
    image_arrived(1)
    near_part(0, 2)
    third(2)
    third(3)
    third(4)
    mlp_in = [
        copies.to(a, b, near["core"]) for a, b in ((raw_in, other_in), (raw_out, other_out))
    ]
    back.append(copies.move(v_q1, q1))
    back.append(copies.move(v_kv1, kv1))
    back.append(copies.move(v_o1, o1))
    back.append(copies.move(v_x1, x1))
    for caption in range(2, captions):
        image_arrived(caption)
    near_part(2, captions - 2)
    for k in range(2, 5):
        arrived(k)
    for i, k in enumerate((0, 1, 2, 4)):
        back.append(copies.move(v_w[k], w_back[i]))
    queries(order[2:])
    back.append(copies.move(v_q2, q2))
    for caption in range(captions):
        cross_part(caption)
    turn(order[2:])
    back.append(copies.move(v_turned, kv_turned))
    back.append(copies.move(v_img, img))
    back.append(copies.move(v_kv2, kv2))
    back.append(copies.move(v_o2, o2))
    back.append(copies.move(v_x2, x2))
    back.append(copies.move(v_h3, own_h3))
    for made in mlp_in + h3_in:
        made.wait_recv()
    copies.drain()
    for made in back:
        made.wait()


def forward(dims, counts, vec, tokens, image, raw, weights):
    captions, length, images, width, part = dims
    rows = captions * length
    shape = jax.ShapeDtypeStruct
    kept = [
        ((4, rows, part), LOW),
        ((4, 2 * part, rows), LOW),
        ((4, rows, part), LOW),
        ((rows, width), HIGH),
        ((4, rows, part), LOW),
        ((4, 2 * part, captions * images), LOW),
        ((4, rows, part), LOW),
        ((rows, width), HIGH),
        ((captions, 4, part, images), LOW),
    ]
    sizes = [(4, *w.shape) for w in weights]
    any_spec = pl.BlockSpec(memory_space=pl.ANY)
    vmem, smem = pl.BlockSpec(memory_space=pltpu.VMEM), pl.BlockSpec(memory_space=pltpu.SMEM)
    remote = 5 * 11 + 4 * captions + 2
    return pl.pallas_call(
        partial(forward_kernel, dims),
        out_shape=[shape(*k) for k in kept]
        + [
            [shape(sizes[k], LOW) for k in (0, 1, 2, 4)],
            shape((width, 8 * part), LOW),
            shape((rows, width), LOW),
            shape((rows, width), LOW),
            shape(raw[0].shape, LOW),
            shape(raw[1].shape, LOW),
        ],
        in_specs=[smem] + [vmem] * 8 + [any_spec] * 9,
        out_specs=[any_spec] * 9 + [[any_spec] * 4] + [any_spec] * 5,
        scratch_shapes=[
            [pltpu.VMEM(*k) for k in kept],
            [pltpu.VMEM(sizes[k], LOW) for k in range(5)],
            pltpu.VMEM((width, 8 * part), LOW),
            pltpu.VMEM((rows, width), LOW),
            pltpu.VMEM((rows, width), LOW),
            pltpu.VMEM((rows, width), LOW),
            pltpu.SemaphoreType.DMA((remote,)),
            pltpu.SemaphoreType.DMA((remote,)),
            pltpu.SemaphoreType.DMA((32,)),
        ],
        name="forward",
        compiler_params=pltpu.CompilerParams(
            collective_id=0, has_side_effects=True, vmem_limit_bytes=62 << 20
        ),
    )(counts, *vec, tokens, image, *raw, *weights)


def backward_kernel(dims, stride, *refs):
    captions, length, images, width, part = dims
    rows = captions * length
    block, wide = width // 8, width // 2
    heads = part // HEAD_SIZE
    window = 2 * length
    (
        counts,
        vec,
        (bias, tokens, grads, raw_in, raw_out, own_h3, other_h3, other_in, other_out),
        (q1, kv1, o1, x1, q2, kv2, o2, x2, img),
        w_back,
        kv_turned,
        sums,
        image_out,
        out_all,
        token_all,
        small_out,
        (v_q1, v_kv1, v_o1, v_x1, v_q2, v_kv2, v_o2, v_x2, v_img),
        (v_w0, v_w1, v_w2, v_w4),
        v_turned,
        (v_in, v_out, g_out, g_in, g_cross, g_self),
        v_bias,
        v_tokens,
        v_grads,
        v_h3,
        v_h,
        v_turn_a,
        v_turn_b,
        v_f0,
        v_f1,
        v_y,
        v_g,
        v_low,
        v_parts,
        v_narrow,
        from_core,
        halves,
        from_y,
        result,
        v_sum,
        sum_in,
        credit,
        send,
        recv,
        local,
    ) = refs
    d, t = lax.axis_index("dp"), lax.axis_index("tensor")
    y, c = t // 2, lax.rem(t, 2)
    near = peers()
    bits = [lax.rem(d // (stride << b), 2) for b in range(3)]
    partner = [(flipped(d, stride << b), t) for b in range(3)]
    order = [3 - t, flipped(t, 2), flipped(t, 1), t]
    copies = Copies(send, recv, local)

    mine = pl.ds(t * rows, rows)
    load_x2 = copies.move(x2, v_x2)
    load_grads = [
        copies.move(grads.at[mine], v_grads.at[0]),
        copies.move(grads.at[pl.ds(flipped(t, 2) * rows, rows)], v_grads.at[1]),
    ]
    load_mlp = [
        [copies.move(a, v_h3.at[i]) for i, a in ((0, own_h3), (1, other_h3))],
        [copies.move(raw_in, v_in.at[c]), copies.move(raw_out, v_out.at[c])],
        [copies.move(other_in, v_in.at[1 - c]), copies.move(other_out, v_out.at[1 - c])],
    ]
    load_rest = [
        copies.move(a, b)
        for a, b in (
            (w_back[3], v_w4),
            (q2, v_q2),
            (kv2, v_kv2),
            (o2, v_o2),
            (x1, v_x1),
            (img, v_img),
            (w_back[2], v_w2),
            (kv_turned, v_turned),
            (w_back[1], v_w1),
            (w_back[0], v_w0),
            (q1, v_q1),
            (kv1, v_kv1),
            (o1, v_o1),
            (tokens.at[mine], v_tokens),
        )
    ]
    greet([*near.values(), *partner])
    bias_in = copies.to(bias, v_bias, near["core"])

    g = as_rows(BACKWARD_VEC, vec)
    slab = 64

    def loop(body, init, step=slab):
        def run(i, carry):
            return body(pl.ds(pl.multiple_of(i * step, step), step), carry)

        return lax.fori_loop(0, rows // step, run, init)

    zeros = jnp.zeros((8, width), HIGH)

    def keep(name, total):
        v_sum[0, name : name + 1, :] = jnp.sum(total, axis=0, keepdims=True)

    pieces = [g_out, g_in, g_cross, g_self]
    plan = {
        (0, 0): (0, 1, 2),
        (0, 1): (1, 0, 2),
        (1, 0): (0, 1, 2),
        (1, 1): (1, 0, 2),
        (2, 0): ("y", 1, 0, 2),
        (2, 1): (1, 0, 2, "y"),
        (3, 0): (0, 1, 2, "y"),
        (3, 1): (1, 0, 2, "y"),
    }
    units = [(p, o, h) for p in range(4) for o in ((1,) if p < 2 else (0, 1)) for h in (0, 1)]
    y_places = {(2, 0): from_y[0], (2, 1): from_y[1], (3, 0): from_y[2], (3, 1): from_y[3]}
    to_core, hops, places = {}, {}, {}
    side = (1 - y, y)

    def lanes(h):
        return pl.ds(h * wide, wide)

    def slot(p, o):
        return p if p < 2 else 2 + o if p == 2 else o

    def own(p, o, core):
        return (core,) if p < 2 else (side[o], core)

    def offer(p, o):
        if p == 3:
            pl.semaphore_wait(credit.at[o], 1)
        to_core[p, o] = copies.to(
            pieces[p].at[own(p, o, 1 - c)], from_core.at[slot(p, o)], near["core"]
        )

    def add(target, left, *others):
        lead = left.shape[:-2]
        total = 1
        for size in lead:
            total *= size
        low = len(others) == 1 and target.dtype == LOW

        def body(i, carry):
            index, rest = [], i
            for size in reversed(lead):
                index.insert(0, lax.rem(rest, size))
                rest = rest // size
            place = (*index, slice(None), slice(None))
            value = left[place] if low else left[place].astype(HIGH)
            for ref in others:
                value = value + (ref[place] if low else ref[place].astype(HIGH))
            target[place] = value.astype(target.dtype)
            return carry

        if total == 1:
            body(0, 0)
        else:
            lax.fori_loop(0, total, body, 0)

    def cut(bit, left, value):
        return tuple(value if b == bit else slice(None) for b in sorted(left, reverse=True))

    back = []

    def advance(p, o, h, stage):
        u = units.index((p, o, h))
        turn = plan[p, h]
        y_first, with_y = turn[0] == "y", "y" in turn
        xyz = [b for b in turn if b != "y"]
        if stage == 0:
            base = pieces[p].at[(*own(p, o, c), *[slice(None)] * 4, lanes(h))]
            sent = from_core.at[(slot(p, o), *[slice(None)] * 4, lanes(h))]
            if (p, o, "core") not in places:
                to_core[p, o].wait_recv()
                places[p, o, "core"] = True
            if y_first and o == 1:
                hops[p, 0, h, "y"].wait_recv()
                add(base, base, sent, y_places[p, h])
            else:
                add(base, base, sent)
            places[u] = base, [0, 1, 2]
            if y_first and o == 0:
                hops[p, 0, h, "y"] = copies.to(base, y_places[p, h], near["y"])
                return
        if stage > 0:
            source, left = places[u]
            bit = xyz[stage - 1]
            hops[p, o, h, stage].wait_recv()
            target = halves[stage - 1].at[u]
            kept = source.at[cut(bit, left, bits[bit])]
            remaining = [b for b in left if b != bit]
            last = stage == 3
            if last and o == 1:
                total = result.at[p, :, lanes(h)]
                if y_first or not with_y:
                    add(total, target, kept)
                else:
                    hops[p, 0, h, "y"].wait_recv()
                    add(total, target, kept, y_places[p, h])
                back.append(copies.move(total, sums[p].at[:, lanes(h)]))
                return
            add(target, target, kept)
            places[u] = target, remaining
            if last:
                hops[p, 0, h, "y"] = copies.to(target, y_places[p, h], near["y"])
                return
        source, left = places[u]
        bit = xyz[stage]
        hops[p, o, h, stage + 1] = copies.to(
            source.at[cut(bit, left, 1 - bits[bit])], halves[stage].at[u], partner[bit]
        )

    def free(o):
        pl.semaphore_signal(credit.at[o], inc=1, device_id=near["core"], device_id_type=MESH)

    def forth(p, o, stage):
        advance(p, o, 0, stage)
        advance(p, o, 1, stage)

    own_rows, other_rows = slice(0, rows), slice(rows, 2 * rows)

    def weight(ref, e):
        return ref[e].reshape(width, width)

    def put(ref, index, first, values):
        half, values = values
        ref[(*index, half, slice(None), slice(None), slice(None), slice(first, first + values.shape[1]))] = (
            values.astype(LOW).reshape(2, 2, block, values.shape[1])
        )

    def half_rows(half):
        return pl.ds(half * (width // 2), width // 2)

    bias_sums = [zeros, zeros]
    hidden = g_self.reshape(4 * width, width)

    def hidden_rows(kind, i, r, size=rows):
        return hidden.at[pl.ds(((kind * 2 + i) * 2 + r) * rows, size)]

    def feed(i, r):
        e = 1 - c if i else c
        v_f0[...] = dot(v_h3[r], weight(v_in, e))
        v_f1[...] = dot_rows(v_grads[r], weight(v_out, e))
        shift = (v_bias if i else bias)[...].reshape(1, -1)

        v_u, v_ga = hidden_rows(0, i, r), hidden_rows(1, i, r)

        def act(place, carry):
            a = v_f0[place, :] + shift
            cumulative = 0.5 * (1.0 + lax.erf(a * (0.5**0.5)))
            density = jnp.exp(-0.5 * a * a) * 0.3989422804014327
            v_u[place, :] = (a * cumulative).astype(LOW)
            ga = (v_f1[place, :] * (cumulative + a * density)).astype(LOW)
            v_ga[place, :] = ga
            return carry + folded(ga.astype(HIGH))

        bias_sums[i] += loop(act, zeros, 16)
        if i == 0:
            v_y[r] = dot(v_u[...], weight(v_out, e))
            v_g[r] = dot_rows(v_ga[...], weight(v_in, e))
        else:
            v_y[r] += dot(v_u[...], weight(v_out, e))
            v_g[r] += dot_rows(v_ga[...], weight(v_in, e))

    for load in load_grads + load_mlp[0] + load_mlp[1]:
        load.wait()
    feed(0, 1)
    for load in load_mlp[2]:
        load.wait()
    bias_in.wait_recv()
    feed(1, 1)

    def rounded(place, carry):
        v_low[0, place, :] = v_g[1, place, :].astype(LOW)
        v_low[1, place, :] = v_y[1, place, :].astype(LOW)
        return carry

    loop(rounded, 0)
    parts_in = [copies.to(v_low.at[i], v_parts.at[i], near["y"]) for i in range(2)]
    feed(0, 0)
    feed(1, 0)

    def start(place, carry):
        return carry + folded(v_grads[0, place, :].astype(HIGH))

    keep(8, loop(start, zeros))
    v_turn_a[:, own_rows] = v_h3[0].T
    v_turn_a[:, other_rows] = v_h3[1].T
    v_turn_b[:, own_rows] = v_grads[0].T
    v_turn_b[:, other_rows] = v_grads[1].T
    for i in (1, 0):
        e = 1 - c if i else c
        u, ga = (hidden_rows(kind, i, 0, size=2 * rows)[...] for kind in (0, 1))
        for half in range(2):
            put(g_out, (e,), 0, (half, dot(v_turn_b[half_rows(half), :], u)))
            put(g_in, (e,), 0, (half, dot(v_turn_a[half_rows(half), :], ga)))
        if i == 1:
            offer(0, 1)
            offer(1, 1)
    for s in range(4):
        total = jnp.sum(jnp.where(c == s % 2, bias_sums[0], bias_sums[1]), axis=0, keepdims=True)
        v_sum[0, 9 + s : 10 + s, :] = jnp.where(y == s // 2, total, 0.0)
    v_sum[0, 13:16, :] = jnp.zeros((3, width), HIGH)
    for p in (0, 1):
        forth(p, 1, 0)
        free(p)

    def shared(source, target):
        place = target.at[pl.ds(t * rows, rows)]
        back.append(copies.move(source, place))
        return [copies.to(source, place, near[name]) for name in ("y", "core")]

    def passed_on(moves, target):
        place = target.at[pl.ds(flipped(t, 2) * rows, rows)]
        moves[0].wait_recv()
        return [moves[1], copies.to(place, place, near["core"])]

    def norm_back(source, gain, old, new, low, more=None):
        def body(place, carry):
            a, b, e = carry
            n, inv_std = norm_parts(source[place, :].astype(HIGH))
            gh = v_g[0, place, :]
            if more is not None:
                gh = gh + more[place, :].astype(HIGH)
            scaled = gh * gain
            grad = inv_std * (
                scaled
                - jnp.mean(scaled, axis=-1, keepdims=True)
                - n * jnp.mean(scaled * n, axis=-1, keepdims=True)
            )
            grad = old[place, :].astype(HIGH) + grad
            if new is not None:
                new[place, :] = grad
                e = e + folded(grad)
            low[place, :] = grad.astype(LOW)
            return a + folded(gh * n), b + folded(gh), e

        return loop(body, (zeros, zeros, zeros))

    def finish(place, carry):
        total = v_x2[place, :] + g["mob"] + v_y[0, place, :] + v_parts[1, place, :].astype(HIGH)
        v_low[2, place, :] = total.astype(LOW)
        return carry

    load_x2.wait()
    parts_in[0].wait_recv()
    own_grads = v_grads.at[0]
    gain_sum, bias_sum, total = norm_back(
        v_x2, g["ln3g"], own_grads, v_f0, own_grads, v_parts.at[0]
    )
    keep(6, gain_sum)
    keep(7, bias_sum)
    keep(5, total)

    for load in load_rest:
        load.wait()

    def again(source, gain, shift):
        def body(place, carry):
            n, _ = norm_parts(source[place, :].astype(HIGH))
            v_h[place, :] = (n * gain + shift).astype(LOW)
            v_g[0, place, :] = jnp.zeros((slab, width), HIGH)
            return carry

        loop(body, 0)

    again(v_x1, g["ln2g"], g["ln2b"])
    v_turn_a[:, own_rows] = v_h[...].T
    v_turn_b[:, own_rows] = v_grads[0].T
    go, gq = v_narrow.at[0], v_narrow.at[1]
    masks, wide_masks = head_masks(part, LOW), head_masks(part, HIGH)

    def attend_back(q, k, v, g_mix, allowed):
        q, g_mix = spread(q, masks), spread(g_mix, masks)
        p = softmax(dot(q, k), allowed)
        low_p = p.astype(LOW)
        gp = dot(g_mix, v)
        inner = jnp.sum(gp * p, axis=-1, keepdims=True)
        gs = (p * (gp - inner)).astype(LOW)
        return (
            (gathered(dot_rows(gs, k), wide_masks) * SCALING).astype(LOW),
            (dot_columns(q, gs) * SCALING).astype(LOW),
            dot_columns(g_mix, low_p).astype(LOW),
        )

    def gradients(piece, s, of_keys, o_kept):
        for half in range(2):
            index = (s // 2, lax.rem(s, 2))
            put(piece, index, 0, (half, of_keys(half)))
            both = [dot(v_turn_a[half_rows(half), own_rows], gq[...])]
            both.append(dot(v_turn_b[half_rows(half), own_rows], o_kept[s]))
            put(piece, index, 2 * part, (half, jnp.concatenate(both, axis=1)))

    def cross_back(s):
        go[...] = dot_rows(v_grads[0], v_w4[s]).astype(LOW)

        def body(caption, carry):
            span = pl.ds(pl.multiple_of(caption * images, images), images)
            own = pl.ds(pl.multiple_of(caption * length, length), length)
            allowed = (
                lax.broadcasted_iota(jnp.int32, (1, images), 1) < counts[t * captions + caption]
            )
            g_q, g_k, g_v = attend_back(
                v_q2[s, own, :], v_kv2[s, :part, span], v_kv2[s, part:, span], go[own, :], allowed
            )
            v_kv2[s, :part, span] = g_k
            v_kv2[s, part:, span] = g_v
            gq[own, :] = g_q
            return carry

        lax.fori_loop(0, captions, body, 0)
        v_g[0] += dot(gq[...], v_w2[s])

        def of_keys(half):
            total = 0
            for caption in range(captions):
                span = slice(caption * images, (caption + 1) * images)
                features = v_img[caption, 2 * half : 2 * half + 2].reshape(width // 2, images)
                total = total + dot_rows(features, v_kv2[s, :, span])
            return total

        gradients(g_cross, s, of_keys, v_o2)

    for i, s in enumerate(order):
        cross_back(s)
        if i == 0:
            parts_in[1].wait_recv()
            loop(finish, 0)
            out_moves = shared(v_low.at[2], out_all)
            offer(2, 0)
            forth(0, 1, 1)
        if i == 1:
            forth(2, 0, 0)
        if i == 2:
            offer(2, 1)
            forth(1, 1, 1)
            out_moves = passed_on(out_moves, out_all)
        if i == 3:
            forth(0, 1, 2)
            advance(2, 1, 1, 0)
    image_span = pl.ds(t * captions, captions)

    def image_part(caption, carry):
        span = pl.ds(pl.multiple_of(caption * images, images), images)
        values = dot(v_turned[...], v_kv2[:, :, span].reshape(8 * part, images))
        v_img[caption] = values.astype(LOW).reshape(4, part, images)
        return carry

    lax.fori_loop(0, captions, image_part, 0)
    forth(1, 1, 2)
    advance(2, 0, 1, 1)
    image_moves = [
        copies.to(v_img.at[:, target], image_out.at[image_span], near[name])
        for name, target in (("y", flipped(t, 2)), ("far", 3 - t), ("core", flipped(t, 1)))
    ]
    back.append(copies.move(v_img.at[:, t], image_out.at[image_span]))
    gain_sum, bias_sum, total = norm_back(v_x1, g["ln2g"], v_f0, v_f1, own_grads)
    keep(3, gain_sum)
    keep(4, bias_sum)
    keep(2, total)
    forth(0, 1, 3)
    advance(2, 1, 0, 0)

    again(v_tokens, g["ln1g"], g["ln1b"])
    v_turn_a[:, own_rows] = v_h[...].T
    v_turn_b[:, own_rows] = v_grads[0].T
    causal = window_allowed(length, window, heads)

    def self_back(s):
        go[...] = dot_rows(v_grads[0], v_w1[s]).astype(LOW)
        for w in range(rows // window):
            span = pl.ds(w * window, window)
            g_q, g_k, g_v = attend_back(
                v_q1[s, span, :], v_kv1[s, :part, span], v_kv1[s, part:, span], go[span, :], causal
            )
            v_kv1[s, :part, span] = g_k
            v_kv1[s, part:, span] = g_v
            gq[span, :] = g_q
        v_g[0] += dot(gq[...], v_w0[s, :part, :]) + dot_columns(v_kv1[s], v_w0[s, part:, :])

        def of_keys(half):
            return dot_rows(v_turn_a[half_rows(half), own_rows], v_kv1[s])

        gradients(g_self, s, of_keys, v_o1)

    for i, s in enumerate(order):
        self_back(s)
        if i == 0:
            offer(3, 0)
            forth(1, 1, 3)
            advance(2, 1, 1, 1)
            advance(2, 0, 1, 2)
        if i == 1:
            forth(3, 0, 0)
            advance(2, 1, 0, 1)
        if i == 2:
            offer(3, 1)
            advance(2, 1, 1, 2)
            advance(2, 0, 1, 3)
    forth(3, 1, 0)
    gain_sum, bias_sum, _ = norm_back(v_tokens, g["ln1g"], v_f1, None, v_h)
    keep(0, gain_sum)
    keep(1, bias_sum)
    small_to = [near["core"], *partner, near["y"]]
    small = []

    def total_start():
        i = len(small)
        small.append(copies.to(v_sum.at[i], sum_in.at[i], small_to[i]))

    def total_end():
        i = len(small) - 1
        small[i].wait_recv()
        v_sum[i + 1] = v_sum[i] + sum_in[i]

    total_start()
    token_moves = shared(v_h, token_all)
    advance(2, 1, 0, 2)
    forth(3, 0, 1)
    forth(2, 1, 3)
    total_end()
    total_start()
    forth(3, 1, 1)
    total_end()
    total_start()
    forth(3, 0, 2)
    total_end()
    total_start()
    forth(3, 1, 2)
    forth(3, 0, 3)
    total_end()
    total_start()
    token_moves = passed_on(token_moves, token_all)
    forth(3, 1, 3)
    total_end()
    back.append(copies.move(v_sum.at[5], small_out))
    for made in out_moves + image_moves + token_moves:
        made.wait_recv()
    copies.drain()
    for made in back:
        made.wait()


def backward(dims, stride, counts, vec, bias, tokens, grads, raw, mlp, kept, w_back, turned):
    captions, length, images, width, part = dims
    rows = captions * length
    block, wide = width // 8, width // 2
    shape = jax.ShapeDtypeStruct
    any_spec = pl.BlockSpec(memory_space=pl.ANY)
    vmem, smem = pl.BlockSpec(memory_space=pltpu.VMEM), pl.BlockSpec(memory_space=pltpu.SMEM)
    shard = (2, 2, 2, block, width)
    raw = [w.reshape(shard) for w in raw]
    own_h3, other_h3, *others = mlp
    mlp = [own_h3, other_h3, *(w.reshape(shard) for w in others)]
    remote = 128

    def scratch(*size, dtype=LOW):
        return pltpu.VMEM(size, dtype)

    flat = [scratch(*k.shape, dtype=k.dtype) for k in kept]
    return pl.pallas_call(
        lambda *refs: backward_kernel(
            dims,
            stride,
            refs[0],
            refs[1:7],
            refs[7:16],
            refs[16:25],
            refs[25:29],
            refs[29],
            refs[30:34],
            *refs[34:],
        ),
        out_shape=[shape((block, width), HIGH)] * 4
        + [
            shape((4 * captions, part, images), LOW),
            shape((4 * rows, width), LOW),
            shape((4 * rows, width), LOW),
            shape((16, width), HIGH),
        ],
        in_specs=[smem] + [vmem] * 7 + [any_spec] * 22,
        out_specs=[any_spec] * 8,
        scratch_shapes=[
            flat,
            [scratch(*w.shape) for w in w_back],
            scratch(*turned.shape),
            [scratch(2, *shard)] * 4 + [scratch(2, 2, *shard)] * 2,
            scratch(*bias.shape, dtype=HIGH),
            scratch(rows, width),
            scratch(2, rows, width),
            scratch(2, rows, width),
            scratch(rows, width),
            scratch(width, 2 * rows),
            scratch(width, 2 * rows),
            scratch(rows, width, dtype=HIGH),
            scratch(rows, width, dtype=HIGH),
            scratch(2, rows, width, dtype=HIGH),
            scratch(2, rows, width, dtype=HIGH),
            scratch(3, rows, width),
            scratch(2, rows, width),
            scratch(2, rows, part),
            scratch(4, *shard),
            [
                scratch(12, 2, 2, block, wide),
                scratch(12, 2, block, wide),
                scratch(12, block, wide),
            ],
            [scratch(2, 2, 2, block, wide)] + [scratch(block, wide)] * 3,
            scratch(4, block, width, dtype=HIGH),
            scratch(6, 16, width, dtype=HIGH),
            scratch(5, 16, width, dtype=HIGH),
            pltpu.SemaphoreType.REGULAR((2,)),
            pltpu.SemaphoreType.DMA((remote,)),
            pltpu.SemaphoreType.DMA((remote,)),
            pltpu.SemaphoreType.DMA((48,)),
        ],
        name="backward",
        compiler_params=pltpu.CompilerParams(
            collective_id=1, has_side_effects=True, vmem_limit_bytes=67043328
        ),
    )(counts, *vec, bias, tokens, grads, *raw, *mlp, *kept, *w_back, turned)


def finish_kernel(dims, *refs):
    captions, length, images, width, part = dims
    ins, refs = refs[:8], refs[8:]
    outs, vectors, refs = (*refs[:9], refs[19]), refs[9:19], refs[20:]
    buffers, made_qkv, made_self, made_q, made_cross, made_kv, arrive, leave = refs
    loads = [
        pltpu.make_async_copy(a, b, arrive.at[i]) for i, (a, b) in enumerate(zip(ins, buffers))
    ]
    for load in loads[::-1]:
        load.start()
    v_self, v_cross, v_small = buffers[:3]
    leaving = []

    def put(source, target):
        made = pltpu.make_async_copy(source, target, leave.at[len(leaving)])
        made.start()
        leaving.append(made)

    def columns(ref, i):
        return ref[:, i * part : (i + 1) * part]

    for i in range(7, 2, -1):
        loads[i].wait()
        put(buffers[i], outs[i + 1])
    loads[0].wait()
    for i, j in enumerate((2, 0, 1)):
        made_qkv[i] = columns(v_self, j)
    put(made_qkv, outs[0])
    made_self[...] = columns(v_self, 3).T
    put(made_self, outs[1])
    loads[1].wait()
    made_q[...] = columns(v_cross, 2)
    put(made_q, outs[2])
    made_cross[...] = columns(v_cross, 3).T
    put(made_cross, outs[3])
    for i in range(2):
        made_kv[:, i, :] = columns(v_cross, i)
    put(made_kv, outs[9])
    loads[2].wait()
    for i, ref in enumerate(vectors[:9]):
        ref[...] = v_small[i : i + 1, :].reshape(width)
    own = v_small[pl.ds(9 + lax.axis_index("tensor"), 1), :]
    vectors[9][...] = own.reshape(width)
    for made in leaving:
        made.wait()


def finish(dims, ins):
    captions, length, images, width, part = dims
    block = ins[0].shape[0]
    any_spec, vmem = pl.BlockSpec(memory_space=pl.ANY), pl.BlockSpec(memory_space=pltpu.VMEM)
    made = [(3, block, part), (part, block), (block, part), (part, block)]
    return pl.pallas_call(
        partial(finish_kernel, dims),
        out_shape=[jax.ShapeDtypeStruct(size, HIGH) for size in made]
        + [jax.ShapeDtypeStruct(x.shape, x.dtype) for x in ins[3:]]
        + [jax.ShapeDtypeStruct((width,), HIGH)] * 10
        + [jax.ShapeDtypeStruct((block, 2, part), HIGH)],
        in_specs=[any_spec] * 8,
        out_specs=[any_spec] * 9 + [vmem] * 10 + [any_spec],
        scratch_shapes=[
            [pltpu.VMEM(x.shape, x.dtype) for x in ins],
            *(pltpu.VMEM(size, HIGH) for size in made),
            pltpu.VMEM((block, 2, part), HIGH),
            pltpu.SemaphoreType.DMA((8,)),
            pltpu.SemaphoreType.DMA((10,)),
        ],
        name="finish",
    )(*ins)


def local(
    tokens,
    image_tokens,
    image_counts,
    ln1_gain,
    ln1_bias,
    self_qkv,
    self_output_weight,
    self_output_bias,
    ln2_gain,
    ln2_bias,
    cross_query_weight,
    cross_kv,
    cross_output_weight,
    cross_output_bias,
    ln3_gain,
    ln3_bias,
    mlp_in,
    mlp_in_bias,
    mlp_out,
    mlp_out_bias,
    grad_out,
):
    stride = lax.axis_size("dp") // 8
    all_captions, length, width = tokens.shape
    images, part = image_tokens.shape[1:]
    captions = all_captions // 4
    dims = (captions, length, images, width, part)
    first = [ln1_gain, ln1_bias, self_output_bias, ln2_gain, ln2_bias, cross_output_bias]
    first += [ln3_gain, ln3_bias]
    second = [ln1_gain, ln1_bias, ln2_gain, ln2_bias, ln3_gain, mlp_out_bias]
    tokens = tokens.reshape(-1, width)
    grads = grad_out.reshape(-1, width)
    weights = [
        self_qkv.transpose(1, 2, 0).reshape(3 * part, width),
        self_output_weight,
        cross_query_weight.T,
        cross_kv.transpose(1, 2, 0).reshape(2 * part, width),
        cross_output_weight,
    ]
    raw = (mlp_in, mlp_out)
    *kept, w_back, turned, own_h3, other_h3, other_in, other_out = forward(
        dims, image_counts, first, tokens, image_tokens.transpose(0, 2, 1), raw, weights
    )
    sum_out, sum_in, sum_cross, sum_self, grad_image, output, grad_tokens, small = backward(
        dims,
        stride,
        image_counts,
        second,
        mlp_in_bias,
        tokens,
        grads,
        raw,
        (own_h3, other_h3, other_in, other_out),
        kept,
        w_back,
        turned,
    )
    if stride > 1:
        groups = [[hi * stride + lo for lo in range(stride)] for hi in range(8)]
        sum_out, sum_in, sum_cross, sum_self = (
            lax.psum_scatter(s, "dp", scatter_dimension=0, axis_index_groups=groups, tiled=True)
            for s in (sum_out, sum_in, sum_cross, sum_self)
        )
        small = lax.psum(small, "dp", axis_index_groups=groups)
    qkv, self_out, cross_q, cross_out, sum_in, sum_out, *rest = finish(
        dims, [sum_self, sum_cross, small, sum_in, sum_out, output, grad_tokens, grad_image]
    )
    output, grad_tokens, grad_image, *vectors, cross_kv = rest
    return (
        output.reshape(all_captions, length, width),
        grad_tokens.reshape(all_captions, length, width),
        grad_image.transpose(0, 2, 1),
        vectors[0],
        vectors[1],
        qkv.transpose(1, 0, 2),
        self_out,
        vectors[2],
        vectors[3],
        vectors[4],
        cross_q,
        cross_kv,
        cross_out,
        vectors[5],
        vectors[6],
        vectors[7],
        sum_in,
        vectors[9],
        sum_out.T,
        vectors[8],
    )


def solution(mesh):
    return jax.shard_map(
        local,
        mesh=mesh,
        in_specs=(
            P("dp", None, None),
            P("dp", None, "tensor"),
            P("dp"),
            P(),
            P(),
            P(None, None, "tensor"),
            P("tensor", None),
            P(),
            P(),
            P(),
            P(None, "tensor"),
            P(None, None, "tensor"),
            P("tensor", None),
            P(),
            P(),
            P(),
            P(None, "tensor"),
            P("tensor"),
            P("tensor", None),
            P(),
            P("dp", None, None),
        ),
        out_specs=(
            P("dp", None, None),
            P("dp", None, None),
            P("dp", None, "tensor"),
            P(),
            P(),
            P("dp", None, "tensor"),
            P("tensor", "dp"),
            P(),
            P(),
            P(),
            P("dp", "tensor"),
            P("dp", None, "tensor"),
            P("tensor", "dp"),
            P(),
            P(),
            P(),
            P("dp", "tensor"),
            P("tensor"),
            P("tensor", "dp"),
            P(),
        ),
        check_vma=False,
    )
```
